512 devices in a mesh: ka: 16 (over x_hi, y), mode: 8 (over z), row: 4 (over x_lo, core).
Axes of the slice: x: 4 (x_hi: 2, x_lo: 2; x = x_hi * 2 + x_lo), y: 8, z: 8, core: 2. Of those that a mesh axis runs over, the one named last changes fastest.
Arguments:
- vectors: float32 [16, 8, 16, 16, 8, 512], P('ka', None, 'mode', 'row'), may hold values from -6 to 6
- previous: float32 [16, 8, 16, 16, 8, 512], P('ka', None, 'mode', 'row'), may hold values from -6 to 6
- beta: float32 [8, 8], replicated, may hold values from -2 to 2
- potential: float32 [16, 16, 8, 512], P('mode', 'row'), may hold values from 0.1 to 10
- coriolis_fn: float32 [16, 16, 8, 512], P('mode', 'row'), may hold values from 0.5 to 2
- second_fn: float32 [16, 16, 8, 512], P('mode', 'row'), may hold values from 0.5 to 2
- rot_const: float32 [16], replicated, may hold values from 0.02 to 0.06
- coupling: float32 [2, 16], replicated, may hold values from 0.3 to 1.5
- kin_one: float32 [16, 16], replicated, may hold values from -1.5 to 1.5
- kin_two: float32 [16, 16], replicated, may hold values from -1.5 to 1.5
- kin_three: float32 [8, 8], replicated, may hold values from -2 to 2
- kin_four: float32 [8, 8], replicated, may hold values from -2 to 2
- kin_five: float32 [8, 8], replicated, may hold values from -2 to 2
- kin_six: float32 [8, 8], replicated, may hold values from -2 to 2
- coriolis_derivative: float32 [8, 8], replicated, may hold values from -2 to 2
Outputs:
- basis: float32 [16, 8, 16, 16, 8, 512], P('ka', None, 'mode', 'row')
- alpha: float32 [8, 8], replicated
- lower_factor: float32 [8, 8], replicated
The draws below stay inside these ranges and needn't reach their ends.
All inputs are finite; a program needn't handle non-finite values.
Results may differ from the reference program's by a relative error of at most 0.0003.
Values sent between devices are 32-bit elements; how exact they have to be, the bound alone decides.
A program may use at most 128 MiB of HBM per device.

```python
import math
import jax
import jax.numpy as jnp
from jax import lax

NV = 8
M1 = 16
M2 = 16
M3 = 8
M4 = 8
M5 = 8
M6 = 8
R = 512
KBLOCKS = 16


def block_levels(key, shape, split, least, high):
    def one(axis_at, blocks):
        heights = jax.random.uniform(jax.random.fold_in(jax.random.fold_in(key, 6), axis_at), (blocks,), jnp.float32, least / len(split), high / len(split))
        return jnp.repeat(jnp.exp(heights), shape[axis_at] // blocks).reshape((-1,) + (1,) * (len(shape) - axis_at - 1))

    factor_of = one(*split[0])
    for cut in split[1:]:
        factor_of = factor_of * one(*cut)
    return factor_of


def centred(key, extent, width, reach, shards=(), kind=jnp.bfloat16):
    array = jax.random.normal(key, extent, jnp.float32) * width
    if len(shards) > 0:
        array = block_levels(key, extent, shards, -0.22, 0.18) * array
    return jnp.clip(array, min=-reach, max=reach).astype(kind)


def setup_inputs(seed: int = 0) -> dict:
    splits = jax.random.split(jax.random.key(seed), 16)
    return {
        "vectors": centred(splits[0], (KBLOCKS, NV, M1, M2, M3, R), 1.0, 6.0, ((0, 16), (2, 8), (3, 4)), jnp.float32),
        "previous": centred(splits[1], (KBLOCKS, NV, M1, M2, M3, R), 1.0, 6.0, ((0, 16), (2, 8), (3, 4)), jnp.float32),
        "beta": centred(splits[2], (NV, NV), NV ** -0.5, 2.0, (), jnp.float32),
        "potential": jnp.clip(jnp.exp(math.log(10.0) - 4.6051702 * jax.random.uniform(splits[3], (M1, M2, M3, R), jnp.float32) ** block_levels(splits[3], (M1, M2, M3, R), ((0, 8), (1, 4)), -0.2, 0.2)), 0.1, 10.0),
        "coriolis_fn": jnp.clip(0.5 + 1.5 * jax.random.uniform(splits[4], (M1, M2, M3, R), jnp.float32) ** block_levels(splits[4], (M1, M2, M3, R), ((0, 8), (1, 4)), -0.2, 0.2), 0.5, 2.0),
        "second_fn": jnp.clip(0.5 + 1.5 * jax.random.uniform(splits[5], (M1, M2, M3, R), jnp.float32) ** block_levels(splits[5], (M1, M2, M3, R), ((0, 8), (1, 4)), -0.2, 0.2), 0.5, 2.0),
        "rot_const": jnp.clip(jnp.exp(jax.random.uniform(splits[6], (KBLOCKS,), jnp.float32, math.log(0.02), math.log(0.06))), 0.02, 0.06),
        "coupling": jnp.clip(jnp.exp(jax.random.uniform(splits[7], (2, KBLOCKS), jnp.float32, math.log(0.3), math.log(1.5))), 0.3, 1.5),
        "kin_one": centred(splits[8], (M1, M1), M1 ** -0.5, 1.5, (), jnp.float32),
        "kin_two": centred(splits[9], (M2, M2), M2 ** -0.5, 1.5, (), jnp.float32),
        "kin_three": centred(splits[10], (M3, M3), M3 ** -0.5, 2.0, (), jnp.float32),
        "kin_four": centred(splits[11], (M4, M4), M4 ** -0.5, 2.0, (), jnp.float32),
        "kin_five": centred(splits[12], (M5, M5), M5 ** -0.5, 2.0, (), jnp.float32),
        "kin_six": centred(splits[13], (M6, M6), M6 ** -0.5, 2.0, (), jnp.float32),
        "coriolis_derivative": centred(splits[14], (M6, M6), M6 ** -0.5, 2.0, (), jnp.float32),
    }


precise_mode = lax.Precision.HIGHEST

def symmetric(matrix):
    return 0.5 * (matrix + matrix.T)

def along(matrix, field, axis):
    moved = jnp.tensordot(field, matrix, axes=((axis,), (1,)), precision=precise_mode)
    return jnp.moveaxis(moved, -1, axis)

def reference(vectors, previous, beta, potential, coriolis_fn, second_fn, rot_const, coupling, kin_one, kin_two, kin_three, kin_four, kin_five, kin_six, coriolis_derivative):
    nblocks = vectors.shape[0]
    shape_seven = (NV, M1, M2, M3, M4, M5, M6)
    matrices = [symmetric(kin_one), symmetric(kin_two), symmetric(kin_three), symmetric(kin_four), symmetric(kin_five), symmetric(kin_six)]
    twist = 0.5 * (coriolis_derivative - coriolis_derivative.T)
    grid_six = (M1, M2, M3, M4, M5, M6)
    energy = potential.reshape(grid_six)
    twist_fn = coriolis_fn.reshape(grid_six)
    skip_fn = second_fn.reshape(grid_six)
    near_coef = coupling[0]
    far_coef = coupling[1]

    def pick(index):
        inside = (index >= 0) & (index < nblocks)
        safe = jnp.clip(index, 0, nblocks - 1).astype(jnp.int32)
        piece = lax.dynamic_index_in_dim(vectors, safe, 0, keepdims=False).reshape(shape_seven)
        return jnp.where(inside, piece, jnp.zeros_like(piece))

    def block(index):
        current = lax.dynamic_index_in_dim(vectors, index, 0, keepdims=False).reshape(shape_seven)
        result = along(matrices[0], current, 1)
        for number in range(1, 6):
            result = result + along(matrices[number], current, number + 1)
        level = (index - nblocks // 2).astype(rot_const.dtype)
        result = result + (energy + rot_const[index] * level * level) * current
        below_one = jnp.maximum(index - 1, 0)
        below_two = jnp.maximum(index - 2, 0)
        result = result + near_coef[index] * twist_fn * along(twist, pick(index + 1), 6)
        result = result + near_coef[below_one] * along(twist.T, twist_fn * pick(index - 1), 6)
        result = result + skip_fn * (far_coef[index] * pick(index + 2) + far_coef[below_two] * pick(index - 2))
        older = lax.dynamic_index_in_dim(previous, index, 0, keepdims=False).reshape(shape_seven)
        result = result - jnp.einsum('ij,jabcdef->iabcdef', beta, older, precision=precise_mode)
        return result.reshape(NV, -1)
    work = lax.map(block, jnp.arange(nblocks, dtype=jnp.int32))
    count = float(nblocks * work.shape[2])
    flat = vectors.reshape(nblocks, NV, -1)

    def inner(left, right):
        return jnp.einsum('kjc,kic->ji', left, right, precision=precise_mode) / count
    first = inner(flat, work)
    work = work - jnp.einsum('kjc,ji->kic', flat, first, precision=precise_mode)
    second = inner(flat, work)
    work = work - jnp.einsum('kjc,ji->kic', flat, second, precision=precise_mode)
    gram = inner(work, work)
    lower = jnp.linalg.cholesky(gram)
    inverse = jax.scipy.linalg.solve_triangular(lower, jnp.eye(NV, dtype=gram.dtype), lower=True)
    basis = jnp.einsum('ij,kjc->kic', inverse, work, precision=precise_mode)
    return (basis.reshape(vectors.shape), first + second, lower)
```

```python
import jax
import jax.numpy as jnp
from jax import lax
from jax.experimental import pallas as pl
from jax.experimental.pallas import tpu as pltpu
from jax.sharding import PartitionSpec as P

F32 = jnp.float32
BF16 = jnp.bfloat16
HI = lax.Precision.HIGHEST
LANES = 128
NT = (((1,), (1,)), ((), ()))


def exact(a, b):
    return jnp.dot(a, b, precision=HI, preferred_element_type=F32)


def exact_nt(a, b):
    return lax.dot_general(a, b, NT, precision=HI, preferred_element_type=F32)


def iota(shape, axis):
    return lax.broadcasted_iota(jnp.int32, shape, axis)


def hot(shape, of):
    return (of(iota(shape, 0)) == iota(shape, 1)).astype(F32)


def halves(x):
    high = x.astype(BF16)
    return high, (x - high.astype(F32)).astype(BF16)


def three_pass(x, high, low):
    xh, xl = halves(x)

    def dot(a, b):
        return jnp.dot(a, b, preferred_element_type=F32)

    return dot(xh, high) + (dot(xl, high) + dot(xh, low))


def splat(table, row):
    return table[pl.ds(row, 8, stride=0), :]


def lane_block(q):
    return pl.ds(q * LANES, LANES)


def spread(rows, left, right, table):
    n = left.shape[1]
    picked = left * (iota((rows, n), 0) % n == iota((rows, n), 1)).astype(F32)
    table[...] = exact(picked, jnp.ones((n, LANES), F32))


def kernel(
    vec,
    prev,
    pot,
    cor,
    sec,
    beta,
    rot,
    coupling,
    kin_one,
    kin_two,
    kin_three,
    kin_four,
    kin_five,
    kin_six,
    deriv,
    out,
    alpha,
    lower,
    v,
    pv,
    po,
    cf,
    sf,
    w,
    zin,
    zout,
    zret,
    rin,
    rout,
    rret,
    yb,
    ob,
    tab1,
    tab2,
    tabb,
    tab3,
    rows4,
    tkh,
    tkl,
    twh,
    twl,
    acc,
    coef,
    arb,
    loc,
    zfs,
    zfr,
    zrs,
    zrr,
    rfs,
    rfr,
    rrs,
    rrr,
    yfs,
    yfr,
    yrs,
    yrr,
    ars,
    arr,
    obs,
):
    ka = lax.axis_index("ka")
    z = lax.axis_index("mode")
    r = lax.axis_index("row")
    x_hi = ka // 8
    y = ka % 8
    nv, n1, n2 = v.shape[0], v.shape[1], v.shape[2]
    u = x_hi * 4 + r
    nblocks = 16

    def local_copy(i, src, dst):
        return pltpu.make_async_copy(src, dst, loc.at[i])

    locals_ = [
        local_copy(0, vec.at[0], v),
        local_copy(1, prev.at[0], pv),
        local_copy(2, pot, po),
        local_copy(3, cor, cf),
        local_copy(4, sec, sf),
        local_copy(5, vec.at[0, z], zin.at[z]),
        local_copy(6, vec.at[0, pl.ds(2 * r, 2)], rin.at[r]),
    ]

    def z_peer(o):
        return {"mode": (z + o) % 8}

    def y_peer(o):
        return {"ka": x_hi * 8 + (y + o) % 8}

    def x_peer(o):
        t = (u + o) % 8
        return {"ka": (t // 4) * 8 + y, "row": t % 4}

    def z_forward(c, o):
        t = (z + o) % 8
        return pltpu.make_async_remote_copy(
            vec.at[0, t, :, c],
            zin.at[z, :, c],
            zfs.at[c, o],
            zfr.at[c, o],
            device_id=z_peer(o),
        )

    def z_back(c, o):
        t = (z + o) % 8
        return pltpu.make_async_remote_copy(
            zout.at[t, :, c],
            zret.at[z, :, c],
            zrs.at[c, o],
            zrr.at[c, o],
            device_id=z_peer(o),
        )

    def r_forward(o):
        t = (r + o) % 4
        return pltpu.make_async_remote_copy(
            vec.at[0, pl.ds(2 * t, 2)],
            rin.at[r],
            rfs.at[o],
            rfr.at[o],
            device_id={"row": t},
        )

    def r_back(o):
        t = (r + o) % 4
        return pltpu.make_async_remote_copy(
            rout.at[t],
            rret.at[pl.ds(2 * r, 2)],
            rrs.at[o],
            rrr.at[o],
            device_id={"row": t},
        )

    def y_own(c, d):
        return pltpu.make_async_remote_copy(
            vec.at[0, :, :, c],
            yb.at[d, :, :, c],
            yfs.at[d, c],
            yfr.at[d, c],
            device_id={"ka": ka + 1 - 2 * d},
        )

    def y_relay(c, d):
        return pltpu.make_async_remote_copy(
            yb.at[d, :, :, c],
            yb.at[d + 2, :, :, c],
            yrs.at[d, c],
            yrr.at[d, c],
            device_id={"ka": ka + 1 - 2 * d},
        )

    can_send = (ka < nblocks - 1, ka > 0)
    has_one = (ka > 0, ka < nblocks - 1)
    has_two = (ka > 1, ka < nblocks - 2)

    barrier = pltpu.get_barrier_semaphore()
    edge = jnp.logical_or(ka == 7, ka == 8)

    @pl.loop(1, 8)
    def _(o):
        pl.semaphore_signal(barrier, inc=1, device_id=z_peer(o))
        pl.semaphore_signal(barrier, inc=1, device_id=y_peer(o))
        pl.semaphore_signal(barrier, inc=1, device_id=x_peer(o))

    @pl.when(edge)
    def _():
        pl.semaphore_signal(barrier, inc=1, device_id={"ka": 15 - ka})

    for copy in locals_:
        copy.start()
    pl.semaphore_wait(barrier, 21 + edge.astype(jnp.int32))

    def start_chunk(c):
        @pl.loop(1, 8)
        def _(o):
            z_forward(c, o).start()

        for d in range(2):

            @pl.when(can_send[d])
            def _():
                y_own(c, d).start()

    start_chunk(0)
    for o in range(1, 4):
        r_forward(o).start()
    for c in range(1, n2):
        start_chunk(c)

    for d in range(2):

        @pl.when(jnp.logical_not(has_one[d]))
        def _():
            yb[d] = jnp.zeros(yb.shape[1:], F32)

        @pl.when(jnp.logical_not(has_two[d]))
        def _():
            yb[d + 2] = jnp.zeros(yb.shape[1:], F32)

    def table_of(matrix, table):
        n = matrix.shape[0]
        pick = hot((n * n, n), lambda q: q // n)
        both = 0.5 * (exact(pick, matrix[...]) + exact_nt(pick, matrix[...]))
        spread(n * n, both, None, table)

    table_of(kin_one, tab1)
    table_of(kin_two, tab2)
    spread(64, exact(hot((64, 8), lambda q: q // 8), beta[...]), None, tabb)
    eye8 = hot((8, 8), lambda q: q)
    sym3 = 0.5 * (kin_three[...] + exact_nt(eye8, kin_three[...]))
    for s in range(8):
        mask = (iota((8, 8), 0) + (8 - s)) % 8 == iota((8, 8), 1)
        tab3[s] = exact(jnp.where(mask, sym3, 0.0), jnp.ones((8, LANES), F32))

    def expand(pick, matrix, pick_t):
        both = 0.5 * (exact(pick, matrix[...]) + exact_nt(pick, matrix[...]))
        return exact_nt(both, pick_t)

    rows4[...] = expand(eye8, kin_four, hot((512, 8), lambda q: q // 64))
    e5 = expand(hot((64, 8), lambda q: q // 8), kin_five, hot((512, 8), lambda q: (q // 8) % 8))
    e6 = expand(hot((64, 8), lambda q: q % 8), kin_six, hot((512, 8), lambda q: q % 8))
    qi = iota((64, 512), 0)
    pi = iota((64, 512), 1)
    m56 = jnp.where(pi % 8 == qi % 8, e5, 0.0) + jnp.where((pi // 8) % 8 == qi // 8, e6, 0.0)
    diag64 = pi % 64 == qi
    for k in range(8):
        block = jnp.where(diag64, rows4[k : k + 1, :], 0.0) + jnp.where(pi // 64 == k, m56, 0.0)
        high, low = halves(block)
        tkh[k * 64 : (k + 1) * 64, :] = high
        tkl[k * 64 : (k + 1) * 64, :] = low
    pick6 = hot((256, 8), lambda q: q % 8)
    turned = 0.5 * (exact_nt(pick6, deriv[...]) - exact(pick6, deriv[...]))
    full = jnp.where(iota((256, 256), 0) // 8 == iota((256, 256), 1) // 8, exact_nt(turned, pick6), 0.0)
    high, low = halves(full)
    twh[...] = high
    twl[...] = low
    acc[...] = jnp.zeros(acc.shape, F32)

    level = (ka - nblocks // 2).astype(F32)
    shift = rot[ka] * level * level
    near = coupling[0, ka]
    near_low = coupling[0, jnp.maximum(ka - 1, 0)]
    far = coupling[1, ka]
    far_low = coupling[1, jnp.maximum(ka - 2, 0)]

    def mix16(load, store, table):
        xs = [[load(b, q) for q in range(2)] for b in range(16)]
        for a in range(16):
            total = None
            for b in range(16):
                k = splat(table, a * 16 + b)
                terms = [k * xs[b][q] for q in range(2)]
                total = terms if total is None else [t + s for t, s in zip(total, terms)]
            for q in range(2):
                store(a, q, total[q])

    def first_mode(c):
        @pl.loop(0, 2)
        def _(h):
            def at(q):
                return pl.ds(pl.multiple_of(h * 256 + q * LANES, LANES), LANES)

            def load(b, q):
                return zin[b // 2, b % 2, c, :, at(q)]

            def store(a, q, val):
                zout[a // 2, a % 2, c, :, at(q)] = val

            mix16(load, store, tab1)

        zret[z, :, c] = zout[z, :, c]

    def second_mode():
        @pl.loop(0, 8)
        def _(k):
            n, m, h = k // 4, (k // 2) % 2, k % 2

            def at(q):
                return pl.ds(pl.multiple_of(h * 256 + q * LANES, LANES), LANES)

            def load(b, q):
                return rin[b // 4, n, m, b % 4, :, at(q)]

            def store(a, q, val):
                rout[a // 4, n, m, a % 4, :, at(q)] = val

            mix16(load, store, tab2)

        rret[pl.ds(2 * r, 2)] = rout[r]

    def gather_products(c, left, right, spots, triangle):
        for g in range(4):
            pairs = [(j, i) for i in (2 * g, 2 * g + 1) for j in range(8) if j <= i or not triangle]
            sums = {}
            for m in range(n1):
                for q in range(4):
                    ls = [left[j, m, c, :, lane_block(q)] for j in range(8)]
                    rs = [right[i, m, c, :, lane_block(q)] for i in (2 * g, 2 * g + 1)]
                    for j, i in pairs:
                        term = ls[j] * rs[i - 2 * g]
                        sums[j, i] = term if (j, i) not in sums else sums[j, i] + term
            for j, i in pairs:
                for spot in spots(j, i):
                    acc[spot * 8 : spot * 8 + 8, :] += sums[j, i]

    def local_terms(c):
        x = v[:, :, c].reshape(nv * n1 * 8, 512)
        w[:, :, c] = three_pass(x, tkh[...], tkl[...]).reshape(nv, n1, 8, 512)

        @pl.loop(0, 4)
        def _(k):
            m, h = k // 2, k % 2
            for q in range(2):
                at = pl.ds(pl.multiple_of(h * 256 + q * LANES, LANES), LANES)
                old = [pv[j, m, c, :, at] for j in range(8)]
                diag = po[m, c, :, at] + shift
                for i in range(8):
                    xi = v[i, m, c, :, at]
                    total = w[i, m, c, :, at] + (diag + tab3[0]) * xi
                    for s in range(1, 8):
                        total = total + tab3[s] * pltpu.roll(xi, s, axis=0)
                    taken = splat(tabb, i * 8) * old[0]
                    for j in range(1, 8):
                        taken = taken + splat(tabb, i * 8 + j) * old[j]
                    w[i, m, c, :, at] = total - taken

        gather_products(c, v, v, lambda j, i: {(8 + j) * 8 + i, (8 + i) * 8 + j}, True)

    def turn(x):
        flat = x.reshape(nv * n1 * 8, 512)
        parts = [three_pass(flat[:, h * 256 : h * 256 + 256], twh[...], twl[...]) for h in range(2)]
        return jnp.concatenate(parts, axis=1).reshape(x.shape)

    def near_terms(c):
        fn = cf[:, c][None]
        above = turn(yb[1, :, :, c])
        w[:, :, c] += (near * fn) * above
        below = turn(fn * yb[0, :, :, c])
        w[:, :, c] -= near_low * below

    def wait_recv_when(cond, copy):
        @pl.when(cond)
        def _():
            copy.wait_recv()

    for copy in locals_:
        copy.wait()

    @pl.loop(0, n2)
    def _(c):
        @pl.loop(1, 8)
        def _(o):
            z_forward(c, o).wait_recv()

        first_mode(c)

        @pl.loop(1, 8)
        def _(o):
            z_back(c, o).start()

        for d in range(2):
            wait_recv_when(has_one[d], y_own(c, d))

            @pl.when(jnp.logical_and(has_one[d], can_send[d]))
            def _():
                y_relay(c, d).start()

        @pl.when(c == 1)
        def _():
            for o in range(1, 4):
                r_forward(o).wait_recv()
            second_mode()
            for o in range(1, 4):
                r_back(o).start()

        local_terms(c)
        near_terms(c)

    for o in range(1, 4):
        r_back(o).wait_recv()

    @pl.loop(0, n2)
    def _(c):
        @pl.loop(1, 8)
        def _(o):
            z_back(c, o).wait_recv()

        for d in range(2):
            wait_recv_when(has_two[d], y_relay(c, d))

        @pl.loop(0, nv)
        def _(n):
            for m in range(n1):
                skip = sf[m, c] * (far * yb[3, n, m, c] + far_low * yb[2, n, m, c])
                w[n, m, c] = (w[n, m, c] + rret[n, m, c]) + (zret[n, m, c] + skip)

        gather_products(c, v, w, lambda j, i: (j * 8 + i, (24 + i) * 8 + j), False)
        gather_products(c, w, w, lambda j, i: {(16 + j) * 8 + i, (16 + i) * 8 + j}, True)

    part = acc[pl.ds(0, 256, stride=8), :]
    for s in range(1, 8):
        part = part + acc[pl.ds(s, 256, stride=8), :]
    sums = jnp.sum(part, axis=1, keepdims=True)
    lane = iota((8, LANES), 1)
    row = iota((8, LANES), 0)
    msg = jnp.zeros((8, LANES), F32)
    for l in range(32):
        msg = jnp.where(lane == l, sums[l * 8 : l * 8 + 8], msg)

    for s, (me, peer) in enumerate(((u, x_peer), (z, z_peer), (y, y_peer))):

        def ar_copy(o, s=s, me=me, peer=peer):
            return pltpu.make_async_remote_copy(
                arb.at[s, me], arb.at[s, me], ars.at[s, o], arr.at[s, o], device_id=peer(o)
            )

        arb[s, me] = msg

        @pl.loop(1, 8)
        def _(o):
            ar_copy(o).start()

        @pl.loop(1, 8)
        def _(o):
            ar_copy(o).wait_recv()

        msg = arb[s, 0]
        for t in range(1, 8):
            msg = msg + arb[s, t]

    msg = msg * (1.0 / float(16 * 8 * 4 * 32768))

    def col(a, k):
        return jnp.broadcast_to(a[:, k : k + 1], (8, LANES))

    def mm(a, b):
        total = col(a, 0) * b[0:1, :]
        for k in range(1, 8):
            total = total + col(a, k) * b[k : k + 1, :]
        return total

    first_t = msg
    overlap = pltpu.roll(msg, LANES - 8, axis=1)
    square = pltpu.roll(msg, LANES - 16, axis=1)
    first = pltpu.roll(msg, LANES - 24, axis=1)
    both_t = 2.0 * first_t - mm(first_t, overlap)
    both = 2.0 * first - mm(overlap, first)
    gram = square - mm(both_t, first) - mm(first_t, both) + mm(mm(both_t, overlap), both)
    alpha[...] = both[:, 0:8]
    work = jnp.where(lane < 8, gram, 0.0)
    work = jnp.where(lane == row + 8, 1.0, work)
    work = jnp.where((lane >= 16) & (lane < 24), pltpu.roll(both_t, 16, axis=1), work)
    factor = jnp.zeros((8, LANES), F32)
    for k in range(8):
        prow = jnp.broadcast_to(work[k : k + 1, :], (8, LANES))
        pivot = col(prow, k)
        column = col(work, k)
        root = lax.rsqrt(pivot)
        factor = jnp.where((lane == k) & (row >= k), column * root, factor)
        below = work - (column / pivot) * prow
        work = jnp.where(row > k, below, jnp.where(row == k, work * root, work))
    lower[...] = factor[:, 0:8]
    for j in range(8):
        coef[j * 8 : j * 8 + 8, :] = col(work, 8 + j)
        coef[64 + j * 8 : 72 + j * 8, :] = -col(work, 16 + j)

    def out_copy(c):
        return pltpu.make_async_copy(ob.at[:, :, c], out.at[0, :, :, c], obs.at[c])

    @pl.loop(0, n2)
    def _(c):
        @pl.loop(0, 4)
        def _(k):
            m, h = k // 2, k % 2
            at = [pl.ds(pl.multiple_of(h * 256 + q * LANES, LANES), LANES) for q in range(2)]
            vs = [[v[j, m, c, :, at[q]] for q in range(2)] for j in range(8)]
            ws = [[w[j, m, c, :, at[q]] for q in range(2)] for j in range(8)]
            for i in range(8):
                total = None
                for base, xs, count in ((64, vs, 8), (0, ws, i + 1)):
                    for j in range(count):
                        k_ = splat(coef, base + j * 8 + i)
                        terms = [k_ * xs[j][q] for q in range(2)]
                        total = terms if total is None else [t + s for t, s in zip(total, terms)]
                for q in range(2):
                    ob[i, m, c, :, at[q]] = total[q]

        out_copy(c).start()

    @pl.loop(0, n2)
    def _(c):
        out_copy(c).wait()

        @pl.loop(1, 8)
        def _(o):
            z_forward(c, o).wait_send()
            z_back(c, o).wait_send()

        for d in range(2):

            @pl.when(can_send[d])
            def _():
                y_own(c, d).wait_send()

            @pl.when(jnp.logical_and(has_one[d], can_send[d]))
            def _():
                y_relay(c, d).wait_send()

    for o in range(1, 4):
        r_forward(o).wait_send()
        r_back(o).wait_send()
    for s, (me, peer) in enumerate(((u, x_peer), (z, z_peer), (y, y_peer))):

        @pl.loop(1, 8)
        def _(o):
            pltpu.make_async_remote_copy(
                arb.at[s, me], arb.at[s, me], ars.at[s, o], arr.at[s, o], device_id=peer(o)
            ).wait_send()


def shards(*args):
    (vectors, previous, beta, potential, coriolis_fn, second_fn, rot_const, coupling, *mats) = args
    block = vectors.shape[1:]
    fn = potential.shape
    any_spec = pl.BlockSpec(memory_space=pl.ANY)
    vmem = pl.BlockSpec(memory_space=pltpu.VMEM)
    smem = pl.BlockSpec(memory_space=pltpu.SMEM)
    nv, n1, n2, n3, nr = block
    dma = pltpu.SemaphoreType.DMA
    scratch = [
        pltpu.VMEM(block, F32),
        pltpu.VMEM(block, F32),
        pltpu.VMEM(fn, F32),
        pltpu.VMEM(fn, F32),
        pltpu.VMEM(fn, F32),
        pltpu.VMEM(block, F32),
        pltpu.VMEM(block, F32),
        pltpu.VMEM(block, F32),
        pltpu.VMEM(block, F32),
        pltpu.VMEM((4, 2) + block[1:], F32),
        pltpu.VMEM((4, 2) + block[1:], F32),
        pltpu.VMEM(block, F32),
        pltpu.VMEM((4,) + block, F32),
        pltpu.VMEM(block, F32),
        pltpu.VMEM((256, LANES), F32),
        pltpu.VMEM((256, LANES), F32),
        pltpu.VMEM((64, LANES), F32),
        pltpu.VMEM((8, 8, LANES), F32),
        pltpu.VMEM((8, nr), F32),
        pltpu.VMEM((nr, nr), BF16),
        pltpu.VMEM((nr, nr), BF16),
        pltpu.VMEM((256, 256), BF16),
        pltpu.VMEM((256, 256), BF16),
        pltpu.VMEM((256 * 8, LANES), F32),
        pltpu.VMEM((128, LANES), F32),
        pltpu.VMEM((3, 8, 8, LANES), F32),
        dma((7,)),
        dma((n2, 8)),
        dma((n2, 8)),
        dma((n2, 8)),
        dma((n2, 8)),
        dma((4,)),
        dma((4,)),
        dma((4,)),
        dma((4,)),
        dma((2, n2)),
        dma((2, n2)),
        dma((2, n2)),
        dma((2, n2)),
        dma((3, 8)),
        dma((3, 8)),
        dma((n2,)),
    ]
    return pl.pallas_call(
        kernel,
        out_shape=(
            jax.ShapeDtypeStruct(vectors.shape, F32),
            jax.ShapeDtypeStruct((nv, nv), F32),
            jax.ShapeDtypeStruct((nv, nv), F32),
        ),
        in_specs=[any_spec] * 5 + [vmem, smem, smem] + [vmem] * 7,
        out_specs=(any_spec, vmem, vmem),
        scratch_shapes=scratch,
        compiler_params=pltpu.CompilerParams(
            collective_id=0, has_side_effects=True, vmem_limit_bytes=48 * 1024 * 1024
        ),
        name="lanczos",
    )(vectors, previous, potential, coriolis_fn, second_fn, beta, rot_const, coupling, *mats)


def solution(mesh):
    split = P("ka", None, "mode", "row", None, None)
    fn = P("mode", "row", None, None)
    return jax.shard_map(
        shards,
        mesh=mesh,
        in_specs=(split, split, P(), fn, fn, fn) + (P(),) * 9,
        out_specs=(split, P(), P()),
        check_vma=False,
    )
```

```python
import jax
import jax.numpy as jnp
from jax import lax
from jax.experimental import pallas as pl
from jax.experimental.pallas import tpu as pltpu
from jax.sharding import PartitionSpec as P

F32 = jnp.float32
BF16 = jnp.bfloat16
HI = lax.Precision.HIGHEST
LANES = 128
NT = (((1,), (1,)), ((), ()))


def exact(a, b):
    return jnp.dot(a, b, precision=HI, preferred_element_type=F32)


def exact_nt(a, b):
    return lax.dot_general(a, b, NT, precision=HI, preferred_element_type=F32)


def iota(shape, axis):
    return lax.broadcasted_iota(jnp.int32, shape, axis)


def hot(shape, of):
    return (of(iota(shape, 0)) == iota(shape, 1)).astype(F32)


def halves(x):
    high = x.astype(BF16)
    return high, (x - high.astype(F32)).astype(BF16)


def three_pass(x, high, low):
    xh, xl = halves(x)

    def dot(a, b):
        return jnp.dot(a, b, preferred_element_type=F32)

    return dot(xh, high) + (dot(xl, high) + dot(xh, low))


def splat(table, row):
    return table[pl.ds(row, 8, stride=0), :]


def lane_block(q):
    return pl.ds(q * LANES, LANES)


def spread(rows, left, right, table):
    n = left.shape[1]
    picked = left * (iota((rows, n), 0) % n == iota((rows, n), 1)).astype(F32)
    table[...] = exact(picked, jnp.ones((n, LANES), F32))


def kernel(
    vec,
    prev,
    pot,
    cor,
    sec,
    beta_hbm,
    rot_hbm,
    coupling_hbm,
    one_hbm,
    two_hbm,
    three_hbm,
    four_hbm,
    five_hbm,
    six_hbm,
    deriv_hbm,
    out,
    alpha,
    lower,
    v,
    pv,
    po,
    cf,
    sf,
    w,
    zin,
    zout,
    zret,
    rin,
    rout,
    rret,
    yb,
    via,
    ob,
    beta,
    rot,
    coupling,
    kin_one,
    kin_two,
    kin_three,
    kin_four,
    kin_five,
    kin_six,
    deriv,
    tab1,
    tab2,
    tabb,
    tab3,
    rows4,
    tkh,
    tkl,
    twh,
    twl,
    acc,
    coef,
    arb,
    loc,
    zfs,
    zfr,
    zrs,
    zrr,
    rfs,
    rfr,
    rrs,
    rrr,
    yfs,
    yfr,
    yrs,
    yrr,
    vr,
    vs,
    ars,
    arr,
    obs,
):
    ka = lax.axis_index("ka")
    z = lax.axis_index("mode")
    r = lax.axis_index("row")
    x_hi = ka // 8
    y = ka % 8
    nv, n1, n2 = v.shape[0], v.shape[1], v.shape[2]
    u = x_hi * 4 + r
    nblocks = 16

    def local_copy(i, src, dst):
        return pltpu.make_async_copy(src, dst, loc.at[i])

    locals_ = [
        local_copy(0, vec.at[0], v),
        local_copy(1, prev.at[0], pv),
        local_copy(2, pot, po),
        local_copy(3, cor, cf),
        local_copy(4, sec, sf),
        local_copy(5, vec.at[0, z], zin.at[z]),
        local_copy(6, vec.at[0, pl.ds(2 * r, 2)], rin.at[r]),
    ]
    small = [
        (beta_hbm, beta),
        (rot_hbm, rot),
        (coupling_hbm, coupling),
        (one_hbm, kin_one),
        (two_hbm, kin_two),
        (three_hbm, kin_three),
        (four_hbm, kin_four),
        (five_hbm, kin_five),
        (six_hbm, kin_six),
        (deriv_hbm, deriv),
    ]
    small = [local_copy(7 + i, *pair) for i, pair in enumerate(small)]

    def z_peer(o):
        return {"mode": (z + o) % 8}

    def y_peer(o):
        return {"ka": x_hi * 8 + (y + o) % 8}

    def x_peer(o):
        t = (u + o) % 8
        return {"ka": (t // 4) * 8 + y, "row": t % 4}

    def z_forward(c, o):
        t = (z + o) % 8
        return pltpu.make_async_remote_copy(
            vec.at[0, t, :, c],
            zin.at[z, :, c],
            zfs.at[c, o],
            zfr.at[c, o],
            device_id=z_peer(o),
        )

    def z_back(c, o):
        t = (z + o) % 8
        return pltpu.make_async_remote_copy(
            zout.at[t, :, c],
            zret.at[z, :, c],
            zrs.at[c, o],
            zrr.at[c, o],
            device_id=z_peer(o),
        )

    def r_forward(o):
        t = (r + o) % 4
        return pltpu.make_async_remote_copy(
            vec.at[0, pl.ds(2 * t, 2)],
            rin.at[r],
            rfs.at[o],
            rfr.at[o],
            device_id={"row": t},
        )

    def r_back(o):
        t = (r + o) % 4
        return pltpu.make_async_remote_copy(
            rout.at[t],
            rret.at[pl.ds(2 * r, 2)],
            rrs.at[o],
            rrr.at[o],
            device_id={"row": t},
        )

    def y_own(c, d):
        return pltpu.make_async_remote_copy(
            vec.at[0, :, :, c],
            yb.at[d, :, :, c],
            yfs.at[d, c],
            yfr.at[d, c],
            device_id={"ka": ka + 1 - 2 * d},
        )

    def y_relay(c, d):
        return pltpu.make_async_remote_copy(
            yb.at[d, :, :, c],
            yb.at[d + 2, :, :, c],
            yrs.at[d, c],
            yrr.at[d, c],
            device_id={"ka": ka + 1 - 2 * d},
        )

    def to_via(k, c, d):
        src = vec.at[0, :, :, c] if k == 0 else yb.at[d, :, :, c]
        return pltpu.make_async_remote_copy(
            src,
            via.at[k * 2 + c // 2],
            (yfs, yrs)[k].at[d, c],
            vr.at[k * 2 + c // 2],
            device_id={"ka": 15 - 15 * d},
        )

    def from_via(k, c, d):
        return pltpu.make_async_remote_copy(
            via.at[k * 2 + c // 2],
            yb.at[d + 2 * k, :, :, c],
            vs.at[k * 2 + c // 2],
            (yfr, yrr)[k].at[d, c],
            device_id={"ka": 8 - d},
        )

    at_edge = (ka == 7, ka == 8)
    is_via = (ka == 15, ka == 0)

    def send_on(k, c, d, cond):
        detour = jnp.logical_and(at_edge[d], c % 2 == 1)

        @pl.when(jnp.logical_and(cond, detour))
        def _():
            to_via(k, c, d).start()

        @pl.when(jnp.logical_and(cond, jnp.logical_not(detour)))
        def _():
            (y_own, y_relay)[k](c, d).start()

    def pass_on(k, c):
        for d in range(2):

            @pl.when(is_via[d])
            def _():
                to_via(k, c, d).wait_recv()
                from_via(k, c, d).start()

    can_send = (ka < nblocks - 1, ka > 0)
    has_one = (ka > 0, ka < nblocks - 1)
    has_two = (ka > 1, ka < nblocks - 2)

    barrier = pltpu.get_barrier_semaphore()
    edge = jnp.logical_or(ka == 7, ka == 8)

    @pl.loop(1, 8)
    def _(o):
        pl.semaphore_signal(barrier, inc=1, device_id=z_peer(o))
        pl.semaphore_signal(barrier, inc=1, device_id=y_peer(o))
        pl.semaphore_signal(barrier, inc=1, device_id=x_peer(o))

    @pl.when(edge)
    def _():
        pl.semaphore_signal(barrier, inc=1, device_id={"ka": 15 - ka})

    for copy in small + locals_:
        copy.start()
    pl.semaphore_wait(barrier, 21 + edge.astype(jnp.int32))

    def start_chunk(c):
        @pl.loop(1, 8)
        def _(o):
            z_forward(c, o).start()

        for d in range(2):

            send_on(0, c, d, can_send[d])

    start_chunk(0)
    for o in range(1, 4):
        r_forward(o).start()
    for c in range(1, n2):
        start_chunk(c)

    for d in range(2):

        @pl.when(jnp.logical_not(has_one[d]))
        def _():
            yb[d] = jnp.zeros(yb.shape[1:], F32)

        @pl.when(jnp.logical_not(has_two[d]))
        def _():
            yb[d + 2] = jnp.zeros(yb.shape[1:], F32)

    for copy in small:
        copy.wait()

    def table_of(matrix, table):
        n = matrix.shape[0]
        pick = hot((n * n, n), lambda q: q // n)
        both = 0.5 * (exact(pick, matrix[...]) + exact_nt(pick, matrix[...]))
        spread(n * n, both, None, table)

    table_of(kin_one, tab1)
    table_of(kin_two, tab2)
    spread(64, exact(hot((64, 8), lambda q: q // 8), beta[...]), None, tabb)
    eye8 = hot((8, 8), lambda q: q)
    sym3 = 0.5 * (kin_three[...] + exact_nt(eye8, kin_three[...]))
    for s in range(8):
        mask = (iota((8, 8), 0) + (8 - s)) % 8 == iota((8, 8), 1)
        tab3[s] = exact(jnp.where(mask, sym3, 0.0), jnp.ones((8, LANES), F32))

    def expand(pick, matrix, pick_t):
        both = 0.5 * (exact(pick, matrix[...]) + exact_nt(pick, matrix[...]))
        return exact_nt(both, pick_t)

    rows4[...] = expand(eye8, kin_four, hot((512, 8), lambda q: q // 64))
    e5 = expand(hot((64, 8), lambda q: q // 8), kin_five, hot((512, 8), lambda q: (q // 8) % 8))
    e6 = expand(hot((64, 8), lambda q: q % 8), kin_six, hot((512, 8), lambda q: q % 8))
    qi = iota((64, 512), 0)
    pi = iota((64, 512), 1)
    m56 = jnp.where(pi % 8 == qi % 8, e5, 0.0) + jnp.where((pi // 8) % 8 == qi // 8, e6, 0.0)
    diag64 = pi % 64 == qi
    for k in range(8):
        block = jnp.where(diag64, rows4[k : k + 1, :], 0.0) + jnp.where(pi // 64 == k, m56, 0.0)
        high, low = halves(block)
        tkh[k * 64 : (k + 1) * 64, :] = high
        tkl[k * 64 : (k + 1) * 64, :] = low
    pick6 = hot((256, 8), lambda q: q % 8)
    turned = 0.5 * (exact_nt(pick6, deriv[...]) - exact(pick6, deriv[...]))
    full = jnp.where(iota((256, 256), 0) // 8 == iota((256, 256), 1) // 8, exact_nt(turned, pick6), 0.0)
    high, low = halves(full)
    twh[...] = high
    twl[...] = low
    acc[...] = jnp.zeros(acc.shape, F32)

    level = (ka - nblocks // 2).astype(F32)
    shift = rot[ka] * level * level
    near = coupling[0, ka]
    near_low = coupling[0, jnp.maximum(ka - 1, 0)]
    far = coupling[1, ka]
    far_low = coupling[1, jnp.maximum(ka - 2, 0)]

    def mix16(load, store, table):
        xs = [[load(b, q) for q in range(2)] for b in range(16)]
        for a in range(16):
            total = None
            for b in range(16):
                k = splat(table, a * 16 + b)
                terms = [k * xs[b][q] for q in range(2)]
                total = terms if total is None else [t + s for t, s in zip(total, terms)]
            for q in range(2):
                store(a, q, total[q])

    def first_mode(c):
        @pl.loop(0, 2)
        def _(h):
            def at(q):
                return pl.ds(pl.multiple_of(h * 256 + q * LANES, LANES), LANES)

            def load(b, q):
                return zin[b // 2, b % 2, c, :, at(q)]

            def store(a, q, val):
                zout[a // 2, a % 2, c, :, at(q)] = val

            mix16(load, store, tab1)

        zret[z, :, c] = zout[z, :, c]

    def second_mode():
        @pl.loop(0, 8)
        def _(k):
            n, m, h = k // 4, (k // 2) % 2, k % 2

            def at(q):
                return pl.ds(pl.multiple_of(h * 256 + q * LANES, LANES), LANES)

            def load(b, q):
                return rin[b // 4, n, m, b % 4, :, at(q)]

            def store(a, q, val):
                rout[a // 4, n, m, a % 4, :, at(q)] = val

            mix16(load, store, tab2)

        rret[pl.ds(2 * r, 2)] = rout[r]

    def gather_products(c, left, right, spots, triangle):
        for g in range(4):
            pairs = [(j, i) for i in (2 * g, 2 * g + 1) for j in range(8) if j <= i or not triangle]
            sums = {}
            for m in range(n1):
                for q in range(4):
                    ls = [left[j, m, c, :, lane_block(q)] for j in range(8)]
                    rs = [right[i, m, c, :, lane_block(q)] for i in (2 * g, 2 * g + 1)]
                    for j, i in pairs:
                        term = ls[j] * rs[i - 2 * g]
                        sums[j, i] = term if (j, i) not in sums else sums[j, i] + term
            for j, i in pairs:
                for spot in spots(j, i):
                    acc[spot * 8 : spot * 8 + 8, :] += sums[j, i]

    def local_terms(c):
        x = v[:, :, c].reshape(nv * n1 * 8, 512)
        w[:, :, c] = three_pass(x, tkh[...], tkl[...]).reshape(nv, n1, 8, 512)

        @pl.loop(0, 4)
        def _(k):
            m, h = k // 2, k % 2
            for q in range(2):
                at = pl.ds(pl.multiple_of(h * 256 + q * LANES, LANES), LANES)
                old = [pv[j, m, c, :, at] for j in range(8)]
                diag = po[m, c, :, at] + shift
                for i in range(8):
                    xi = v[i, m, c, :, at]
                    total = w[i, m, c, :, at] + (diag + tab3[0]) * xi
                    for s in range(1, 8):
                        total = total + tab3[s] * pltpu.roll(xi, s, axis=0)
                    taken = splat(tabb, i * 8) * old[0]
                    for j in range(1, 8):
                        taken = taken + splat(tabb, i * 8 + j) * old[j]
                    w[i, m, c, :, at] = total - taken

        gather_products(c, v, v, lambda j, i: {(8 + j) * 8 + i, (8 + i) * 8 + j}, True)

    def turn(x):
        flat = x.reshape(nv * n1 * 8, 512)
        parts = [three_pass(flat[:, h * 256 : h * 256 + 256], twh[...], twl[...]) for h in range(2)]
        return jnp.concatenate(parts, axis=1).reshape(x.shape)

    def near_terms(c):
        fn = cf[:, c][None]
        above = turn(yb[1, :, :, c])
        w[:, :, c] += (near * fn) * above
        below = turn(fn * yb[0, :, :, c])
        w[:, :, c] -= near_low * below

    def wait_recv_when(cond, copy):
        @pl.when(cond)
        def _():
            copy.wait_recv()

    for copy in locals_:
        copy.wait()

    @pl.loop(0, n2)
    def _(c):
        @pl.loop(1, 8)
        def _(o):
            z_forward(c, o).wait_recv()

        first_mode(c)

        @pl.loop(1, 8)
        def _(o):
            z_back(c, o).start()

        for d in range(2):
            wait_recv_when(has_one[d], y_own(c, d))

            send_on(1, c, d, jnp.logical_and(has_one[d], can_send[d]))

        @pl.when(c % 2 == 1)
        def _():
            pass_on(0, c)

        @pl.when(c == 1)
        def _():
            for o in range(1, 4):
                r_forward(o).wait_recv()
            second_mode()
            for o in range(1, 4):
                r_back(o).start()

        local_terms(c)
        near_terms(c)

    for o in range(1, 4):
        r_back(o).wait_recv()

    @pl.loop(0, n2)
    def _(c):
        @pl.when(c < 2)
        def _():
            pass_on(1, 2 * c + 1)

        @pl.loop(1, 8)
        def _(o):
            z_back(c, o).wait_recv()

        for d in range(2):
            wait_recv_when(has_two[d], y_relay(c, d))

        @pl.loop(0, nv)
        def _(n):
            for m in range(n1):
                skip = sf[m, c] * (far * yb[3, n, m, c] + far_low * yb[2, n, m, c])
                w[n, m, c] = (w[n, m, c] + rret[n, m, c]) + (zret[n, m, c] + skip)

        gather_products(c, v, w, lambda j, i: (j * 8 + i, (24 + i) * 8 + j), False)
        gather_products(c, w, w, lambda j, i: {(16 + j) * 8 + i, (16 + i) * 8 + j}, True)

    part = acc[pl.ds(0, 256, stride=8), :]
    for s in range(1, 8):
        part = part + acc[pl.ds(s, 256, stride=8), :]
    sums = jnp.sum(part, axis=1, keepdims=True)
    lane = iota((8, LANES), 1)
    row = iota((8, LANES), 0)
    msg = jnp.zeros((8, LANES), F32)
    for l in range(32):
        msg = jnp.where(lane == l, sums[l * 8 : l * 8 + 8], msg)

    for s, (me, peer) in enumerate(((u, x_peer), (z, z_peer), (y, y_peer))):

        def ar_copy(o, s=s, me=me, peer=peer):
            return pltpu.make_async_remote_copy(
                arb.at[s, me], arb.at[s, me], ars.at[s, o], arr.at[s, o], device_id=peer(o)
            )

        arb[s, me] = msg

        @pl.loop(1, 8)
        def _(o):
            ar_copy(o).start()

        @pl.loop(1, 8)
        def _(o):
            ar_copy(o).wait_recv()

        msg = arb[s, 0]
        for t in range(1, 8):
            msg = msg + arb[s, t]

    msg = msg * (1.0 / float(16 * 8 * 4 * 32768))

    def col(a, k):
        return jnp.broadcast_to(a[:, k : k + 1], (8, LANES))

    def mm(a, b):
        total = col(a, 0) * b[0:1, :]
        for k in range(1, 8):
            total = total + col(a, k) * b[k : k + 1, :]
        return total

    first_t = msg
    overlap = pltpu.roll(msg, LANES - 8, axis=1)
    square = pltpu.roll(msg, LANES - 16, axis=1)
    first = pltpu.roll(msg, LANES - 24, axis=1)
    both_t = 2.0 * first_t - mm(first_t, overlap)
    both = 2.0 * first - mm(overlap, first)
    gram = square - mm(both_t, first) - mm(first_t, both) + mm(mm(both_t, overlap), both)
    alpha[...] = both[:, 0:8]
    work = jnp.where(lane < 8, gram, 0.0)
    work = jnp.where(lane == row + 8, 1.0, work)
    work = jnp.where((lane >= 16) & (lane < 24), pltpu.roll(both_t, 16, axis=1), work)
    factor = jnp.zeros((8, LANES), F32)
    for k in range(8):
        prow = jnp.broadcast_to(work[k : k + 1, :], (8, LANES))
        pivot = col(prow, k)
        column = col(work, k)
        root = lax.rsqrt(pivot)
        factor = jnp.where((lane == k) & (row >= k), column * root, factor)
        below = work - (column / pivot) * prow
        work = jnp.where(row > k, below, jnp.where(row == k, work * root, work))
    lower[...] = factor[:, 0:8]
    for j in range(8):
        coef[j * 8 : j * 8 + 8, :] = col(work, 8 + j)
        coef[64 + j * 8 : 72 + j * 8, :] = -col(work, 16 + j)

    def out_copy(c):
        return pltpu.make_async_copy(ob.at[:, :, c], out.at[0, :, :, c], obs.at[c])

    @pl.loop(0, n2)
    def _(c):
        @pl.loop(0, 4)
        def _(k):
            m, h = k // 2, k % 2
            at = [pl.ds(pl.multiple_of(h * 256 + q * LANES, LANES), LANES) for q in range(2)]
            vs = [[v[j, m, c, :, at[q]] for q in range(2)] for j in range(8)]
            ws = [[w[j, m, c, :, at[q]] for q in range(2)] for j in range(8)]
            for i in range(8):
                total = None
                for base, xs, count in ((64, vs, 8), (0, ws, i + 1)):
                    for j in range(count):
                        k_ = splat(coef, base + j * 8 + i)
                        terms = [k_ * xs[j][q] for q in range(2)]
                        total = terms if total is None else [t + s for t, s in zip(total, terms)]
                for q in range(2):
                    ob[i, m, c, :, at[q]] = total[q]

        out_copy(c).start()

    @pl.loop(0, n2)
    def _(c):
        out_copy(c).wait()

        @pl.loop(1, 8)
        def _(o):
            z_forward(c, o).wait_send()
            z_back(c, o).wait_send()

        for d in range(2):

            @pl.when(can_send[d])
            def _():
                y_own(c, d).wait_send()

            @pl.when(jnp.logical_and(has_one[d], can_send[d]))
            def _():
                y_relay(c, d).wait_send()

    for k in range(2):
        for c in (1, 3):
            for d in range(2):

                @pl.when(is_via[d])
                def _():
                    from_via(k, c, d).wait_send()

    for o in range(1, 4):
        r_forward(o).wait_send()
        r_back(o).wait_send()
    for s, (me, peer) in enumerate(((u, x_peer), (z, z_peer), (y, y_peer))):

        @pl.loop(1, 8)
        def _(o):
            pltpu.make_async_remote_copy(
                arb.at[s, me], arb.at[s, me], ars.at[s, o], arr.at[s, o], device_id=peer(o)
            ).wait_send()


def shards(*args):
    (vectors, previous, beta, potential, coriolis_fn, second_fn, rot_const, coupling, *mats) = args
    block = vectors.shape[1:]
    fn = potential.shape
    any_spec = pl.BlockSpec(memory_space=pltpu.HBM)
    vmem = pl.BlockSpec(memory_space=pltpu.VMEM)
    nv, n1, n2, n3, nr = block
    dma = pltpu.SemaphoreType.DMA
    scratch = [
        pltpu.VMEM(block, F32),
        pltpu.VMEM(block, F32),
        pltpu.VMEM(fn, F32),
        pltpu.VMEM(fn, F32),
        pltpu.VMEM(fn, F32),
        pltpu.VMEM(block, F32),
        pltpu.VMEM(block, F32),
        pltpu.VMEM(block, F32),
        pltpu.VMEM(block, F32),
        pltpu.VMEM((4, 2) + block[1:], F32),
        pltpu.VMEM((4, 2) + block[1:], F32),
        pltpu.VMEM(block, F32),
        pltpu.VMEM((4,) + block, F32),
        pltpu.VMEM((4, nv, n1, n3, nr), F32),
        pltpu.VMEM(block, F32),
        pltpu.VMEM((8, 8), F32),
        pltpu.SMEM((16,), F32),
        pltpu.SMEM((2, 16), F32),
        pltpu.VMEM((16, 16), F32),
        pltpu.VMEM((16, 16), F32),
        *[pltpu.VMEM((8, 8), F32)] * 5,
        pltpu.VMEM((256, LANES), F32),
        pltpu.VMEM((256, LANES), F32),
        pltpu.VMEM((64, LANES), F32),
        pltpu.VMEM((8, 8, LANES), F32),
        pltpu.VMEM((8, nr), F32),
        pltpu.VMEM((nr, nr), BF16),
        pltpu.VMEM((nr, nr), BF16),
        pltpu.VMEM((256, 256), BF16),
        pltpu.VMEM((256, 256), BF16),
        pltpu.VMEM((256 * 8, LANES), F32),
        pltpu.VMEM((128, LANES), F32),
        pltpu.VMEM((3, 8, 8, LANES), F32),
        dma((17,)),
        dma((n2, 8)),
        dma((n2, 8)),
        dma((n2, 8)),
        dma((n2, 8)),
        dma((4,)),
        dma((4,)),
        dma((4,)),
        dma((4,)),
        dma((2, n2)),
        dma((2, n2)),
        dma((2, n2)),
        dma((2, n2)),
        dma((4,)),
        dma((4,)),
        dma((3, 8)),
        dma((3, 8)),
        dma((n2,)),
    ]
    return pl.pallas_call(
        kernel,
        out_shape=(
            jax.ShapeDtypeStruct(vectors.shape, F32),
            jax.ShapeDtypeStruct((nv, nv), F32),
            jax.ShapeDtypeStruct((nv, nv), F32),
        ),
        in_specs=[any_spec] * 15,
        out_specs=(any_spec, vmem, vmem),
        scratch_shapes=scratch,
        compiler_params=pltpu.CompilerParams(
            collective_id=0, has_side_effects=True, vmem_limit_bytes=67043328
        ),
        name="lanczos",
    )(vectors, previous, potential, coriolis_fn, second_fn, beta, rot_const, coupling, *mats)


def solution(mesh):
    split = P("ka", None, "mode", "row", None, None)
    fn = P("mode", "row", None, None)
    return jax.shard_map(
        shards,
        mesh=mesh,
        in_specs=(split, split, P(), fn, fn, fn) + (P(),) * 9,
        out_specs=(split, P(), P()),
        check_vma=False,
    )
```

```python
import jax
import jax.numpy as jnp
from jax import lax
from jax.experimental import pallas as pl
from jax.experimental.pallas import tpu as pltpu
from jax.sharding import PartitionSpec as P

F32 = jnp.float32
BF16 = jnp.bfloat16
HI = lax.Precision.HIGHEST
LANES = 128
NT = (((1,), (1,)), ((), ()))


def exact(a, b):
    return jnp.dot(a, b, precision=HI, preferred_element_type=F32)


def exact_nt(a, b):
    return lax.dot_general(a, b, NT, precision=HI, preferred_element_type=F32)


def iota(shape, axis):
    return lax.broadcasted_iota(jnp.int32, shape, axis)


def hot(shape, of):
    return (of(iota(shape, 0)) == iota(shape, 1)).astype(F32)


def halves(x):
    high = x.astype(BF16)
    return high, (x - high.astype(F32)).astype(BF16)


def three_pass(x, high, low):
    xh, xl = halves(x)

    def dot(a, b):
        return jnp.dot(a, b, preferred_element_type=F32)

    return dot(xh, high) + (dot(xl, high) + dot(xh, low))


def col(a, k):
    return jnp.broadcast_to(a[:, k : k + 1], (8, LANES))


def splat(table, row):
    return table[pl.ds(row, 8, stride=0), :]


def far_first(i):
    return 4 + (i // 2) * (1 - 2 * (i % 2))


def lane_block(q):
    return pl.ds(q * LANES, LANES)


def spread(rows, left, right, table):
    n = left.shape[1]
    picked = left * (iota((rows, n), 0) % n == iota((rows, n), 1)).astype(F32)
    table[...] = exact(picked, jnp.ones((n, LANES), F32))


def kernel(
    vec,
    prev,
    pot,
    cor,
    sec,
    beta_hbm,
    rot_hbm,
    coupling_hbm,
    one_hbm,
    two_hbm,
    three_hbm,
    four_hbm,
    five_hbm,
    six_hbm,
    deriv_hbm,
    wout,
    pack,
    v,
    pv,
    po,
    cf,
    sf,
    w,
    zin,
    zout,
    zret,
    rin,
    rout,
    rret,
    yb,
    via,
    beta,
    rot,
    coupling,
    kin_one,
    kin_two,
    kin_three,
    kin_four,
    kin_five,
    kin_six,
    deriv,
    tab1,
    tab2,
    tabb,
    tab3,
    rows4,
    tkh,
    tkl,
    twh,
    twl,
    acc,
    arb,
    loc,
    zfs,
    zfr,
    zrs,
    zrr,
    rfs,
    rfr,
    rrs,
    rrr,
    yfs,
    yfr,
    yrs,
    yrr,
    vr,
    vs,
    ars,
    arr,
    obs,
):
    ka = lax.axis_index("ka")
    z = lax.axis_index("mode")
    r = lax.axis_index("row")
    x_hi = ka // 8
    y = ka % 8
    nv, n1, n2 = v.shape[0], v.shape[1], v.shape[2]
    u = x_hi * 4 + r
    nblocks = 16

    def local_copy(i, src, dst):
        return pltpu.make_async_copy(src, dst, loc.at[i])

    locals_ = [
        local_copy(0, vec.at[0], v),
        local_copy(1, prev.at[0], pv),
        local_copy(2, pot, po),
        local_copy(3, cor, cf),
        local_copy(4, sec, sf),
        local_copy(5, vec.at[0, z], zin.at[z]),
        local_copy(6, vec.at[0, pl.ds(2 * r, 2)], rin.at[r]),
    ]
    small = [
        (beta_hbm, beta),
        (rot_hbm, rot),
        (coupling_hbm, coupling),
        (one_hbm, kin_one),
        (two_hbm, kin_two),
        (three_hbm, kin_three),
        (four_hbm, kin_four),
        (five_hbm, kin_five),
        (six_hbm, kin_six),
        (deriv_hbm, deriv),
    ]
    small = [local_copy(7 + i, *pair) for i, pair in enumerate(small)]

    def z_peer(o):
        return {"mode": (z + o) % 8}

    def y_peer(o):
        return {"ka": x_hi * 8 + (y + o) % 8}

    def x_peer(o):
        t = (u + o) % 8
        return {"ka": (t // 4) * 8 + y, "row": t % 4}

    def z_forward(c, o):
        t = (z + o) % 8
        return pltpu.make_async_remote_copy(
            vec.at[0, t, :, c],
            zin.at[z, :, c],
            zfs.at[c, o],
            zfr.at[c, o],
            device_id=z_peer(o),
        )

    def z_back(c, o):
        t = (z + o) % 8
        return pltpu.make_async_remote_copy(
            zout.at[t, :, c],
            zret.at[z, :, c],
            zrs.at[c, o],
            zrr.at[c, o],
            device_id=z_peer(o),
        )

    def r_forward(o):
        t = (r + o) % 4
        return pltpu.make_async_remote_copy(
            vec.at[0, pl.ds(2 * t, 2)],
            rin.at[r],
            rfs.at[o],
            rfr.at[o],
            device_id={"row": t},
        )

    def r_back(o):
        t = (r + o) % 4
        return pltpu.make_async_remote_copy(
            rout.at[t],
            rret.at[pl.ds(2 * r, 2)],
            rrs.at[o],
            rrr.at[o],
            device_id={"row": t},
        )

    def y_own(c, d):
        return pltpu.make_async_remote_copy(
            vec.at[0, :, :, c],
            yb.at[d, :, :, c],
            yfs.at[d, c],
            yfr.at[d, c],
            device_id={"ka": ka + 1 - 2 * d},
        )

    def y_relay(c, d):
        return pltpu.make_async_remote_copy(
            yb.at[d, :, :, c],
            yb.at[d + 2, :, :, c],
            yrs.at[d, c],
            yrr.at[d, c],
            device_id={"ka": ka + 1 - 2 * d},
        )

    def to_via(k, c, d):
        src = vec.at[0, :, :, c] if k == 0 else yb.at[d, :, :, c]
        return pltpu.make_async_remote_copy(
            src,
            via.at[k * 2 + c // 2],
            (yfs, yrs)[k].at[d, c],
            vr.at[k * 2 + c // 2],
            device_id={"ka": 15 - 15 * d},
        )

    def from_via(k, c, d):
        return pltpu.make_async_remote_copy(
            via.at[k * 2 + c // 2],
            yb.at[d + 2 * k, :, :, c],
            vs.at[k * 2 + c // 2],
            (yfr, yrr)[k].at[d, c],
            device_id={"ka": 8 - d},
        )

    at_edge = (ka == 7, ka == 8)
    is_via = (ka == 15, ka == 0)

    def send_on(k, c, d, cond):
        detour = jnp.logical_and(at_edge[d], c % 2 == 1)

        @pl.when(jnp.logical_and(cond, detour))
        def _():
            to_via(k, c, d).start()

        @pl.when(jnp.logical_and(cond, jnp.logical_not(detour)))
        def _():
            (y_own, y_relay)[k](c, d).start()

    def pass_on(k, c):
        for d in range(2):

            @pl.when(is_via[d])
            def _():
                to_via(k, c, d).wait_recv()
                from_via(k, c, d).start()

    can_send = (ka < nblocks - 1, ka > 0)
    has_one = (ka > 0, ka < nblocks - 1)
    has_two = (ka > 1, ka < nblocks - 2)

    barrier = pltpu.get_barrier_semaphore()
    edge = jnp.logical_or(ka == 7, ka == 8)

    @pl.loop(1, 8)
    def _(o):
        pl.semaphore_signal(barrier, inc=1, device_id=z_peer(o))
        pl.semaphore_signal(barrier, inc=1, device_id=y_peer(o))
        pl.semaphore_signal(barrier, inc=1, device_id=x_peer(o))

    @pl.when(edge)
    def _():
        pl.semaphore_signal(barrier, inc=1, device_id={"ka": 15 - ka})

    for copy in small + locals_:
        copy.start()
    pl.semaphore_wait(barrier, 21 + edge.astype(jnp.int32))

    def start_chunk(c):
        @pl.loop(1, 8)
        def _(o):
            z_forward(c, far_first(o)).start()

        for d in range(2):

            send_on(0, c, d, can_send[d])

    start_chunk(0)
    for o in range(1, 4):
        r_forward(o).start()
    for c in range(1, n2):
        start_chunk(c)

    for d in range(2):

        @pl.when(jnp.logical_not(has_one[d]))
        def _():
            yb[d] = jnp.zeros(yb.shape[1:], F32)

        @pl.when(jnp.logical_not(has_two[d]))
        def _():
            yb[d + 2] = jnp.zeros(yb.shape[1:], F32)

    for copy in small:
        copy.wait()

    def table_of(matrix, table):
        n = matrix.shape[0]
        pick = hot((n * n, n), lambda q: q // n)
        both = 0.5 * (exact(pick, matrix[...]) + exact_nt(pick, matrix[...]))
        spread(n * n, both, None, table)

    table_of(kin_one, tab1)
    table_of(kin_two, tab2)
    spread(64, exact(hot((64, 8), lambda q: q // 8), beta[...]), None, tabb)
    eye8 = hot((8, 8), lambda q: q)
    sym3 = 0.5 * (kin_three[...] + exact_nt(eye8, kin_three[...]))
    for s in range(8):
        mask = (iota((8, 8), 0) + (8 - s)) % 8 == iota((8, 8), 1)
        tab3[s] = exact(jnp.where(mask, sym3, 0.0), jnp.ones((8, LANES), F32))

    def expand(pick, matrix, pick_t):
        both = 0.5 * (exact(pick, matrix[...]) + exact_nt(pick, matrix[...]))
        return exact_nt(both, pick_t)

    rows4[...] = expand(eye8, kin_four, hot((512, 8), lambda q: q // 64))
    e5 = expand(hot((64, 8), lambda q: q // 8), kin_five, hot((512, 8), lambda q: (q // 8) % 8))
    e6 = expand(hot((64, 8), lambda q: q % 8), kin_six, hot((512, 8), lambda q: q % 8))
    qi = iota((64, 512), 0)
    pi = iota((64, 512), 1)
    m56 = jnp.where(pi % 8 == qi % 8, e5, 0.0) + jnp.where((pi // 8) % 8 == qi // 8, e6, 0.0)
    diag64 = pi % 64 == qi
    for k in range(8):
        block = jnp.where(diag64, rows4[k : k + 1, :], 0.0) + jnp.where(pi // 64 == k, m56, 0.0)
        high, low = halves(block)
        tkh[k * 64 : (k + 1) * 64, :] = high
        tkl[k * 64 : (k + 1) * 64, :] = low
    pick6 = hot((256, 8), lambda q: q % 8)
    turned = 0.5 * (exact_nt(pick6, deriv[...]) - exact(pick6, deriv[...]))
    full = jnp.where(iota((256, 256), 0) // 8 == iota((256, 256), 1) // 8, exact_nt(turned, pick6), 0.0)
    high, low = halves(full)
    twh[...] = high
    twl[...] = low
    acc[...] = jnp.zeros(acc.shape, F32)

    level = (ka - nblocks // 2).astype(F32)
    shift = rot[ka] * level * level
    near = coupling[0, ka]
    near_low = coupling[0, jnp.maximum(ka - 1, 0)]
    far = coupling[1, ka]
    far_low = coupling[1, jnp.maximum(ka - 2, 0)]

    def mix16(load, store, table):
        xs = [[load(b, q) for q in range(2)] for b in range(16)]
        for a in range(16):
            total = None
            for b in range(16):
                k = splat(table, a * 16 + b)
                terms = [k * xs[b][q] for q in range(2)]
                total = terms if total is None else [t + s for t, s in zip(total, terms)]
            for q in range(2):
                store(a, q, total[q])

    def first_mode(c):
        @pl.loop(0, 2)
        def _(h):
            def at(q):
                return pl.ds(pl.multiple_of(h * 256 + q * LANES, LANES), LANES)

            def load(b, q):
                return zin[b // 2, b % 2, c, :, at(q)]

            def store(a, q, val):
                zout[a // 2, a % 2, c, :, at(q)] = val

            mix16(load, store, tab1)

        zret[z, :, c] = zout[z, :, c]

    def second_mode():
        @pl.loop(0, 8)
        def _(k):
            n, m, h = k // 4, (k // 2) % 2, k % 2

            def at(q):
                return pl.ds(pl.multiple_of(h * 256 + q * LANES, LANES), LANES)

            def load(b, q):
                return rin[b // 4, n, m, b % 4, :, at(q)]

            def store(a, q, val):
                rout[a // 4, n, m, a % 4, :, at(q)] = val

            mix16(load, store, tab2)

        rret[pl.ds(2 * r, 2)] = rout[r]

    def gather_products(c, left, right, spots, triangle):
        for g in range(4):
            pairs = [(j, i) for i in (2 * g, 2 * g + 1) for j in range(8) if j <= i or not triangle]
            sums = {}
            for m in range(n1):
                for q in range(4):
                    ls = [left[j, m, c, :, lane_block(q)] for j in range(8)]
                    rs = [right[i, m, c, :, lane_block(q)] for i in (2 * g, 2 * g + 1)]
                    for j, i in pairs:
                        term = ls[j] * rs[i - 2 * g]
                        sums[j, i] = term if (j, i) not in sums else sums[j, i] + term
            for j, i in pairs:
                for spot in spots(j, i):
                    acc[spot * 8 : spot * 8 + 8, :] += sums[j, i]

    def local_terms(c):
        x = v[:, :, c].reshape(nv * n1 * 8, 512)
        w[:, :, c] = three_pass(x, tkh[...], tkl[...]).reshape(nv, n1, 8, 512)

        @pl.loop(0, 4)
        def _(k):
            m, h = k // 2, k % 2
            for q in range(2):
                at = pl.ds(pl.multiple_of(h * 256 + q * LANES, LANES), LANES)
                old = [pv[j, m, c, :, at] for j in range(8)]
                diag = po[m, c, :, at] + shift
                for i in range(8):
                    xi = v[i, m, c, :, at]
                    total = w[i, m, c, :, at] + (diag + tab3[0]) * xi
                    for s in range(1, 8):
                        total = total + tab3[s] * pltpu.roll(xi, s, axis=0)
                    taken = splat(tabb, i * 8) * old[0]
                    for j in range(1, 8):
                        taken = taken + splat(tabb, i * 8 + j) * old[j]
                    w[i, m, c, :, at] = total - taken

        gather_products(c, v, v, lambda j, i: {(8 + j) * 8 + i, (8 + i) * 8 + j}, True)

    def turn(x):
        flat = x.reshape(nv * n1 * 8, 512)
        parts = [three_pass(flat[:, h * 256 : h * 256 + 256], twh[...], twl[...]) for h in range(2)]
        return jnp.concatenate(parts, axis=1).reshape(x.shape)

    def near_terms(c):
        fn = cf[:, c][None]
        above = turn(yb[1, :, :, c])
        w[:, :, c] += (near * fn) * above
        below = turn(fn * yb[0, :, :, c])
        w[:, :, c] -= near_low * below

    def wait_recv_when(cond, copy):
        @pl.when(cond)
        def _():
            copy.wait_recv()

    for copy in locals_:
        copy.wait()

    @pl.loop(0, n2)
    def _(c):
        @pl.loop(1, 8)
        def _(o):
            z_forward(c, o).wait_recv()

        first_mode(c)

        @pl.loop(1, 8)
        def _(o):
            z_back(c, far_first(o)).start()

        for d in range(2):
            wait_recv_when(has_one[d], y_own(c, d))

            send_on(1, c, d, jnp.logical_and(has_one[d], can_send[d]))

        @pl.when(c % 2 == 1)
        def _():
            pass_on(0, c)

        @pl.when(c == 2)
        def _():
            for o in range(1, 4):
                r_forward(o).wait_recv()
            second_mode()
            for o in range(1, 4):
                r_back(o).start()

        local_terms(c)
        near_terms(c)

    def w_copy(c):
        return pltpu.make_async_copy(w.at[:, :, c], wout.at[:, :, c], obs.at[c])

    for c in (1, 3):
        pass_on(1, c)
    for o in range(1, 4):
        r_back(o).wait_recv()

    @pl.loop(0, n2)
    def _(c):
        @pl.loop(1, 8)
        def _(o):
            z_back(c, o).wait_recv()

        for d in range(2):
            wait_recv_when(has_two[d], y_relay(c, d))

        @pl.loop(0, nv)
        def _(n):
            for m in range(n1):
                skip = sf[m, c] * (far * yb[3, n, m, c] + far_low * yb[2, n, m, c])
                w[n, m, c] = (w[n, m, c] + rret[n, m, c]) + (zret[n, m, c] + skip)

        w_copy(c).start()
        gather_products(c, v, w, lambda j, i: (j * 8 + i, (24 + i) * 8 + j), False)
        gather_products(c, w, w, lambda j, i: {(16 + j) * 8 + i, (16 + i) * 8 + j}, True)

    part = acc[pl.ds(0, 256, stride=8), :]
    for s in range(1, 8):
        part = part + acc[pl.ds(s, 256, stride=8), :]
    sums = jnp.sum(part, axis=1, keepdims=True)
    lane = iota((8, LANES), 1)
    row = iota((8, LANES), 0)
    msg = jnp.zeros((8, LANES), F32)
    for l in range(32):
        msg = jnp.where(lane == l, sums[l * 8 : l * 8 + 8], msg)

    for s, (me, peer) in enumerate(((u, x_peer), (z, z_peer), (y, y_peer))):

        def ar_copy(o, s=s, me=me, peer=peer):
            return pltpu.make_async_remote_copy(
                arb.at[s, me], arb.at[s, me], ars.at[s, o], arr.at[s, o], device_id=peer(o)
            )

        arb[s, me] = msg

        @pl.loop(1, 8)
        def _(o):
            ar_copy(o).start()

        @pl.loop(1, 8)
        def _(o):
            ar_copy(o).wait_recv()

        msg = arb[s, 0]
        for t in range(1, 8):
            msg = msg + arb[s, t]

    msg = msg * (1.0 / float(16 * 8 * 4 * 32768))

    def mm(a, b):
        total = col(a, 0) * b[0:1, :]
        for k in range(1, 8):
            total = total + col(a, k) * b[k : k + 1, :]
        return total

    first_t = msg
    overlap = pltpu.roll(msg, LANES - 8, axis=1)
    square = pltpu.roll(msg, LANES - 16, axis=1)
    first = pltpu.roll(msg, LANES - 24, axis=1)
    both_t = 2.0 * first_t - mm(first_t, overlap)
    both = 2.0 * first - mm(overlap, first)
    gram = square - mm(both_t, first) - mm(first_t, both) + mm(mm(both_t, overlap), both)
    work = jnp.where(lane < 8, gram, 0.0)
    work = jnp.where(lane == row + 8, 1.0, work)
    work = jnp.where((lane >= 16) & (lane < 24), pltpu.roll(both_t, 16, axis=1), work)
    factor = jnp.zeros((8, LANES), F32)
    for k in range(8):
        prow = jnp.broadcast_to(work[k : k + 1, :], (8, LANES))
        pivot = col(prow, k)
        column = col(work, k)
        root = lax.rsqrt(pivot)
        factor = jnp.where((lane == k) & (row >= k), column * root, factor)
        below = work - (column / pivot) * prow
        work = jnp.where(row > k, below, jnp.where(row == k, work * root, work))
    pack[0] = work
    pack[1] = both
    pack[2] = factor

    @pl.loop(0, n2)
    def _(c):
        w_copy(c).wait()

        @pl.loop(1, 8)
        def _(o):
            z_forward(c, o).wait_send()
            z_back(c, o).wait_send()

        for d in range(2):

            @pl.when(can_send[d])
            def _():
                y_own(c, d).wait_send()

            @pl.when(jnp.logical_and(has_one[d], can_send[d]))
            def _():
                y_relay(c, d).wait_send()

    for k in range(2):
        for c in (1, 3):
            for d in range(2):

                @pl.when(is_via[d])
                def _():
                    from_via(k, c, d).wait_send()

    for o in range(1, 4):
        r_forward(o).wait_send()
        r_back(o).wait_send()
    for s, (me, peer) in enumerate(((u, x_peer), (z, z_peer), (y, y_peer))):

        @pl.loop(1, 8)
        def _(o):
            pltpu.make_async_remote_copy(
                arb.at[s, me], arb.at[s, me], ars.at[s, o], arr.at[s, o], device_id=peer(o)
            ).wait_send()


def finish(vec, wfin, pack_hbm, out, alpha_hbm, lower_hbm, v, w, ob, pack, coef, small, sem):
    n2 = v.shape[2]

    def loads(c):
        return (
            pltpu.make_async_copy(vec.at[0, :, :, c], v.at[:, :, c], sem.at[0, c]),
            pltpu.make_async_copy(wfin.at[:, :, c], w.at[:, :, c], sem.at[1, c]),
        )

    first = pltpu.make_async_copy(pack_hbm, pack, sem.at[3, 0])
    first.start()
    for c in range(n2):
        for copy in loads(c):
            copy.start()
    first.wait()
    small[0] = pack[1, :, 0:8]
    small[1] = pack[2, :, 0:8]
    tiny = [
        pltpu.make_async_copy(small.at[0], alpha_hbm, sem.at[3, 1]),
        pltpu.make_async_copy(small.at[1], lower_hbm, sem.at[3, 2]),
    ]
    for copy in tiny:
        copy.start()
    work = pack[0]
    for j in range(8):
        coef[j * 8 : j * 8 + 8, :] = col(work, 8 + j)
        coef[64 + j * 8 : 72 + j * 8, :] = -col(work, 16 + j)

    def out_copy(c):
        return pltpu.make_async_copy(ob.at[:, :, c], out.at[0, :, :, c], sem.at[2, c])

    @pl.loop(0, n2)
    def _(c):
        for copy in loads(c):
            copy.wait()

        @pl.loop(0, 4)
        def _(k):
            m, h = k // 2, k % 2
            at = [pl.ds(pl.multiple_of(h * 256 + q * LANES, LANES), LANES) for q in range(2)]
            vs = [[v[j, m, c, :, at[q]] for q in range(2)] for j in range(8)]
            ws = [[w[j, m, c, :, at[q]] for q in range(2)] for j in range(8)]
            for i in range(8):
                total = None
                for base, xs, count in ((64, vs, 8), (0, ws, i + 1)):
                    for j in range(count):
                        factor = splat(coef, base + j * 8 + i)
                        terms = [factor * xs[j][q] for q in range(2)]
                        total = terms if total is None else [t + s for t, s in zip(total, terms)]
                for q in range(2):
                    ob[i, m, c, :, at[q]] = total[q]

        out_copy(c).start()

    @pl.loop(0, n2)
    def _(c):
        out_copy(c).wait()

    for copy in tiny:
        copy.wait()


def shards(*args):
    (vectors, previous, beta, potential, coriolis_fn, second_fn, rot_const, coupling, *mats) = args
    block = vectors.shape[1:]
    fn = potential.shape
    any_spec = pl.BlockSpec(memory_space=pltpu.HBM)
    vmem = pl.BlockSpec(memory_space=pltpu.VMEM)
    nv, n1, n2, n3, nr = block
    dma = pltpu.SemaphoreType.DMA
    scratch = [
        pltpu.VMEM(block, F32),
        pltpu.VMEM(block, F32),
        pltpu.VMEM(fn, F32),
        pltpu.VMEM(fn, F32),
        pltpu.VMEM(fn, F32),
        pltpu.VMEM(block, F32),
        pltpu.VMEM(block, F32),
        pltpu.VMEM(block, F32),
        pltpu.VMEM(block, F32),
        pltpu.VMEM((4, 2) + block[1:], F32),
        pltpu.VMEM((4, 2) + block[1:], F32),
        pltpu.VMEM(block, F32),
        pltpu.VMEM((4,) + block, F32),
        pltpu.VMEM((4, nv, n1, n3, nr), F32),
        pltpu.VMEM((8, 8), F32),
        pltpu.SMEM((16,), F32),
        pltpu.SMEM((2, 16), F32),
        pltpu.VMEM((16, 16), F32),
        pltpu.VMEM((16, 16), F32),
        *[pltpu.VMEM((8, 8), F32)] * 5,
        pltpu.VMEM((256, LANES), F32),
        pltpu.VMEM((256, LANES), F32),
        pltpu.VMEM((64, LANES), F32),
        pltpu.VMEM((8, 8, LANES), F32),
        pltpu.VMEM((8, nr), F32),
        pltpu.VMEM((nr, nr), BF16),
        pltpu.VMEM((nr, nr), BF16),
        pltpu.VMEM((256, 256), BF16),
        pltpu.VMEM((256, 256), BF16),
        pltpu.VMEM((256 * 8, LANES), F32),
        pltpu.VMEM((3, 8, 8, LANES), F32),
        dma((17,)),
        dma((n2, 8)),
        dma((n2, 8)),
        dma((n2, 8)),
        dma((n2, 8)),
        dma((4,)),
        dma((4,)),
        dma((4,)),
        dma((4,)),
        dma((2, n2)),
        dma((2, n2)),
        dma((2, n2)),
        dma((2, n2)),
        dma((4,)),
        dma((4,)),
        dma((3, 8)),
        dma((3, 8)),
        dma((n2,)),
    ]
    wfin, pack = pl.pallas_call(
        kernel,
        out_shape=(
            jax.ShapeDtypeStruct(block, F32),
            jax.ShapeDtypeStruct((3, nv, LANES), F32),
        ),
        in_specs=[any_spec] * 15,
        out_specs=(any_spec, vmem),
        scratch_shapes=scratch,
        compiler_params=pltpu.CompilerParams(
            collective_id=0, has_side_effects=True, vmem_limit_bytes=67043328
        ),
        name="lanczos",
    )(vectors, previous, potential, coriolis_fn, second_fn, beta, rot_const, coupling, *mats)
    return pl.pallas_call(
        finish,
        out_shape=(
            jax.ShapeDtypeStruct(vectors.shape, F32),
            jax.ShapeDtypeStruct((nv, nv), F32),
            jax.ShapeDtypeStruct((nv, nv), F32),
        ),
        in_specs=[any_spec] * 3,
        out_specs=(any_spec,) * 3,
        scratch_shapes=[
            pltpu.VMEM(block, F32),
            pltpu.VMEM(block, F32),
            pltpu.VMEM(block, F32),
            pltpu.VMEM((3, nv, LANES), F32),
            pltpu.VMEM((128, LANES), F32),
            pltpu.VMEM((2, nv, nv), F32),
            dma((4, n2)),
        ],
        compiler_params=pltpu.CompilerParams(vmem_limit_bytes=67043328),
        name="basis",
    )(vectors, wfin, pack)


def solution(mesh):
    split = P("ka", None, "mode", "row", None, None)
    fn = P("mode", "row", None, None)
    return jax.shard_map(
        shards,
        mesh=mesh,
        in_specs=(split, split, P(), fn, fn, fn) + (P(),) * 9,
        out_specs=(split, P(), P()),
        check_vma=False,
    )
```

```python
import jax
import jax.numpy as jnp
from jax import lax
from jax.experimental import pallas as pl
from jax.experimental.pallas import tpu as pltpu
from jax.sharding import PartitionSpec as P

F32 = jnp.float32
BF16 = jnp.bfloat16
HI = lax.Precision.HIGHEST
LANES = 128
NT = (((1,), (1,)), ((), ()))


def exact(a, b):
    return jnp.dot(a, b, precision=HI, preferred_element_type=F32)


def exact_nt(a, b):
    return lax.dot_general(a, b, NT, precision=HI, preferred_element_type=F32)


def iota(shape, axis):
    return lax.broadcasted_iota(jnp.int32, shape, axis)


def hot(shape, of):
    return (of(iota(shape, 0)) == iota(shape, 1)).astype(F32)


def halves(x):
    high = x.astype(BF16)
    return high, (x - high.astype(F32)).astype(BF16)


def three_pass(x, high, low):
    xh, xl = halves(x)

    def dot(a, b):
        return jnp.dot(a, b, preferred_element_type=F32)

    return dot(xh, high) + (dot(xl, high) + dot(xh, low))


def col(a, k):
    return jnp.broadcast_to(a[:, k : k + 1], (8, LANES))


def splat(table, row):
    return table[pl.ds(row, 8, stride=0), :]


def far_first(i):
    return 4 + (i // 2) * (1 - 2 * (i % 2))


def lane_block(q):
    return pl.ds(q * LANES, LANES)


def spread(rows, left, right, table):
    n = left.shape[1]
    picked = left * (iota((rows, n), 0) % n == iota((rows, n), 1)).astype(F32)
    table[...] = exact(picked, jnp.ones((n, LANES), F32))


def kernel(
    vec,
    prev,
    pot,
    cor,
    sec,
    beta_hbm,
    rot_hbm,
    coupling_hbm,
    one_hbm,
    two_hbm,
    three_hbm,
    four_hbm,
    five_hbm,
    six_hbm,
    deriv_hbm,
    wout,
    pack,
    v,
    pv,
    po,
    cf,
    sf,
    w,
    zin,
    zout,
    zret,
    rin,
    rout,
    rret,
    yb,
    via,
    beta,
    rot,
    coupling,
    kin_one,
    kin_two,
    kin_three,
    kin_four,
    kin_five,
    kin_six,
    deriv,
    tab1,
    tab2,
    tabb,
    tab3,
    rows4,
    tkh,
    tkl,
    twh,
    twl,
    acc,
    total,
    arb,
    loc,
    zfs,
    zfr,
    zrs,
    zrr,
    rfs,
    rfr,
    rrs,
    rrr,
    yfs,
    yfr,
    yrs,
    yrr,
    vr,
    vs,
    ars,
    arr,
    obs,
):
    ka = lax.axis_index("ka")
    z = lax.axis_index("mode")
    r = lax.axis_index("row")
    x_hi = ka // 8
    y = ka % 8
    nv, n1, n2 = v.shape[0], v.shape[1], v.shape[2]
    u = x_hi * 4 + r
    nblocks = 16

    def local_copy(i, src, dst):
        return pltpu.make_async_copy(src, dst, loc.at[i])

    locals_ = [
        local_copy(0, vec.at[0], v),
        local_copy(1, prev.at[0], pv),
        local_copy(2, pot, po),
        local_copy(3, cor, cf),
        local_copy(4, sec, sf),
        local_copy(5, vec.at[0, z], zin.at[z]),
        local_copy(6, vec.at[0, pl.ds(2 * r, 2)], rin.at[r]),
    ]
    small = [
        (beta_hbm, beta),
        (rot_hbm, rot),
        (coupling_hbm, coupling),
        (one_hbm, kin_one),
        (two_hbm, kin_two),
        (three_hbm, kin_three),
        (four_hbm, kin_four),
        (five_hbm, kin_five),
        (six_hbm, kin_six),
        (deriv_hbm, deriv),
    ]
    small = [local_copy(7 + i, *pair) for i, pair in enumerate(small)]

    def z_peer(o):
        return {"mode": (z + o) % 8}

    def y_peer(o):
        return {"ka": x_hi * 8 + (y + o) % 8}

    def x_peer(o):
        t = (u + o) % 8
        return {"ka": (t // 4) * 8 + y, "row": t % 4}

    def z_forward(c, o):
        t = (z + o) % 8
        return pltpu.make_async_remote_copy(
            vec.at[0, t, :, c],
            zin.at[z, :, c],
            zfs.at[c, o],
            zfr.at[c, o],
            device_id=z_peer(o),
        )

    def z_back(c, o):
        t = (z + o) % 8
        return pltpu.make_async_remote_copy(
            zout.at[t, :, c],
            zret.at[z, :, c],
            zrs.at[c, o],
            zrr.at[c, o],
            device_id=z_peer(o),
        )

    def r_forward(o):
        t = (r + o) % 4
        return pltpu.make_async_remote_copy(
            vec.at[0, pl.ds(2 * t, 2)],
            rin.at[r],
            rfs.at[o],
            rfr.at[o],
            device_id={"row": t},
        )

    def r_back(o):
        t = (r + o) % 4
        return pltpu.make_async_remote_copy(
            rout.at[t],
            rret.at[pl.ds(2 * r, 2)],
            rrs.at[o],
            rrr.at[o],
            device_id={"row": t},
        )

    def y_own(c, d):
        return pltpu.make_async_remote_copy(
            vec.at[0, :, :, c],
            yb.at[d, :, :, c],
            yfs.at[d, c],
            yfr.at[d, c],
            device_id={"ka": ka + 1 - 2 * d},
        )

    def y_relay(c, d):
        return pltpu.make_async_remote_copy(
            yb.at[d, :, :, c],
            yb.at[d + 2, :, :, c],
            yrs.at[d, c],
            yrr.at[d, c],
            device_id={"ka": ka + 1 - 2 * d},
        )

    def to_via(k, c, d):
        src = vec.at[0, :, :, c] if k == 0 else yb.at[d, :, :, c]
        return pltpu.make_async_remote_copy(
            src,
            via.at[k * 2 + c // 2],
            (yfs, yrs)[k].at[d, c],
            vr.at[k * 2 + c // 2],
            device_id={"ka": 15 - 15 * d},
        )

    def from_via(k, c, d):
        return pltpu.make_async_remote_copy(
            via.at[k * 2 + c // 2],
            yb.at[d + 2 * k, :, :, c],
            vs.at[k * 2 + c // 2],
            (yfr, yrr)[k].at[d, c],
            device_id={"ka": 8 - d},
        )

    at_edge = (ka == 7, ka == 8)
    is_via = (ka == 15, ka == 0)

    def send_on(k, c, d, cond):
        detour = jnp.logical_and(at_edge[d], c % 2 == 1)

        @pl.when(jnp.logical_and(cond, detour))
        def _():
            to_via(k, c, d).start()

        @pl.when(jnp.logical_and(cond, jnp.logical_not(detour)))
        def _():
            (y_own, y_relay)[k](c, d).start()

    def pass_on(k, c):
        for d in range(2):

            @pl.when(is_via[d])
            def _():
                to_via(k, c, d).wait_recv()
                from_via(k, c, d).start()

    can_send = (ka < nblocks - 1, ka > 0)
    has_one = (ka > 0, ka < nblocks - 1)
    has_two = (ka > 1, ka < nblocks - 2)

    barrier = pltpu.get_barrier_semaphore()
    edge = jnp.logical_or(ka == 7, ka == 8)

    for i in range(1, 8):
        for peer in (z_peer, y_peer, x_peer):
            pl.semaphore_signal(barrier, inc=1, device_id=peer(far_first(i)))

    @pl.when(edge)
    def _():
        pl.semaphore_signal(barrier, inc=1, device_id={"ka": 15 - ka})

    pl.semaphore_wait(barrier, 21 + edge.astype(jnp.int32))

    def start_chunk(c):
        @pl.loop(1, 8)
        def _(o):
            z_forward(c, far_first(o)).start()

        for d in range(2):

            send_on(0, c, d, can_send[d])

    start_chunk(0)
    for o in range(1, 4):
        r_forward(o).start()
    for copy in small + locals_:
        copy.start()
    for c in range(1, n2):
        start_chunk(c)

    for d in range(2):

        @pl.when(jnp.logical_not(has_one[d]))
        def _():
            yb[d] = jnp.zeros(yb.shape[1:], F32)

        @pl.when(jnp.logical_not(has_two[d]))
        def _():
            yb[d + 2] = jnp.zeros(yb.shape[1:], F32)

    for copy in small:
        copy.wait()

    def table_of(matrix, table):
        n = matrix.shape[0]
        pick = hot((n * n, n), lambda q: q // n)
        both = 0.5 * (exact(pick, matrix[...]) + exact_nt(pick, matrix[...]))
        spread(n * n, both, None, table)

    table_of(kin_one, tab1)
    table_of(kin_two, tab2)
    spread(64, exact(hot((64, 8), lambda q: q // 8), beta[...]), None, tabb)
    eye8 = hot((8, 8), lambda q: q)
    sym3 = 0.5 * (kin_three[...] + exact_nt(eye8, kin_three[...]))
    for s in range(8):
        mask = (iota((8, 8), 0) + (8 - s)) % 8 == iota((8, 8), 1)
        tab3[s] = exact(jnp.where(mask, sym3, 0.0), jnp.ones((8, LANES), F32))

    def expand(pick, matrix, pick_t):
        both = 0.5 * (exact(pick, matrix[...]) + exact_nt(pick, matrix[...]))
        return exact_nt(both, pick_t)

    rows4[...] = expand(eye8, kin_four, hot((512, 8), lambda q: q // 64))
    e5 = expand(hot((64, 8), lambda q: q // 8), kin_five, hot((512, 8), lambda q: (q // 8) % 8))
    e6 = expand(hot((64, 8), lambda q: q % 8), kin_six, hot((512, 8), lambda q: q % 8))
    qi = iota((64, 512), 0)
    pi = iota((64, 512), 1)
    m56 = jnp.where(pi % 8 == qi % 8, e5, 0.0) + jnp.where((pi // 8) % 8 == qi // 8, e6, 0.0)
    diag64 = pi % 64 == qi
    for k in range(8):
        block = jnp.where(diag64, rows4[k : k + 1, :], 0.0) + jnp.where(pi // 64 == k, m56, 0.0)
        high, low = halves(block)
        tkh[k * 64 : (k + 1) * 64, :] = high
        tkl[k * 64 : (k + 1) * 64, :] = low
    pick6 = hot((256, 8), lambda q: q % 8)
    turned = 0.5 * (exact_nt(pick6, deriv[...]) - exact(pick6, deriv[...]))
    full = jnp.where(iota((256, 256), 0) // 8 == iota((256, 256), 1) // 8, exact_nt(turned, pick6), 0.0)
    high, low = halves(full)
    twh[...] = high
    twl[...] = low
    acc[...] = jnp.zeros(acc.shape, F32)

    level = (ka - nblocks // 2).astype(F32)
    shift = rot[ka] * level * level
    near = coupling[0, ka]
    near_low = coupling[0, jnp.maximum(ka - 1, 0)]
    far = coupling[1, ka]
    far_low = coupling[1, jnp.maximum(ka - 2, 0)]

    def mix16(load, store, table):
        xs = [[load(b, q) for q in range(2)] for b in range(16)]
        for a in range(16):
            total = None
            for b in range(16):
                k = splat(table, a * 16 + b)
                terms = [k * xs[b][q] for q in range(2)]
                total = terms if total is None else [t + s for t, s in zip(total, terms)]
            for q in range(2):
                store(a, q, total[q])

    def first_mode(c):
        @pl.loop(0, 2)
        def _(h):
            def at(q):
                return pl.ds(pl.multiple_of(h * 256 + q * LANES, LANES), LANES)

            def load(b, q):
                return zin[b // 2, b % 2, c, :, at(q)]

            def store(a, q, val):
                zout[a // 2, a % 2, c, :, at(q)] = val

            mix16(load, store, tab1)

        zret[z, :, c] = zout[z, :, c]

    def second_mode():
        @pl.loop(0, 8)
        def _(k):
            n, m, h = k // 4, (k // 2) % 2, k % 2

            def at(q):
                return pl.ds(pl.multiple_of(h * 256 + q * LANES, LANES), LANES)

            def load(b, q):
                return rin[b // 4, n, m, b % 4, :, at(q)]

            def store(a, q, val):
                rout[a // 4, n, m, a % 4, :, at(q)] = val

            mix16(load, store, tab2)

        rret[pl.ds(2 * r, 2)] = rout[r]

    def gather_products(c, left, right, spots, triangle):
        for g in range(4):
            pairs = [(j, i) for i in (2 * g, 2 * g + 1) for j in range(8) if j <= i or not triangle]
            sums = {}
            for m in range(n1):
                for q in range(4):
                    ls = [left[j, m, c, :, lane_block(q)] for j in range(8)]
                    rs = [right[i, m, c, :, lane_block(q)] for i in (2 * g, 2 * g + 1)]
                    for j, i in pairs:
                        term = ls[j] * rs[i - 2 * g]
                        sums[j, i] = term if (j, i) not in sums else sums[j, i] + term
            for j, i in pairs:
                for spot in spots(j, i):
                    acc[spot * 8 : spot * 8 + 8, :] += sums[j, i]

    def local_terms(c):
        x = v[:, :, c].reshape(nv * n1 * 8, 512)
        w[:, :, c] = three_pass(x, tkh[...], tkl[...]).reshape(nv, n1, 8, 512)

        @pl.loop(0, 4)
        def _(k):
            m, h = k // 2, k % 2
            for q in range(2):
                at = pl.ds(pl.multiple_of(h * 256 + q * LANES, LANES), LANES)
                old = [pv[j, m, c, :, at] for j in range(8)]
                diag = po[m, c, :, at] + shift
                for i in range(8):
                    xi = v[i, m, c, :, at]
                    total = w[i, m, c, :, at] + (diag + tab3[0]) * xi
                    for s in range(1, 8):
                        total = total + tab3[s] * pltpu.roll(xi, s, axis=0)
                    taken = splat(tabb, i * 8) * old[0]
                    for j in range(1, 8):
                        taken = taken + splat(tabb, i * 8 + j) * old[j]
                    w[i, m, c, :, at] = total - taken

        gather_products(c, v, v, lambda j, i: {(24 + j) * 8 + i, (24 + i) * 8 + j}, True)

    def turn(x):
        flat = x.reshape(nv * n1 * 8, 512)
        parts = [three_pass(flat[:, h * 256 : h * 256 + 256], twh[...], twl[...]) for h in range(2)]
        return jnp.concatenate(parts, axis=1).reshape(x.shape)

    def near_terms(c):
        fn = cf[:, c][None]
        above = turn(yb[1, :, :, c])
        w[:, :, c] += (near * fn) * above
        below = turn(fn * yb[0, :, :, c])
        w[:, :, c] -= near_low * below

    def wait_recv_when(cond, copy):
        @pl.when(cond)
        def _():
            copy.wait_recv()

    for copy in locals_:
        copy.wait()

    @pl.loop(0, n2)
    def _(c):
        @pl.loop(1, 8)
        def _(o):
            z_forward(c, o).wait_recv()

        first_mode(c)

        @pl.loop(1, 8)
        def _(o):
            z_back(c, far_first(o)).start()

        for d in range(2):
            wait_recv_when(has_one[d], y_own(c, d))

            send_on(1, c, d, jnp.logical_and(has_one[d], can_send[d]))

        @pl.when(c % 2 == 1)
        def _():
            pass_on(0, c)

        @pl.when(c == 2)
        def _():
            for o in range(1, 4):
                r_forward(o).wait_recv()
            second_mode()
            for o in range(1, 4):
                r_back(o).start()

        local_terms(c)
        near_terms(c)

    lane = iota((8, LANES), 1)
    row = iota((8, LANES), 0)

    def sum_into(count, shift, at):
        rows = count * 8
        part = acc[pl.ds(at * 64, rows, stride=8), :]
        for s in range(1, 8):
            part = part + acc[pl.ds(at * 64 + s, rows, stride=8), :]
        sums = jnp.sum(part, axis=1, keepdims=True)
        msg = total[...]
        for l in range(count):
            msg = jnp.where(lane == l + shift, sums[l * 8 : l * 8 + 8], msg)
        total[...] = msg

    total[...] = jnp.zeros((8, LANES), F32)
    sum_into(8, 0, 24)

    def w_copy(c):
        return pltpu.make_async_copy(w.at[:, :, c], wout.at[:, :, c], obs.at[c])

    for c in (1, 3):
        pass_on(1, c)

    @pl.loop(0, n2)
    def _(c):
        @pl.loop(1, 8)
        def _(o):
            z_forward(c, o).wait_send()

        for d in range(2):

            @pl.when(can_send[d])
            def _():
                y_own(c, d).wait_send()

    for o in range(1, 4):
        r_forward(o).wait_send()

    def wait_sends_back():
        @pl.loop(0, n2)
        def _(c):
            w_copy(c).wait()

            @pl.loop(1, 8)
            def _(o):
                z_back(c, o).wait_send()

            for d in range(2):

                @pl.when(jnp.logical_and(has_one[d], can_send[d]))
                def _():
                    y_relay(c, d).wait_send()

        for k in range(2):
            for c in (1, 3):
                for d in range(2):

                    @pl.when(is_via[d])
                    def _():
                        from_via(k, c, d).wait_send()

        for o in range(1, 4):
            r_back(o).wait_send()

    for o in range(1, 4):
        r_back(o).wait_recv()

    @pl.loop(0, n2)
    def _(c):
        @pl.loop(1, 8)
        def _(o):
            z_back(c, o).wait_recv()

        for d in range(2):
            wait_recv_when(has_two[d], y_relay(c, d))

        @pl.loop(0, nv)
        def _(n):
            for m in range(n1):
                skip = sf[m, c] * (far * yb[3, n, m, c] + far_low * yb[2, n, m, c])
                w[n, m, c] = (w[n, m, c] + rret[n, m, c]) + (zret[n, m, c] + skip)

        w_copy(c).start()
        gather_products(c, v, w, lambda j, i: (j * 8 + i, (16 + i) * 8 + j), False)
        gather_products(c, w, w, lambda j, i: {(8 + j) * 8 + i, (8 + i) * 8 + j}, True)

    sum_into(24, 8, 0)
    msg = total[...]

    groups = ((u, x_peer), (z, z_peer), (y, y_peer))

    def ar_copy(g, o):
        me, peer = groups[g]
        return pltpu.make_async_remote_copy(
            arb.at[g, me], arb.at[g, me], ars.at[g, o], arr.at[g, o], device_id=peer(o)
        )

    for g in range(3):
        arb[g, groups[g][0]] = msg
        for i in range(1, 8):
            ar_copy(g, far_first(i)).start()
        if g == 0:
            wait_sends_back()
        else:
            for i in range(1, 8):
                ar_copy(g - 1, i).wait_send()
        for i in range(1, 8):
            ar_copy(g, i).wait_recv()
        msg = arb[g, 0]
        for t in range(1, 8):
            msg = msg + arb[g, t]

    msg = msg * (1.0 / float(16 * 8 * 4 * 32768))

    def mm(a, b):
        total = col(a, 0) * b[0:1, :]
        for k in range(1, 8):
            total = total + col(a, k) * b[k : k + 1, :]
        return total

    overlap = msg
    first_t = pltpu.roll(msg, LANES - 8, axis=1)
    square = pltpu.roll(msg, LANES - 16, axis=1)
    first = pltpu.roll(msg, LANES - 24, axis=1)
    both_t = 2.0 * first_t - mm(first_t, overlap)
    both = 2.0 * first - mm(overlap, first)
    gram = square - mm(both_t, first) - mm(first_t, both) + mm(mm(both_t, overlap), both)
    work = jnp.where(lane < 8, gram, 0.0)
    work = jnp.where(lane == row + 8, 1.0, work)
    work = jnp.where((lane >= 16) & (lane < 24), pltpu.roll(both_t, 16, axis=1), work)
    factor = jnp.zeros((8, LANES), F32)
    for k in range(8):
        prow = jnp.broadcast_to(work[k : k + 1, :], (8, LANES))
        pivot = col(prow, k)
        column = col(work, k)
        root = lax.rsqrt(pivot)
        factor = jnp.where((lane == k) & (row >= k), column * root, factor)
        below = work - (column / pivot) * prow
        work = jnp.where(row > k, below, jnp.where(row == k, work * root, work))
    pack[0] = work
    pack[1] = both
    pack[2] = factor

    for i in range(1, 8):
        ar_copy(2, i).wait_send()


def finish(vec, wfin, pack_hbm, out, alpha_hbm, lower_hbm, v, w, ob, pack, coef, small, sem):
    n2 = v.shape[2]

    def loads(c):
        return (
            pltpu.make_async_copy(vec.at[0, :, :, c], v.at[:, :, c], sem.at[0, c]),
            pltpu.make_async_copy(wfin.at[:, :, c], w.at[:, :, c], sem.at[1, c]),
        )

    first = pltpu.make_async_copy(pack_hbm, pack, sem.at[3, 0])
    first.start()
    for c in range(n2):
        for copy in loads(c):
            copy.start()
    first.wait()
    small[0] = pack[1, :, 0:8]
    small[1] = pack[2, :, 0:8]
    tiny = [
        pltpu.make_async_copy(small.at[0], alpha_hbm, sem.at[3, 1]),
        pltpu.make_async_copy(small.at[1], lower_hbm, sem.at[3, 2]),
    ]
    for copy in tiny:
        copy.start()
    work = pack[0]
    for j in range(8):
        coef[j * 8 : j * 8 + 8, :] = col(work, 8 + j)
        coef[64 + j * 8 : 72 + j * 8, :] = -col(work, 16 + j)

    def out_copy(c):
        return pltpu.make_async_copy(ob.at[:, :, c], out.at[0, :, :, c], sem.at[2, c])

    @pl.loop(0, n2)
    def _(c):
        for copy in loads(c):
            copy.wait()

        @pl.loop(0, 4)
        def _(k):
            m, h = k // 2, k % 2
            at = [pl.ds(pl.multiple_of(h * 256 + q * LANES, LANES), LANES) for q in range(2)]
            vs = [[v[j, m, c, :, at[q]] for q in range(2)] for j in range(8)]
            ws = [[w[j, m, c, :, at[q]] for q in range(2)] for j in range(8)]
            for i in range(8):
                total = None
                for base, xs, count in ((64, vs, 8), (0, ws, i + 1)):
                    for j in range(count):
                        factor = splat(coef, base + j * 8 + i)
                        terms = [factor * xs[j][q] for q in range(2)]
                        total = terms if total is None else [t + s for t, s in zip(total, terms)]
                for q in range(2):
                    ob[i, m, c, :, at[q]] = total[q]

        out_copy(c).start()

    @pl.loop(0, n2)
    def _(c):
        out_copy(c).wait()

    for copy in tiny:
        copy.wait()


def shards(*args):
    (vectors, previous, beta, potential, coriolis_fn, second_fn, rot_const, coupling, *mats) = args
    block = vectors.shape[1:]
    fn = potential.shape
    any_spec = pl.BlockSpec(memory_space=pltpu.HBM)
    vmem = pl.BlockSpec(memory_space=pltpu.VMEM)
    nv, n1, n2, n3, nr = block
    dma = pltpu.SemaphoreType.DMA
    scratch = [
        pltpu.VMEM(block, F32),
        pltpu.VMEM(block, F32),
        pltpu.VMEM(fn, F32),
        pltpu.VMEM(fn, F32),
        pltpu.VMEM(fn, F32),
        pltpu.VMEM(block, F32),
        pltpu.VMEM(block, F32),
        pltpu.VMEM(block, F32),
        pltpu.VMEM(block, F32),
        pltpu.VMEM((4, 2) + block[1:], F32),
        pltpu.VMEM((4, 2) + block[1:], F32),
        pltpu.VMEM(block, F32),
        pltpu.VMEM((4,) + block, F32),
        pltpu.VMEM((4, nv, n1, n3, nr), F32),
        pltpu.VMEM((8, 8), F32),
        pltpu.SMEM((16,), F32),
        pltpu.SMEM((2, 16), F32),
        pltpu.VMEM((16, 16), F32),
        pltpu.VMEM((16, 16), F32),
        *[pltpu.VMEM((8, 8), F32)] * 5,
        pltpu.VMEM((256, LANES), F32),
        pltpu.VMEM((256, LANES), F32),
        pltpu.VMEM((64, LANES), F32),
        pltpu.VMEM((8, 8, LANES), F32),
        pltpu.VMEM((8, nr), F32),
        pltpu.VMEM((nr, nr), BF16),
        pltpu.VMEM((nr, nr), BF16),
        pltpu.VMEM((256, 256), BF16),
        pltpu.VMEM((256, 256), BF16),
        pltpu.VMEM((256 * 8, LANES), F32),
        pltpu.VMEM((8, LANES), F32),
        pltpu.VMEM((3, 8, 8, LANES), F32),
        dma((17,)),
        dma((n2, 8)),
        dma((n2, 8)),
        dma((n2, 8)),
        dma((n2, 8)),
        dma((4,)),
        dma((4,)),
        dma((4,)),
        dma((4,)),
        dma((2, n2)),
        dma((2, n2)),
        dma((2, n2)),
        dma((2, n2)),
        dma((4,)),
        dma((4,)),
        dma((3, 8)),
        dma((3, 8)),
        dma((n2,)),
    ]
    wfin, pack = pl.pallas_call(
        kernel,
        out_shape=(
            jax.ShapeDtypeStruct(block, F32),
            jax.ShapeDtypeStruct((3, nv, LANES), F32),
        ),
        in_specs=[any_spec] * 15,
        out_specs=(any_spec, vmem),
        scratch_shapes=scratch,
        compiler_params=pltpu.CompilerParams(
            collective_id=0, has_side_effects=True, vmem_limit_bytes=67043328
        ),
        name="lanczos",
    )(vectors, previous, potential, coriolis_fn, second_fn, beta, rot_const, coupling, *mats)
    return pl.pallas_call(
        finish,
        out_shape=(
            jax.ShapeDtypeStruct(vectors.shape, F32),
            jax.ShapeDtypeStruct((nv, nv), F32),
            jax.ShapeDtypeStruct((nv, nv), F32),
        ),
        in_specs=[any_spec] * 3,
        out_specs=(any_spec,) * 3,
        scratch_shapes=[
            pltpu.VMEM(block, F32),
            pltpu.VMEM(block, F32),
            pltpu.VMEM(block, F32),
            pltpu.VMEM((3, nv, LANES), F32),
            pltpu.VMEM((128, LANES), F32),
            pltpu.VMEM((2, nv, nv), F32),
            dma((4, n2)),
        ],
        compiler_params=pltpu.CompilerParams(vmem_limit_bytes=67043328),
        name="basis",
    )(vectors, wfin, pack)


def solution(mesh):
    split = P("ka", None, "mode", "row", None, None)
    fn = P("mode", "row", None, None)
    return jax.shard_map(
        shards,
        mesh=mesh,
        in_specs=(split, split, P(), fn, fn, fn) + (P(),) * 9,
        out_specs=(split, P(), P()),
        check_vma=False,
    )
```

```python
import jax
import jax.numpy as jnp
from jax import lax
from jax.experimental import pallas as pl
from jax.experimental.pallas import tpu as pltpu
from jax.sharding import PartitionSpec as P

F32 = jnp.float32
BF16 = jnp.bfloat16
HI = lax.Precision.HIGHEST
LANES = 128
VIA = 2
NT = (((1,), (1,)), ((), ()))


def exact(a, b):
    return jnp.dot(a, b, precision=HI, preferred_element_type=F32)


def exact_nt(a, b):
    return lax.dot_general(a, b, NT, precision=HI, preferred_element_type=F32)


def iota(shape, axis):
    return lax.broadcasted_iota(jnp.int32, shape, axis)


def hot(shape, of):
    return (of(iota(shape, 0)) == iota(shape, 1)).astype(F32)


def halves(x):
    high = x.astype(BF16)
    return high, (x - high.astype(F32)).astype(BF16)


def three_pass(x, high, low):
    xh, xl = halves(x)

    def dot(a, b):
        return jnp.dot(a, b, preferred_element_type=F32)

    return dot(xh, high) + (dot(xl, high) + dot(xh, low))


def col(a, k):
    return jnp.broadcast_to(a[:, k : k + 1], (8, LANES))


def splat(table, row):
    return table[pl.ds(row, 8, stride=0), :]


def far_first(i):
    return 4 + (i // 2) * (1 - 2 * (i % 2))


def lane_block(q):
    return pl.ds(q * LANES, LANES)


def spread(rows, left, right, table):
    n = left.shape[1]
    picked = left * (iota((rows, n), 0) % n == iota((rows, n), 1)).astype(F32)
    table[...] = exact(picked, jnp.ones((n, LANES), F32))


def kernel(
    vec,
    prev,
    pot,
    cor,
    sec,
    beta_hbm,
    rot_hbm,
    coupling_hbm,
    one_hbm,
    two_hbm,
    three_hbm,
    four_hbm,
    five_hbm,
    six_hbm,
    deriv_hbm,
    wout,
    pack,
    v,
    pv,
    po,
    cf,
    sf,
    w,
    zin,
    zout,
    zret,
    rin,
    rout,
    rret,
    yb,
    via,
    beta,
    rot,
    coupling,
    kin_one,
    kin_two,
    kin_three,
    kin_four,
    kin_five,
    kin_six,
    deriv,
    tab1,
    tab2,
    tabb,
    tab3,
    rows4,
    tkh,
    tkl,
    twh,
    twl,
    acc,
    total,
    arb,
    loc,
    zfs,
    zfr,
    zrs,
    zrr,
    rfs,
    rfr,
    rrs,
    rrr,
    yfs,
    yfr,
    yrs,
    yrr,
    vr,
    vs,
    ars,
    arr,
    obs,
):
    ka = lax.axis_index("ka")
    z = lax.axis_index("mode")
    r = lax.axis_index("row")
    x_hi = ka // 8
    y = ka % 8
    nv, n1, n2 = v.shape[0], v.shape[1], v.shape[2]
    u = x_hi * 4 + r
    nblocks = 16

    def local_copy(i, src, dst):
        return pltpu.make_async_copy(src, dst, loc.at[i])

    locals_ = [
        local_copy(0, vec.at[0], v),
        local_copy(1, prev.at[0], pv),
        local_copy(2, pot, po),
        local_copy(3, cor, cf),
        local_copy(4, sec, sf),
        local_copy(5, vec.at[0, z], zin.at[z]),
        local_copy(6, vec.at[0, pl.ds(2 * r, 2)], rin.at[r]),
    ]
    small = [
        (beta_hbm, beta),
        (rot_hbm, rot),
        (coupling_hbm, coupling),
        (one_hbm, kin_one),
        (two_hbm, kin_two),
        (three_hbm, kin_three),
        (four_hbm, kin_four),
        (five_hbm, kin_five),
        (six_hbm, kin_six),
        (deriv_hbm, deriv),
    ]
    small = [local_copy(7 + i, *pair) for i, pair in enumerate(small)]

    def z_peer(o):
        return {"mode": (z + o) % 8}

    def y_peer(o):
        return {"ka": x_hi * 8 + (y + o) % 8}

    def x_peer(o):
        t = (u + o) % 8
        return {"ka": (t // 4) * 8 + y, "row": t % 4}

    def z_forward(c, o):
        t = (z + o) % 8
        return pltpu.make_async_remote_copy(
            vec.at[0, t, :, c],
            zin.at[z, :, c],
            zfs.at[c, o],
            zfr.at[c, o],
            device_id=z_peer(o),
        )

    def z_back(c, o):
        t = (z + o) % 8
        return pltpu.make_async_remote_copy(
            zout.at[t, :, c],
            zret.at[z, :, c],
            zrs.at[c, o],
            zrr.at[c, o],
            device_id=z_peer(o),
        )

    def r_forward(o):
        t = (r + o) % 4
        return pltpu.make_async_remote_copy(
            vec.at[0, pl.ds(2 * t, 2)],
            rin.at[r],
            rfs.at[o],
            rfr.at[o],
            device_id={"row": t},
        )

    def r_back(o):
        t = (r + o) % 4
        return pltpu.make_async_remote_copy(
            rout.at[t],
            rret.at[pl.ds(2 * r, 2)],
            rrs.at[o],
            rrr.at[o],
            device_id={"row": t},
        )

    def y_own(c, d):
        return pltpu.make_async_remote_copy(
            vec.at[0, :, :, c],
            yb.at[d, :, :, c],
            yfs.at[d, c],
            yfr.at[d, c],
            device_id={"ka": ka + 1 - 2 * d},
        )

    def y_relay(c, d):
        return pltpu.make_async_remote_copy(
            yb.at[d, :, :, c],
            yb.at[d + 2, :, :, c],
            yrs.at[d, c],
            yrr.at[d, c],
            device_id={"ka": ka + 1 - 2 * d},
        )

    def to_via(k, c, d):
        src = vec.at[0, :, :, c] if k == 0 else yb.at[d, :, :, c]
        return pltpu.make_async_remote_copy(
            src,
            via.at[k * n2 + c],
            (yfs, yrs)[k].at[d, c],
            vr.at[k * n2 + c],
            device_id={"ka": 15 - 15 * d},
        )

    def from_via(k, c, d):
        return pltpu.make_async_remote_copy(
            via.at[k * n2 + c],
            yb.at[d + 2 * k, :, :, c],
            vs.at[k * n2 + c],
            (yfr, yrr)[k].at[d, c],
            device_id={"ka": 8 - d},
        )

    at_edge = (ka == 7, ka == 8)
    is_via = (ka == 15, ka == 0)

    def send_on(k, c, d, cond):
        detour = jnp.logical_and(at_edge[d], c < VIA)

        @pl.when(jnp.logical_and(cond, detour))
        def _():
            to_via(k, c, d).start()

        @pl.when(jnp.logical_and(cond, jnp.logical_not(detour)))
        def _():
            (y_own, y_relay)[k](c, d).start()

    def pass_on(k, c):
        for d in range(2):

            @pl.when(is_via[d])
            def _():
                to_via(k, c, d).wait_recv()
                from_via(k, c, d).start()

    can_send = (ka < nblocks - 1, ka > 0)
    has_one = (ka > 0, ka < nblocks - 1)
    has_two = (ka > 1, ka < nblocks - 2)

    barrier = pltpu.get_barrier_semaphore()
    edge = jnp.logical_or(ka == 7, ka == 8)

    for i in range(1, 8):
        for peer in (z_peer, y_peer, x_peer):
            pl.semaphore_signal(barrier, inc=1, device_id=peer(far_first(i)))

    @pl.when(edge)
    def _():
        pl.semaphore_signal(barrier, inc=1, device_id={"ka": 15 - ka})

    pl.semaphore_wait(barrier, 21 + edge.astype(jnp.int32))

    def start_chunk(c):
        @pl.loop(1, 8)
        def _(o):
            z_forward(c, far_first(o)).start()

        for d in range(2):

            send_on(0, c, d, can_send[d])

    for o in range(1, 4):
        r_forward(o).start()
    start_chunk(0)
    for copy in small + locals_:
        copy.start()
    for c in range(1, n2):
        start_chunk(c)

    for d in range(2):

        @pl.when(jnp.logical_not(has_one[d]))
        def _():
            yb[d] = jnp.zeros(yb.shape[1:], F32)

        @pl.when(jnp.logical_not(has_two[d]))
        def _():
            yb[d + 2] = jnp.zeros(yb.shape[1:], F32)

    for copy in small:
        copy.wait()

    def table_of(matrix, table):
        n = matrix.shape[0]
        pick = hot((n * n, n), lambda q: q // n)
        both = 0.5 * (exact(pick, matrix[...]) + exact_nt(pick, matrix[...]))
        spread(n * n, both, None, table)

    table_of(kin_one, tab1)
    table_of(kin_two, tab2)
    spread(64, exact(hot((64, 8), lambda q: q // 8), beta[...]), None, tabb)
    eye8 = hot((8, 8), lambda q: q)
    sym3 = 0.5 * (kin_three[...] + exact_nt(eye8, kin_three[...]))
    for s in range(8):
        mask = (iota((8, 8), 0) + (8 - s)) % 8 == iota((8, 8), 1)
        tab3[s] = exact(jnp.where(mask, sym3, 0.0), jnp.ones((8, LANES), F32))

    def expand(pick, matrix, pick_t):
        both = 0.5 * (exact(pick, matrix[...]) + exact_nt(pick, matrix[...]))
        return exact_nt(both, pick_t)

    rows4[...] = expand(eye8, kin_four, hot((512, 8), lambda q: q // 64))
    e5 = expand(hot((64, 8), lambda q: q // 8), kin_five, hot((512, 8), lambda q: (q // 8) % 8))
    e6 = expand(hot((64, 8), lambda q: q % 8), kin_six, hot((512, 8), lambda q: q % 8))
    qi = iota((64, 512), 0)
    pi = iota((64, 512), 1)
    m56 = jnp.where(pi % 8 == qi % 8, e5, 0.0) + jnp.where((pi // 8) % 8 == qi // 8, e6, 0.0)
    diag64 = pi % 64 == qi
    for k in range(8):
        block = jnp.where(diag64, rows4[k : k + 1, :], 0.0) + jnp.where(pi // 64 == k, m56, 0.0)
        high, low = halves(block)
        tkh[k * 64 : (k + 1) * 64, :] = high
        tkl[k * 64 : (k + 1) * 64, :] = low
    pick6 = hot((256, 8), lambda q: q % 8)
    turned = 0.5 * (exact_nt(pick6, deriv[...]) - exact(pick6, deriv[...]))
    full = jnp.where(iota((256, 256), 0) // 8 == iota((256, 256), 1) // 8, exact_nt(turned, pick6), 0.0)
    high, low = halves(full)
    twh[...] = high
    twl[...] = low
    acc[...] = jnp.zeros(acc.shape, F32)

    level = (ka - nblocks // 2).astype(F32)
    shift = rot[ka] * level * level
    near = coupling[0, ka]
    near_low = coupling[0, jnp.maximum(ka - 1, 0)]
    far = coupling[1, ka]
    far_low = coupling[1, jnp.maximum(ka - 2, 0)]

    def mix16(load, store, table):
        xs = [[load(b, q) for q in range(2)] for b in range(16)]
        for a in range(16):
            total = None
            for b in range(16):
                k = splat(table, a * 16 + b)
                terms = [k * xs[b][q] for q in range(2)]
                total = terms if total is None else [t + s for t, s in zip(total, terms)]
            for q in range(2):
                store(a, q, total[q])

    def first_mode(c):
        @pl.loop(0, 2)
        def _(h):
            def at(q):
                return pl.ds(pl.multiple_of(h * 256 + q * LANES, LANES), LANES)

            def load(b, q):
                return zin[b // 2, b % 2, c, :, at(q)]

            def store(a, q, val):
                zout[a // 2, a % 2, c, :, at(q)] = val

            mix16(load, store, tab1)

        zret[z, :, c] = zout[z, :, c]

    def second_mode():
        @pl.loop(0, 8)
        def _(k):
            n, m, h = k // 4, (k // 2) % 2, k % 2

            def at(q):
                return pl.ds(pl.multiple_of(h * 256 + q * LANES, LANES), LANES)

            def load(b, q):
                return rin[b // 4, n, m, b % 4, :, at(q)]

            def store(a, q, val):
                rout[a // 4, n, m, a % 4, :, at(q)] = val

            mix16(load, store, tab2)

        rret[pl.ds(2 * r, 2)] = rout[r]

    def gather_products(c, left, right, spots, triangle):
        for g in range(4):
            pairs = [(j, i) for i in (2 * g, 2 * g + 1) for j in range(8) if j <= i or not triangle]
            sums = {}
            for m in range(n1):
                for q in range(4):
                    ls = [left[j, m, c, :, lane_block(q)] for j in range(8)]
                    rs = [right[i, m, c, :, lane_block(q)] for i in (2 * g, 2 * g + 1)]
                    for j, i in pairs:
                        term = ls[j] * rs[i - 2 * g]
                        sums[j, i] = term if (j, i) not in sums else sums[j, i] + term
            for j, i in pairs:
                for spot in spots(j, i):
                    acc[spot * 8 : spot * 8 + 8, :] += sums[j, i]

    def local_terms(c):
        x = v[:, :, c].reshape(nv * n1 * 8, 512)
        w[:, :, c] = three_pass(x, tkh[...], tkl[...]).reshape(nv, n1, 8, 512)

        @pl.loop(0, 4)
        def _(k):
            m, h = k // 2, k % 2
            for q in range(2):
                at = pl.ds(pl.multiple_of(h * 256 + q * LANES, LANES), LANES)
                old = [pv[j, m, c, :, at] for j in range(8)]
                diag = po[m, c, :, at] + shift
                for i in range(8):
                    xi = v[i, m, c, :, at]
                    total = w[i, m, c, :, at] + (diag + tab3[0]) * xi
                    for s in range(1, 8):
                        total = total + tab3[s] * pltpu.roll(xi, s, axis=0)
                    taken = splat(tabb, i * 8) * old[0]
                    for j in range(1, 8):
                        taken = taken + splat(tabb, i * 8 + j) * old[j]
                    w[i, m, c, :, at] = total - taken

        gather_products(c, v, v, lambda j, i: {(24 + j) * 8 + i, (24 + i) * 8 + j}, True)

    def turn(x):
        flat = x.reshape(nv * n1 * 8, 512)
        parts = [three_pass(flat[:, h * 256 : h * 256 + 256], twh[...], twl[...]) for h in range(2)]
        return jnp.concatenate(parts, axis=1).reshape(x.shape)

    def near_terms(c):
        fn = cf[:, c][None]
        above = turn(yb[1, :, :, c])
        w[:, :, c] += (near * fn) * above
        below = turn(fn * yb[0, :, :, c])
        w[:, :, c] -= near_low * below

    def wait_recv_when(cond, copy):
        @pl.when(cond)
        def _():
            copy.wait_recv()

    for copy in locals_:
        copy.wait()

    @pl.loop(0, n2)
    def _(c):
        @pl.loop(1, 8)
        def _(o):
            z_forward(c, o).wait_recv()

        first_mode(c)

        @pl.loop(1, 8)
        def _(o):
            z_back(c, far_first(o)).start()

        for d in range(2):
            wait_recv_when(has_one[d], y_own(c, d))

            send_on(1, c, d, jnp.logical_and(has_one[d], can_send[d]))

        @pl.when(c < VIA)
        def _():
            pass_on(0, c)

        @pl.when(c == 1)
        def _():
            for o in range(1, 4):
                r_forward(o).wait_recv()
            second_mode()
            for o in range(1, 4):
                r_back(o).start()

        local_terms(c)
        near_terms(c)

    lane = iota((8, LANES), 1)
    row = iota((8, LANES), 0)

    def sum_into(count, shift, at):
        rows = count * 8
        part = acc[pl.ds(at * 64, rows, stride=8), :]
        for s in range(1, 8):
            part = part + acc[pl.ds(at * 64 + s, rows, stride=8), :]
        sums = jnp.sum(part, axis=1, keepdims=True)
        for a in range(2):
            packed = total[a]
            for l in range(count):
                q = l + shift
                if q // 16 == a:
                    here = lane == row + (q % 16) * 8
                    packed = jnp.where(here, sums[l * 8 : l * 8 + 8], packed)
            total[a] = packed

    total[...] = jnp.zeros((2, 8, LANES), F32)
    sum_into(8, 0, 24)

    def w_copy(c):
        return pltpu.make_async_copy(w.at[:, :, c], wout.at[:, :, c], obs.at[c])

    for c in range(VIA):
        pass_on(1, c)

    @pl.loop(0, n2)
    def _(c):
        @pl.loop(1, 8)
        def _(o):
            z_forward(c, o).wait_send()

        for d in range(2):

            @pl.when(can_send[d])
            def _():
                y_own(c, d).wait_send()

    for o in range(1, 4):
        r_forward(o).wait_send()

    def wait_sends_back():
        @pl.loop(0, n2)
        def _(c):
            w_copy(c).wait()

            @pl.loop(1, 8)
            def _(o):
                z_back(c, o).wait_send()

            for d in range(2):

                @pl.when(jnp.logical_and(has_one[d], can_send[d]))
                def _():
                    y_relay(c, d).wait_send()

        for k in range(2):
            for c in range(VIA):
                for d in range(2):

                    @pl.when(is_via[d])
                    def _():
                        from_via(k, c, d).wait_send()

        for o in range(1, 4):
            r_back(o).wait_send()

    for o in range(1, 4):
        r_back(o).wait_recv()

    @pl.loop(0, n2)
    def _(c):
        @pl.loop(1, 8)
        def _(o):
            z_back(c, o).wait_recv()

        for d in range(2):
            wait_recv_when(has_two[d], y_relay(c, d))

        @pl.loop(0, nv)
        def _(n):
            for m in range(n1):
                skip = sf[m, c] * (far * yb[3, n, m, c] + far_low * yb[2, n, m, c])
                w[n, m, c] = (w[n, m, c] + rret[n, m, c]) + (zret[n, m, c] + skip)

        w_copy(c).start()
        gather_products(c, v, w, lambda j, i: (j * 8 + i, (16 + i) * 8 + j), False)
        gather_products(c, w, w, lambda j, i: {(8 + j) * 8 + i, (8 + i) * 8 + j}, True)

    sum_into(24, 8, 0)
    msg = jnp.concatenate([jnp.sum(total[a], axis=0, keepdims=True) for a in range(2)], axis=0)

    groups = ((u, x_peer), (z, z_peer), (y, y_peer))

    def ar_copy(g, o):
        me, peer = groups[g]
        return pltpu.make_async_remote_copy(
            arb.at[g, me], arb.at[g, me], ars.at[g, o], arr.at[g, o], device_id=peer(o)
        )

    for g in range(3):
        arb[g, groups[g][0]] = msg
        for i in range(1, 8):
            ar_copy(g, far_first(i)).start()
        if g == 0:
            wait_sends_back()
        else:
            for i in range(1, 8):
                ar_copy(g - 1, i).wait_send()
        for i in range(1, 8):
            ar_copy(g, i).wait_recv()
        msg = arb[g, 0]
        for t in range(1, 8):
            msg = msg + arb[g, t]

    msg = msg * (1.0 / float(16 * 8 * 4 * 32768))

    def mm(a, b):
        total = col(a, 0) * b[0:1, :]
        for k in range(1, 8):
            total = total + col(a, k) * b[k : k + 1, :]
        return total

    own = [jnp.where(lane % 8 == row, msg[a : a + 1, :], 0.0) for a in range(2)]
    whole = exact(jnp.concatenate(own, axis=0), hot((LANES, LANES), lambda q: q // 8))
    overlap = whole[0:8]
    first_t = pltpu.roll(overlap, LANES - 8, axis=1)
    square = whole[8:16]
    first = pltpu.roll(square, LANES - 8, axis=1)
    both_t = 2.0 * first_t - mm(first_t, overlap)
    both = 2.0 * first - mm(overlap, first)
    gram = square - mm(both_t, first) - mm(first_t, both) + mm(mm(both_t, overlap), both)
    work = jnp.where(lane < 8, gram, 0.0)
    work = jnp.where(lane == row + 8, 1.0, work)
    work = jnp.where((lane >= 16) & (lane < 24), pltpu.roll(both_t, 16, axis=1), work)
    factor = jnp.zeros((8, LANES), F32)
    for k in range(8):
        prow = jnp.broadcast_to(work[k : k + 1, :], (8, LANES))
        pivot = col(prow, k)
        column = col(work, k)
        root = lax.rsqrt(pivot)
        factor = jnp.where((lane == k) & (row >= k), column * root, factor)
        below = work - (column / pivot) * prow
        work = jnp.where(row > k, below, jnp.where(row == k, work * root, work))
    pack[0] = work
    pack[1] = both
    pack[2] = factor

    for i in range(1, 8):
        ar_copy(2, i).wait_send()


def finish(vec, wfin, pack_hbm, out, alpha_hbm, lower_hbm, v, w, ob, pack, coef, small, sem):
    n2 = v.shape[2]

    def loads(c):
        return (
            pltpu.make_async_copy(vec.at[0, :, :, c], v.at[:, :, c], sem.at[0, c]),
            pltpu.make_async_copy(wfin.at[:, :, c], w.at[:, :, c], sem.at[1, c]),
        )

    first = pltpu.make_async_copy(pack_hbm, pack, sem.at[3, 0])
    first.start()
    for c in range(n2):
        for copy in loads(c):
            copy.start()
    first.wait()
    small[0] = pack[1, :, 0:8]
    small[1] = pack[2, :, 0:8]
    tiny = [
        pltpu.make_async_copy(small.at[0], alpha_hbm, sem.at[3, 1]),
        pltpu.make_async_copy(small.at[1], lower_hbm, sem.at[3, 2]),
    ]
    for copy in tiny:
        copy.start()
    work = pack[0]
    for j in range(8):
        coef[j * 8 : j * 8 + 8, :] = col(work, 8 + j)
        coef[64 + j * 8 : 72 + j * 8, :] = -col(work, 16 + j)

    def out_copy(c):
        return pltpu.make_async_copy(ob.at[:, :, c], out.at[0, :, :, c], sem.at[2, c])

    @pl.loop(0, n2)
    def _(c):
        for copy in loads(c):
            copy.wait()

        @pl.loop(0, 4)
        def _(k):
            m, h = k // 2, k % 2
            at = [pl.ds(pl.multiple_of(h * 256 + q * LANES, LANES), LANES) for q in range(2)]
            vs = [[v[j, m, c, :, at[q]] for q in range(2)] for j in range(8)]
            ws = [[w[j, m, c, :, at[q]] for q in range(2)] for j in range(8)]
            for i in range(8):
                total = None
                for base, xs, count in ((64, vs, 8), (0, ws, i + 1)):
                    for j in range(count):
                        factor = splat(coef, base + j * 8 + i)
                        terms = [factor * xs[j][q] for q in range(2)]
                        total = terms if total is None else [t + s for t, s in zip(total, terms)]
                for q in range(2):
                    ob[i, m, c, :, at[q]] = total[q]

        out_copy(c).start()

    @pl.loop(0, n2)
    def _(c):
        out_copy(c).wait()

    for copy in tiny:
        copy.wait()


def shards(*args):
    (vectors, previous, beta, potential, coriolis_fn, second_fn, rot_const, coupling, *mats) = args
    block = vectors.shape[1:]
    fn = potential.shape
    any_spec = pl.BlockSpec(memory_space=pltpu.HBM)
    vmem = pl.BlockSpec(memory_space=pltpu.VMEM)
    nv, n1, n2, n3, nr = block
    dma = pltpu.SemaphoreType.DMA
    scratch = [
        pltpu.VMEM(block, F32),
        pltpu.VMEM(block, F32),
        pltpu.VMEM(fn, F32),
        pltpu.VMEM(fn, F32),
        pltpu.VMEM(fn, F32),
        pltpu.VMEM(block, F32),
        pltpu.VMEM(block, F32),
        pltpu.VMEM(block, F32),
        pltpu.VMEM(block, F32),
        pltpu.VMEM((4, 2) + block[1:], F32),
        pltpu.VMEM((4, 2) + block[1:], F32),
        pltpu.VMEM(block, F32),
        pltpu.VMEM((4,) + block, F32),
        pltpu.VMEM((2 * n2, nv, n1, n3, nr), F32),
        pltpu.VMEM((8, 8), F32),
        pltpu.SMEM((16,), F32),
        pltpu.SMEM((2, 16), F32),
        pltpu.VMEM((16, 16), F32),
        pltpu.VMEM((16, 16), F32),
        *[pltpu.VMEM((8, 8), F32)] * 5,
        pltpu.VMEM((256, LANES), F32),
        pltpu.VMEM((256, LANES), F32),
        pltpu.VMEM((64, LANES), F32),
        pltpu.VMEM((8, 8, LANES), F32),
        pltpu.VMEM((8, nr), F32),
        pltpu.VMEM((nr, nr), BF16),
        pltpu.VMEM((nr, nr), BF16),
        pltpu.VMEM((256, 256), BF16),
        pltpu.VMEM((256, 256), BF16),
        pltpu.VMEM((256 * 8, LANES), F32),
        pltpu.VMEM((2, 8, LANES), F32),
        pltpu.VMEM((3, 8, 2, LANES), F32),
        dma((17,)),
        dma((n2, 8)),
        dma((n2, 8)),
        dma((n2, 8)),
        dma((n2, 8)),
        dma((4,)),
        dma((4,)),
        dma((4,)),
        dma((4,)),
        dma((2, n2)),
        dma((2, n2)),
        dma((2, n2)),
        dma((2, n2)),
        dma((2 * n2,)),
        dma((2 * n2,)),
        dma((3, 8)),
        dma((3, 8)),
        dma((n2,)),
    ]
    wfin, pack = pl.pallas_call(
        kernel,
        out_shape=(
            jax.ShapeDtypeStruct(block, F32),
            jax.ShapeDtypeStruct((3, nv, LANES), F32),
        ),
        in_specs=[any_spec] * 15,
        out_specs=(any_spec, vmem),
        scratch_shapes=scratch,
        compiler_params=pltpu.CompilerParams(
            collective_id=0, has_side_effects=True, vmem_limit_bytes=67043328
        ),
        name="lanczos",
    )(vectors, previous, potential, coriolis_fn, second_fn, beta, rot_const, coupling, *mats)
    return pl.pallas_call(
        finish,
        out_shape=(
            jax.ShapeDtypeStruct(vectors.shape, F32),
            jax.ShapeDtypeStruct((nv, nv), F32),
            jax.ShapeDtypeStruct((nv, nv), F32),
        ),
        in_specs=[any_spec] * 3,
        out_specs=(any_spec,) * 3,
        scratch_shapes=[
            pltpu.VMEM(block, F32),
            pltpu.VMEM(block, F32),
            pltpu.VMEM(block, F32),
            pltpu.VMEM((3, nv, LANES), F32),
            pltpu.VMEM((128, LANES), F32),
            pltpu.VMEM((2, nv, nv), F32),
            dma((4, n2)),
        ],
        compiler_params=pltpu.CompilerParams(vmem_limit_bytes=67043328),
        name="basis",
    )(vectors, wfin, pack)


def solution(mesh):
    split = P("ka", None, "mode", "row", None, None)
    fn = P("mode", "row", None, None)
    return jax.shard_map(
        shards,
        mesh=mesh,
        in_specs=(split, split, P(), fn, fn, fn) + (P(),) * 9,
        out_specs=(split, P(), P()),
        check_vma=False,
    )
```

```python
import jax
import jax.numpy as jnp
from jax import lax
from jax.experimental import pallas as pl
from jax.experimental.pallas import tpu as pltpu
from jax.sharding import PartitionSpec as P

F32 = jnp.float32
BF16 = jnp.bfloat16
HI = lax.Precision.HIGHEST
LANES = 128
VIA = 2
NT = (((1,), (1,)), ((), ()))


def exact(a, b):
    return jnp.dot(a, b, precision=HI, preferred_element_type=F32)


def exact_nt(a, b):
    return lax.dot_general(a, b, NT, precision=HI, preferred_element_type=F32)


def iota(shape, axis):
    return lax.broadcasted_iota(jnp.int32, shape, axis)


def hot(shape, of):
    return (of(iota(shape, 0)) == iota(shape, 1)).astype(F32)


def halves(x):
    high = x.astype(BF16)
    return high, (x - high.astype(F32)).astype(BF16)


def three_pass(x, high, low):
    xh, xl = halves(x)

    def dot(a, b):
        return jnp.dot(a, b, preferred_element_type=F32)

    return dot(xh, high) + (dot(xl, high) + dot(xh, low))


def col(a, k):
    return jnp.broadcast_to(a[:, k : k + 1], (8, LANES))


def splat(table, row):
    return table[pl.ds(row, 8, stride=0), :]


def far_first(i):
    return 4 + (i // 2) * (1 - 2 * (i % 2))


def lane_block(q):
    return pl.ds(q * LANES, LANES)


def spread(rows, left, right, table):
    n = left.shape[1]
    picked = left * (iota((rows, n), 0) % n == iota((rows, n), 1)).astype(F32)
    table[...] = exact(picked, jnp.ones((n, LANES), F32))


def kernel(
    vec,
    prev,
    pot,
    cor,
    sec,
    beta_hbm,
    rot_hbm,
    coupling_hbm,
    one_hbm,
    two_hbm,
    three_hbm,
    four_hbm,
    five_hbm,
    six_hbm,
    deriv_hbm,
    wout,
    pack,
    v,
    pv,
    po,
    cf,
    sf,
    w,
    zin,
    zout,
    zret,
    rin,
    rout,
    rret,
    yb,
    via,
    beta,
    rot,
    coupling,
    kin_one,
    kin_two,
    kin_three,
    kin_four,
    kin_five,
    kin_six,
    deriv,
    tab1,
    tab2,
    tabb,
    tab3,
    rows4,
    tkh,
    tkl,
    twh,
    twl,
    acc,
    total,
    arb,
    loc,
    zfs,
    zfr,
    zrs,
    zrr,
    rfs,
    rfr,
    rrs,
    rrr,
    yfs,
    yfr,
    yrs,
    yrr,
    vr,
    vs,
    ars,
    arr,
    obs,
    zc,
    yc,
):
    ka = lax.axis_index("ka")
    z = lax.axis_index("mode")
    r = lax.axis_index("row")
    x_hi = ka // 8
    y = ka % 8
    nv, n1, n2 = v.shape[0], v.shape[1], v.shape[2]
    u = x_hi * 4 + r
    nblocks = 16

    def local_copy(i, src, dst):
        return pltpu.make_async_copy(src, dst, loc.at[i])

    locals_ = [
        local_copy(0, vec.at[0], v),
        local_copy(1, prev.at[0], pv),
        local_copy(2, pot, po),
        local_copy(3, cor, cf),
        local_copy(4, sec, sf),
        local_copy(5, vec.at[0, z], zin.at[z]),
        local_copy(6, vec.at[0, pl.ds(2 * r, 2)], rin.at[r]),
    ]
    small = [
        (beta_hbm, beta),
        (rot_hbm, rot),
        (coupling_hbm, coupling),
        (one_hbm, kin_one),
        (two_hbm, kin_two),
        (three_hbm, kin_three),
        (four_hbm, kin_four),
        (five_hbm, kin_five),
        (six_hbm, kin_six),
        (deriv_hbm, deriv),
    ]
    small = [local_copy(7 + i, *pair) for i, pair in enumerate(small)]

    def z_peer(o):
        return {"mode": (z + o) % 8}

    def y_peer(o):
        return {"ka": x_hi * 8 + (y + o) % 8}

    def x_peer(o):
        t = (u + o) % 8
        return {"ka": (t // 4) * 8 + y, "row": t % 4}

    def z_forward(c, o):
        t = (z + o) % 8
        return pltpu.make_async_remote_copy(
            vec.at[0, t, :, c],
            zin.at[z, :, c],
            zfs.at[c, o],
            zfr.at[c, o],
            device_id=z_peer(o),
        )

    def z_back(c, o):
        t = (z + o) % 8
        return pltpu.make_async_remote_copy(
            zout.at[t, :, c],
            zret.at[z, :, c],
            zrs.at[c, o],
            zrr.at[c, o],
            device_id=z_peer(o),
        )

    def r_forward(o):
        t = (r + o) % 4
        return pltpu.make_async_remote_copy(
            vec.at[0, pl.ds(2 * t, 2)],
            rin.at[r],
            rfs.at[o],
            rfr.at[o],
            device_id={"row": t},
        )

    def r_back(o):
        t = (r + o) % 4
        return pltpu.make_async_remote_copy(
            rout.at[t],
            rret.at[pl.ds(2 * r, 2)],
            rrs.at[o],
            rrr.at[o],
            device_id={"row": t},
        )

    def y_own(c, d):
        return pltpu.make_async_remote_copy(
            vec.at[0, :, :, c],
            yb.at[d, :, :, c],
            yfs.at[d, c],
            yfr.at[d, c],
            device_id={"ka": ka + 1 - 2 * d},
        )

    def y_relay(c, d):
        return pltpu.make_async_remote_copy(
            yb.at[d, :, :, c],
            yb.at[d + 2, :, :, c],
            yrs.at[d, c],
            yrr.at[d, c],
            device_id={"ka": ka + 1 - 2 * d},
        )

    def to_via(k, c, d):
        src = vec.at[0, :, :, c] if k == 0 else yb.at[d, :, :, c]
        return pltpu.make_async_remote_copy(
            src,
            via.at[k * n2 + c],
            (yfs, yrs)[k].at[d, c],
            vr.at[k * n2 + c],
            device_id={"ka": 15 - 15 * d},
        )

    def from_via(k, c, d):
        return pltpu.make_async_remote_copy(
            via.at[k * n2 + c],
            yb.at[d + 2 * k, :, :, c],
            vs.at[k * n2 + c],
            (yfr, yrr)[k].at[d, c],
            device_id={"ka": 8 - d},
        )

    at_edge = (ka == 7, ka == 8)
    is_via = (ka == 15, ka == 0)

    def send_on(k, c, d, cond):
        detour = jnp.logical_and(at_edge[d], c < VIA)

        @pl.when(jnp.logical_and(cond, detour))
        def _():
            to_via(k, c, d).start()

        @pl.when(jnp.logical_and(cond, jnp.logical_not(detour)))
        def _():
            (y_own, y_relay)[k](c, d).start()

    def pass_on(k, c):
        for d in range(2):

            @pl.when(is_via[d])
            def _():
                to_via(k, c, d).wait_recv()
                from_via(k, c, d).start()

    can_send = (ka < nblocks - 1, ka > 0)
    has_one = (ka > 0, ka < nblocks - 1)
    has_two = (ka > 1, ka < nblocks - 2)

    barrier = pltpu.get_barrier_semaphore()
    edge = jnp.logical_or(ka == 7, ka == 8)

    for o in range(1, 8):
        pl.semaphore_signal(barrier, inc=1, device_id=x_peer(o))
    for o in (1, 7):
        pl.semaphore_signal(barrier, inc=1, device_id=y_peer(o))
        pl.semaphore_signal(barrier, inc=1, device_id=z_peer(o))

    @pl.when(edge)
    def _():
        pl.semaphore_signal(barrier, inc=1, device_id={"ka": 15 - ka})

    pl.semaphore_wait(barrier, 11 + edge.astype(jnp.int32))

    def farther(sem, peer):
        pl.semaphore_signal(sem.at[0], inc=1, device_id=peer(1))
        pl.semaphore_signal(sem.at[1], inc=1, device_id=peer(7))
        pl.semaphore_wait(sem.at[0], 1)
        pl.semaphore_wait(sem.at[1], 1)

    def z_sends(offsets):
        for c in range(n2):
            for o in offsets:
                z_forward(c, o).start()

    for o in range(1, 4):
        r_forward(o).start()
    z_sends((1, 7))
    for c in range(n2):
        for d in range(2):
            send_on(0, c, d, can_send[d])
    for offsets in ((2, 6), (3, 5), (4,)):
        farther(zc, z_peer)
        z_sends(offsets)
    for copy in small + locals_:
        copy.start()
    for _ in range(3):
        farther(yc, y_peer)

    for d in range(2):

        @pl.when(jnp.logical_not(has_one[d]))
        def _():
            yb[d] = jnp.zeros(yb.shape[1:], F32)

        @pl.when(jnp.logical_not(has_two[d]))
        def _():
            yb[d + 2] = jnp.zeros(yb.shape[1:], F32)

    for copy in small:
        copy.wait()

    def table_of(matrix, table):
        n = matrix.shape[0]
        pick = hot((n * n, n), lambda q: q // n)
        both = 0.5 * (exact(pick, matrix[...]) + exact_nt(pick, matrix[...]))
        spread(n * n, both, None, table)

    table_of(kin_one, tab1)
    table_of(kin_two, tab2)
    spread(64, exact(hot((64, 8), lambda q: q // 8), beta[...]), None, tabb)
    eye8 = hot((8, 8), lambda q: q)
    sym3 = 0.5 * (kin_three[...] + exact_nt(eye8, kin_three[...]))
    for s in range(8):
        mask = (iota((8, 8), 0) + (8 - s)) % 8 == iota((8, 8), 1)
        tab3[s] = exact(jnp.where(mask, sym3, 0.0), jnp.ones((8, LANES), F32))

    def expand(pick, matrix, pick_t):
        both = 0.5 * (exact(pick, matrix[...]) + exact_nt(pick, matrix[...]))
        return exact_nt(both, pick_t)

    rows4[...] = expand(eye8, kin_four, hot((512, 8), lambda q: q // 64))
    e5 = expand(hot((64, 8), lambda q: q // 8), kin_five, hot((512, 8), lambda q: (q // 8) % 8))
    e6 = expand(hot((64, 8), lambda q: q % 8), kin_six, hot((512, 8), lambda q: q % 8))
    qi = iota((64, 512), 0)
    pi = iota((64, 512), 1)
    m56 = jnp.where(pi % 8 == qi % 8, e5, 0.0) + jnp.where((pi // 8) % 8 == qi // 8, e6, 0.0)
    diag64 = pi % 64 == qi
    for k in range(8):
        block = jnp.where(diag64, rows4[k : k + 1, :], 0.0) + jnp.where(pi // 64 == k, m56, 0.0)
        high, low = halves(block)
        tkh[k * 64 : (k + 1) * 64, :] = high
        tkl[k * 64 : (k + 1) * 64, :] = low
    pick6 = hot((256, 8), lambda q: q % 8)
    turned = 0.5 * (exact_nt(pick6, deriv[...]) - exact(pick6, deriv[...]))
    full = jnp.where(iota((256, 256), 0) // 8 == iota((256, 256), 1) // 8, exact_nt(turned, pick6), 0.0)
    high, low = halves(full)
    twh[...] = high
    twl[...] = low
    acc[...] = jnp.zeros(acc.shape, F32)

    level = (ka - nblocks // 2).astype(F32)
    shift = rot[ka] * level * level
    near = coupling[0, ka]
    near_low = coupling[0, jnp.maximum(ka - 1, 0)]
    far = coupling[1, ka]
    far_low = coupling[1, jnp.maximum(ka - 2, 0)]

    def mix16(load, store, table):
        xs = [[load(b, q) for q in range(2)] for b in range(16)]
        for a in range(16):
            total = None
            for b in range(16):
                k = splat(table, a * 16 + b)
                terms = [k * xs[b][q] for q in range(2)]
                total = terms if total is None else [t + s for t, s in zip(total, terms)]
            for q in range(2):
                store(a, q, total[q])

    def first_mode(c):
        @pl.loop(0, 2)
        def _(h):
            def at(q):
                return pl.ds(pl.multiple_of(h * 256 + q * LANES, LANES), LANES)

            def load(b, q):
                return zin[b // 2, b % 2, c, :, at(q)]

            def store(a, q, val):
                zout[a // 2, a % 2, c, :, at(q)] = val

            mix16(load, store, tab1)

        zret[z, :, c] = zout[z, :, c]

    def second_mode():
        @pl.loop(0, 8)
        def _(k):
            n, m, h = k // 4, (k // 2) % 2, k % 2

            def at(q):
                return pl.ds(pl.multiple_of(h * 256 + q * LANES, LANES), LANES)

            def load(b, q):
                return rin[b // 4, n, m, b % 4, :, at(q)]

            def store(a, q, val):
                rout[a // 4, n, m, a % 4, :, at(q)] = val

            mix16(load, store, tab2)

        rret[pl.ds(2 * r, 2)] = rout[r]

    def gather_products(c, left, right, spots, triangle):
        for g in range(4):
            pairs = [(j, i) for i in (2 * g, 2 * g + 1) for j in range(8) if j <= i or not triangle]
            sums = {}
            for m in range(n1):
                for q in range(4):
                    ls = [left[j, m, c, :, lane_block(q)] for j in range(8)]
                    rs = [right[i, m, c, :, lane_block(q)] for i in (2 * g, 2 * g + 1)]
                    for j, i in pairs:
                        term = ls[j] * rs[i - 2 * g]
                        sums[j, i] = term if (j, i) not in sums else sums[j, i] + term
            for j, i in pairs:
                for spot in spots(j, i):
                    acc[spot * 8 : spot * 8 + 8, :] += sums[j, i]

    def local_terms(c):
        x = v[:, :, c].reshape(nv * n1 * 8, 512)
        w[:, :, c] = three_pass(x, tkh[...], tkl[...]).reshape(nv, n1, 8, 512)

        @pl.loop(0, 4)
        def _(k):
            m, h = k // 2, k % 2
            for q in range(2):
                at = pl.ds(pl.multiple_of(h * 256 + q * LANES, LANES), LANES)
                old = [pv[j, m, c, :, at] for j in range(8)]
                diag = po[m, c, :, at] + shift
                for i in range(8):
                    xi = v[i, m, c, :, at]
                    total = w[i, m, c, :, at] + (diag + tab3[0]) * xi
                    for s in range(1, 8):
                        total = total + tab3[s] * pltpu.roll(xi, s, axis=0)
                    taken = splat(tabb, i * 8) * old[0]
                    for j in range(1, 8):
                        taken = taken + splat(tabb, i * 8 + j) * old[j]
                    w[i, m, c, :, at] = total - taken

        gather_products(c, v, v, lambda j, i: {(24 + j) * 8 + i, (24 + i) * 8 + j}, True)

    def turn(x):
        flat = x.reshape(nv * n1 * 8, 512)
        parts = [three_pass(flat[:, h * 256 : h * 256 + 256], twh[...], twl[...]) for h in range(2)]
        return jnp.concatenate(parts, axis=1).reshape(x.shape)

    def near_terms(c):
        fn = cf[:, c][None]
        above = turn(yb[1, :, :, c])
        w[:, :, c] += (near * fn) * above
        below = turn(fn * yb[0, :, :, c])
        w[:, :, c] -= near_low * below

    def wait_recv_when(cond, copy):
        @pl.when(cond)
        def _():
            copy.wait_recv()

    for copy in locals_:
        copy.wait()

    @pl.loop(0, n2)
    def _(c):
        @pl.loop(1, 8)
        def _(o):
            z_forward(c, o).wait_recv()

        first_mode(c)

        @pl.loop(1, 8)
        def _(o):
            z_back(c, far_first(o)).start()

        for d in range(2):
            wait_recv_when(has_one[d], y_own(c, d))

            send_on(1, c, d, jnp.logical_and(has_one[d], can_send[d]))

        @pl.when(c < VIA)
        def _():
            pass_on(0, c)

        @pl.when(c == 1)
        def _():
            for o in range(1, 4):
                r_forward(o).wait_recv()
            second_mode()
            for o in range(1, 4):
                r_back(o).start()

        local_terms(c)
        near_terms(c)

    lane = iota((8, LANES), 1)
    row = iota((8, LANES), 0)

    def sum_into(count, shift, at):
        rows = count * 8
        part = acc[pl.ds(at * 64, rows, stride=8), :]
        for s in range(1, 8):
            part = part + acc[pl.ds(at * 64 + s, rows, stride=8), :]
        sums = jnp.sum(part, axis=1, keepdims=True)
        for a in range(2):
            packed = total[a]
            for l in range(count):
                q = l + shift
                if q // 16 == a:
                    here = lane == row + (q % 16) * 8
                    packed = jnp.where(here, sums[l * 8 : l * 8 + 8], packed)
            total[a] = packed

    total[...] = jnp.zeros((2, 8, LANES), F32)
    sum_into(8, 0, 24)

    def w_copy(c):
        return pltpu.make_async_copy(w.at[:, :, c], wout.at[:, :, c], obs.at[c])

    for c in range(VIA):
        pass_on(1, c)

    @pl.loop(0, n2)
    def _(c):
        @pl.loop(1, 8)
        def _(o):
            z_forward(c, o).wait_send()

        for d in range(2):

            @pl.when(can_send[d])
            def _():
                y_own(c, d).wait_send()

    for o in range(1, 4):
        r_forward(o).wait_send()

    def wait_sends_back():
        @pl.loop(0, n2)
        def _(c):
            w_copy(c).wait()

            @pl.loop(1, 8)
            def _(o):
                z_back(c, o).wait_send()

            for d in range(2):

                @pl.when(jnp.logical_and(has_one[d], can_send[d]))
                def _():
                    y_relay(c, d).wait_send()

        for k in range(2):
            for c in range(VIA):
                for d in range(2):

                    @pl.when(is_via[d])
                    def _():
                        from_via(k, c, d).wait_send()

        for o in range(1, 4):
            r_back(o).wait_send()

    for o in range(1, 4):
        r_back(o).wait_recv()

    @pl.loop(0, n2)
    def _(c):
        @pl.loop(1, 8)
        def _(o):
            z_back(c, o).wait_recv()

        for d in range(2):
            wait_recv_when(has_two[d], y_relay(c, d))

        @pl.loop(0, nv)
        def _(n):
            for m in range(n1):
                skip = sf[m, c] * (far * yb[3, n, m, c] + far_low * yb[2, n, m, c])
                w[n, m, c] = (w[n, m, c] + rret[n, m, c]) + (zret[n, m, c] + skip)

        w_copy(c).start()
        gather_products(c, v, w, lambda j, i: (j * 8 + i, (16 + i) * 8 + j), False)
        gather_products(c, w, w, lambda j, i: {(8 + j) * 8 + i, (8 + i) * 8 + j}, True)

    sum_into(24, 8, 0)
    msg = jnp.concatenate([jnp.sum(total[a], axis=0, keepdims=True) for a in range(2)], axis=0)

    groups = ((u, x_peer), (z, z_peer), (y, y_peer))

    def ar_copy(g, o):
        me, peer = groups[g]
        return pltpu.make_async_remote_copy(
            arb.at[g, me], arb.at[g, me], ars.at[g, o], arr.at[g, o], device_id=peer(o)
        )

    for g in range(3):
        arb[g, groups[g][0]] = msg
        for i in range(1, 8):
            ar_copy(g, far_first(i)).start()
        if g == 0:
            wait_sends_back()
        else:
            for i in range(1, 8):
                ar_copy(g - 1, i).wait_send()
        for i in range(1, 8):
            ar_copy(g, i).wait_recv()
        msg = arb[g, 0]
        for t in range(1, 8):
            msg = msg + arb[g, t]

    msg = msg * (1.0 / float(16 * 8 * 4 * 32768))

    def mm(a, b):
        total = col(a, 0) * b[0:1, :]
        for k in range(1, 8):
            total = total + col(a, k) * b[k : k + 1, :]
        return total

    own = [jnp.where(lane % 8 == row, msg[a : a + 1, :], 0.0) for a in range(2)]
    whole = exact(jnp.concatenate(own, axis=0), hot((LANES, LANES), lambda q: q // 8))
    overlap = whole[0:8]
    first_t = pltpu.roll(overlap, LANES - 8, axis=1)
    square = whole[8:16]
    first = pltpu.roll(square, LANES - 8, axis=1)
    both_t = 2.0 * first_t - mm(first_t, overlap)
    both = 2.0 * first - mm(overlap, first)
    gram = square - mm(both_t, first) - mm(first_t, both) + mm(mm(both_t, overlap), both)
    work = jnp.where(lane < 8, gram, 0.0)
    work = jnp.where(lane == row + 8, 1.0, work)
    work = jnp.where((lane >= 16) & (lane < 24), pltpu.roll(both_t, 16, axis=1), work)
    factor = jnp.zeros((8, LANES), F32)
    for k in range(8):
        prow = jnp.broadcast_to(work[k : k + 1, :], (8, LANES))
        pivot = col(prow, k)
        column = col(work, k)
        root = lax.rsqrt(pivot)
        factor = jnp.where((lane == k) & (row >= k), column * root, factor)
        below = work - (column / pivot) * prow
        work = jnp.where(row > k, below, jnp.where(row == k, work * root, work))
    pack[0] = work
    pack[1] = both
    pack[2] = factor

    for i in range(1, 8):
        ar_copy(2, i).wait_send()


def finish(vec, wfin, pack_hbm, out, alpha_hbm, lower_hbm, v, w, ob, pack, coef, small, sem, osem):
    n2 = v.shape[2]

    def loads(c):
        return (
            pltpu.make_async_copy(vec.at[0, :, :, c], v.at[:, :, c], sem.at[0, c]),
            pltpu.make_async_copy(wfin.at[:, :, c], w.at[:, :, c], sem.at[1, c]),
        )

    first = pltpu.make_async_copy(pack_hbm, pack, sem.at[3, 0])
    first.start()
    for c in range(n2):
        for copy in loads(c):
            copy.start()
    first.wait()
    small[0] = pack[1, :, 0:8]
    small[1] = pack[2, :, 0:8]
    tiny = [
        pltpu.make_async_copy(small.at[0], alpha_hbm, sem.at[3, 1]),
        pltpu.make_async_copy(small.at[1], lower_hbm, sem.at[3, 2]),
    ]
    for copy in tiny:
        copy.start()
    work = pack[0]
    for j in range(8):
        coef[j * 8 : j * 8 + 8, :] = col(work, 8 + j)
        coef[64 + j * 8 : 72 + j * 8, :] = -col(work, 16 + j)

    def out_copy(k):
        m, c = k % 2, k // 2
        return pltpu.make_async_copy(ob.at[:, m, c], out.at[0, :, m, c], osem.at[k])

    @pl.loop(0, n2)
    def _(c):
        for copy in loads(c):
            copy.wait()

        @pl.loop(0, 4)
        def _(k):
            m, h = k // 2, k % 2
            at = [pl.ds(pl.multiple_of(h * 256 + q * LANES, LANES), LANES) for q in range(2)]
            vs = [[v[j, m, c, :, at[q]] for q in range(2)] for j in range(8)]
            ws = [[w[j, m, c, :, at[q]] for q in range(2)] for j in range(8)]
            for i in range(8):
                total = None
                for base, xs, count in ((64, vs, 8), (0, ws, i + 1)):
                    for j in range(count):
                        factor = splat(coef, base + j * 8 + i)
                        terms = [factor * xs[j][q] for q in range(2)]
                        total = terms if total is None else [t + s for t, s in zip(total, terms)]
                for q in range(2):
                    ob[i, m, c, :, at[q]] = total[q]

            @pl.when(h == 1)
            def _():
                out_copy(2 * c + m).start()


    @pl.loop(0, 2 * n2)
    def _(k):
        out_copy(k).wait()

    for copy in tiny:
        copy.wait()


def shards(*args):
    (vectors, previous, beta, potential, coriolis_fn, second_fn, rot_const, coupling, *mats) = args
    block = vectors.shape[1:]
    fn = potential.shape
    any_spec = pl.BlockSpec(memory_space=pltpu.HBM)
    vmem = pl.BlockSpec(memory_space=pltpu.VMEM)
    nv, n1, n2, n3, nr = block
    dma = pltpu.SemaphoreType.DMA
    scratch = [
        pltpu.VMEM(block, F32),
        pltpu.VMEM(block, F32),
        pltpu.VMEM(fn, F32),
        pltpu.VMEM(fn, F32),
        pltpu.VMEM(fn, F32),
        pltpu.VMEM(block, F32),
        pltpu.VMEM(block, F32),
        pltpu.VMEM(block, F32),
        pltpu.VMEM(block, F32),
        pltpu.VMEM((4, 2) + block[1:], F32),
        pltpu.VMEM((4, 2) + block[1:], F32),
        pltpu.VMEM(block, F32),
        pltpu.VMEM((4,) + block, F32),
        pltpu.VMEM((2 * n2, nv, n1, n3, nr), F32),
        pltpu.VMEM((8, 8), F32),
        pltpu.SMEM((16,), F32),
        pltpu.SMEM((2, 16), F32),
        pltpu.VMEM((16, 16), F32),
        pltpu.VMEM((16, 16), F32),
        *[pltpu.VMEM((8, 8), F32)] * 5,
        pltpu.VMEM((256, LANES), F32),
        pltpu.VMEM((256, LANES), F32),
        pltpu.VMEM((64, LANES), F32),
        pltpu.VMEM((8, 8, LANES), F32),
        pltpu.VMEM((8, nr), F32),
        pltpu.VMEM((nr, nr), BF16),
        pltpu.VMEM((nr, nr), BF16),
        pltpu.VMEM((256, 256), BF16),
        pltpu.VMEM((256, 256), BF16),
        pltpu.VMEM((256 * 8, LANES), F32),
        pltpu.VMEM((2, 8, LANES), F32),
        pltpu.VMEM((3, 8, 2, LANES), F32),
        dma((17,)),
        dma((n2, 8)),
        dma((n2, 8)),
        dma((n2, 8)),
        dma((n2, 8)),
        dma((4,)),
        dma((4,)),
        dma((4,)),
        dma((4,)),
        dma((2, n2)),
        dma((2, n2)),
        dma((2, n2)),
        dma((2, n2)),
        dma((2 * n2,)),
        dma((2 * n2,)),
        dma((3, 8)),
        dma((3, 8)),
        dma((n2,)),
        pltpu.SemaphoreType.REGULAR((2,)),
        pltpu.SemaphoreType.REGULAR((2,)),
    ]
    wfin, pack = pl.pallas_call(
        kernel,
        out_shape=(
            jax.ShapeDtypeStruct(block, F32),
            jax.ShapeDtypeStruct((3, nv, LANES), F32),
        ),
        in_specs=[any_spec] * 15,
        out_specs=(any_spec, vmem),
        scratch_shapes=scratch,
        compiler_params=pltpu.CompilerParams(
            collective_id=0, has_side_effects=True, vmem_limit_bytes=67043328
        ),
        name="lanczos",
    )(vectors, previous, potential, coriolis_fn, second_fn, beta, rot_const, coupling, *mats)
    return pl.pallas_call(
        finish,
        out_shape=(
            jax.ShapeDtypeStruct(vectors.shape, F32),
            jax.ShapeDtypeStruct((nv, nv), F32),
            jax.ShapeDtypeStruct((nv, nv), F32),
        ),
        in_specs=[any_spec] * 3,
        out_specs=(any_spec,) * 3,
        scratch_shapes=[
            pltpu.VMEM(block, F32),
            pltpu.VMEM(block, F32),
            pltpu.VMEM(block, F32),
            pltpu.VMEM((3, nv, LANES), F32),
            pltpu.VMEM((128, LANES), F32),
            pltpu.VMEM((2, nv, nv), F32),
            dma((4, n2)),
            dma((2 * n2,)),
        ],
        compiler_params=pltpu.CompilerParams(vmem_limit_bytes=67043328),
        name="basis",
    )(vectors, wfin, pack)


def solution(mesh):
    split = P("ka", None, "mode", "row", None, None)
    fn = P("mode", "row", None, None)
    return jax.shard_map(
        shards,
        mesh=mesh,
        in_specs=(split, split, P(), fn, fn, fn) + (P(),) * 9,
        out_specs=(split, P(), P()),
        check_vma=False,
    )
```

```python
import jax
import jax.numpy as jnp
from jax import lax
from jax.experimental import pallas as pl
from jax.experimental.pallas import tpu as pltpu
from jax.sharding import PartitionSpec as P

F32 = jnp.float32
BF16 = jnp.bfloat16
HI = lax.Precision.HIGHEST
LANES = 128
VIA = 2
NT = (((1,), (1,)), ((), ()))


def exact(a, b):
    return jnp.dot(a, b, precision=HI, preferred_element_type=F32)


def exact_nt(a, b):
    return lax.dot_general(a, b, NT, precision=HI, preferred_element_type=F32)


def iota(shape, axis):
    return lax.broadcasted_iota(jnp.int32, shape, axis)


def hot(shape, of):
    return (of(iota(shape, 0)) == iota(shape, 1)).astype(F32)


def halves(x):
    high = x.astype(BF16)
    return high, (x - high.astype(F32)).astype(BF16)


def three_pass(x, high, low):
    xh, xl = halves(x)

    def dot(a, b):
        return jnp.dot(a, b, preferred_element_type=F32)

    return dot(xh, high) + (dot(xl, high) + dot(xh, low))


def col(a, k):
    return jnp.broadcast_to(a[:, k : k + 1], (8, LANES))


def splat(table, row):
    return table[pl.ds(row, 8, stride=0), :]


def far_first(i):
    return 4 + (i // 2) * (1 - 2 * (i % 2))


def lane_block(q):
    return pl.ds(q * LANES, LANES)


def spread(rows, left, right, table):
    n = left.shape[1]
    picked = left * (iota((rows, n), 0) % n == iota((rows, n), 1)).astype(F32)
    table[...] = exact(picked, jnp.ones((n, LANES), F32))


def kernel(
    vec,
    prev,
    pot,
    cor,
    sec,
    beta_hbm,
    rot_hbm,
    coupling_hbm,
    one_hbm,
    two_hbm,
    three_hbm,
    four_hbm,
    five_hbm,
    six_hbm,
    deriv_hbm,
    wout,
    pack,
    v,
    pv,
    po,
    cf,
    sf,
    w,
    zin,
    zout,
    zret,
    rin,
    rout,
    rret,
    yb,
    via,
    beta,
    rot,
    coupling,
    kin_one,
    kin_two,
    kin_three,
    kin_four,
    kin_five,
    kin_six,
    deriv,
    tab1,
    tab2,
    tabb,
    tab3,
    rows4,
    tkh,
    tkl,
    twh,
    twl,
    acc,
    total,
    arb,
    loc,
    zfs,
    zfr,
    zrs,
    zrr,
    rfs,
    rfr,
    rrs,
    rrr,
    yfs,
    yfr,
    yrs,
    yrr,
    vr,
    vs,
    ars,
    arr,
    obs,
    zc,
    yc,
):
    ka = lax.axis_index("ka")
    z = lax.axis_index("mode")
    r = lax.axis_index("row")
    x_hi = ka // 8
    y = ka % 8
    nv, n1, n2 = v.shape[0], v.shape[1], v.shape[2]
    u = x_hi * 4 + r
    nblocks = 16

    def local_copy(i, src, dst):
        return pltpu.make_async_copy(src, dst, loc.at[i])

    locals_ = [
        local_copy(0, vec.at[0], v),
        local_copy(1, prev.at[0], pv),
        local_copy(2, pot, po),
        local_copy(3, cor, cf),
        local_copy(4, sec, sf),
        local_copy(5, vec.at[0, z], zin.at[z]),
        local_copy(6, vec.at[0, pl.ds(2 * r, 2)], rin.at[r]),
    ]
    small = [
        (beta_hbm, beta),
        (rot_hbm, rot),
        (coupling_hbm, coupling),
        (one_hbm, kin_one),
        (two_hbm, kin_two),
        (three_hbm, kin_three),
        (four_hbm, kin_four),
        (five_hbm, kin_five),
        (six_hbm, kin_six),
        (deriv_hbm, deriv),
    ]
    small = [local_copy(7 + i, *pair) for i, pair in enumerate(small)]

    def z_peer(o):
        return {"mode": (z + o) % 8}

    def y_peer(o):
        return {"ka": x_hi * 8 + (y + o) % 8}

    def x_peer(o):
        t = (u + o) % 8
        return {"ka": (t // 4) * 8 + y, "row": t % 4}

    def z_forward(c, o):
        t = (z + o) % 8
        return pltpu.make_async_remote_copy(
            vec.at[0, t, :, c],
            zin.at[z, :, c],
            zfs.at[c, o],
            zfr.at[c, o],
            device_id=z_peer(o),
        )

    def z_back(c, o):
        t = (z + o) % 8
        return pltpu.make_async_remote_copy(
            zout.at[t, :, c],
            zret.at[z, :, c],
            zrs.at[c, o],
            zrr.at[c, o],
            device_id=z_peer(o),
        )

    def r_forward(o):
        t = (r + o) % 4
        return pltpu.make_async_remote_copy(
            vec.at[0, pl.ds(2 * t, 2)],
            rin.at[r],
            rfs.at[o],
            rfr.at[o],
            device_id={"row": t},
        )

    def r_back(o):
        t = (r + o) % 4
        return pltpu.make_async_remote_copy(
            rout.at[t],
            rret.at[pl.ds(2 * r, 2)],
            rrs.at[o],
            rrr.at[o],
            device_id={"row": t},
        )

    def y_own(c, d):
        return pltpu.make_async_remote_copy(
            vec.at[0, :, :, c],
            yb.at[d, :, :, c],
            yfs.at[d, c],
            yfr.at[d, c],
            device_id={"ka": ka + 1 - 2 * d},
        )

    def y_relay(c, d):
        return pltpu.make_async_remote_copy(
            yb.at[d, :, :, c],
            yb.at[d + 2, :, :, c],
            yrs.at[d, c],
            yrr.at[d, c],
            device_id={"ka": ka + 1 - 2 * d},
        )

    def to_via(k, c, d):
        src = vec.at[0, :, :, c] if k == 0 else yb.at[d, :, :, c]
        return pltpu.make_async_remote_copy(
            src,
            via.at[k * n2 + c],
            (yfs, yrs)[k].at[d, c],
            vr.at[k * n2 + c],
            device_id={"ka": 15 - 15 * d},
        )

    def from_via(k, c, d):
        return pltpu.make_async_remote_copy(
            via.at[k * n2 + c],
            yb.at[d + 2 * k, :, :, c],
            vs.at[k * n2 + c],
            (yfr, yrr)[k].at[d, c],
            device_id={"ka": 8 - d},
        )

    at_edge = (ka == 7, ka == 8)
    is_via = (ka == 15, ka == 0)

    def send_on(k, c, d, cond):
        detour = jnp.logical_and(at_edge[d], c < VIA)

        @pl.when(jnp.logical_and(cond, detour))
        def _():
            to_via(k, c, d).start()

        @pl.when(jnp.logical_and(cond, jnp.logical_not(detour)))
        def _():
            (y_own, y_relay)[k](c, d).start()

    def pass_on(k, c):
        for d in range(2):

            @pl.when(is_via[d])
            def _():
                to_via(k, c, d).wait_recv()
                from_via(k, c, d).start()

    can_send = (ka < nblocks - 1, ka > 0)
    has_one = (ka > 0, ka < nblocks - 1)
    has_two = (ka > 1, ka < nblocks - 2)

    barrier = pltpu.get_barrier_semaphore()
    edge = jnp.logical_or(ka == 7, ka == 8)

    for o in range(1, 8):
        pl.semaphore_signal(barrier, inc=1, device_id=x_peer(o))
    for o in (1, 7):
        pl.semaphore_signal(barrier, inc=1, device_id=y_peer(o))
        pl.semaphore_signal(barrier, inc=1, device_id=z_peer(o))

    @pl.when(edge)
    def _():
        pl.semaphore_signal(barrier, inc=1, device_id={"ka": 15 - ka})

    pl.semaphore_wait(barrier, 11 + edge.astype(jnp.int32))

    def farther(sem, peer):
        pl.semaphore_signal(sem.at[0], inc=1, device_id=peer(1))
        pl.semaphore_signal(sem.at[1], inc=1, device_id=peer(7))
        pl.semaphore_wait(sem.at[0], 1)
        pl.semaphore_wait(sem.at[1], 1)

    for o in range(1, 4):
        r_forward(o).start()
    for o in (1, 7):
        z_forward(0, o).start()
    for c in range(n2):
        for d in range(2):
            send_on(0, c, d, can_send[d])
    for offsets in ((2, 6), (3, 5), (4,)):
        farther(zc, z_peer)
        for o in offsets:
            z_forward(0, o).start()
    for c in range(1, n2):

        @pl.loop(1, 8)
        def _(i):
            z_forward(c, far_first(i)).start()

    for copy in small + locals_:
        copy.start()
    for _ in range(3):
        farther(yc, y_peer)

    for d in range(2):

        @pl.when(jnp.logical_not(has_one[d]))
        def _():
            yb[d] = jnp.zeros(yb.shape[1:], F32)

        @pl.when(jnp.logical_not(has_two[d]))
        def _():
            yb[d + 2] = jnp.zeros(yb.shape[1:], F32)

    for copy in small:
        copy.wait()

    def table_of(matrix, table):
        n = matrix.shape[0]
        pick = hot((n * n, n), lambda q: q // n)
        both = 0.5 * (exact(pick, matrix[...]) + exact_nt(pick, matrix[...]))
        spread(n * n, both, None, table)

    table_of(kin_one, tab1)
    table_of(kin_two, tab2)
    spread(64, exact(hot((64, 8), lambda q: q // 8), beta[...]), None, tabb)
    eye8 = hot((8, 8), lambda q: q)
    sym3 = 0.5 * (kin_three[...] + exact_nt(eye8, kin_three[...]))
    for s in range(8):
        mask = (iota((8, 8), 0) + (8 - s)) % 8 == iota((8, 8), 1)
        tab3[s] = exact(jnp.where(mask, sym3, 0.0), jnp.ones((8, LANES), F32))

    def expand(pick, matrix, pick_t):
        both = 0.5 * (exact(pick, matrix[...]) + exact_nt(pick, matrix[...]))
        return exact_nt(both, pick_t)

    rows4[...] = expand(eye8, kin_four, hot((512, 8), lambda q: q // 64))
    e5 = expand(hot((64, 8), lambda q: q // 8), kin_five, hot((512, 8), lambda q: (q // 8) % 8))
    e6 = expand(hot((64, 8), lambda q: q % 8), kin_six, hot((512, 8), lambda q: q % 8))
    qi = iota((64, 512), 0)
    pi = iota((64, 512), 1)
    m56 = jnp.where(pi % 8 == qi % 8, e5, 0.0) + jnp.where((pi // 8) % 8 == qi // 8, e6, 0.0)
    diag64 = pi % 64 == qi
    for k in range(8):
        block = jnp.where(diag64, rows4[k : k + 1, :], 0.0) + jnp.where(pi // 64 == k, m56, 0.0)
        high, low = halves(block)
        tkh[k * 64 : (k + 1) * 64, :] = high
        tkl[k * 64 : (k + 1) * 64, :] = low
    pick6 = hot((256, 8), lambda q: q % 8)
    turned = 0.5 * (exact_nt(pick6, deriv[...]) - exact(pick6, deriv[...]))
    full = jnp.where(iota((256, 256), 0) // 8 == iota((256, 256), 1) // 8, exact_nt(turned, pick6), 0.0)
    high, low = halves(full)
    twh[...] = high
    twl[...] = low
    acc[...] = jnp.zeros(acc.shape, F32)

    level = (ka - nblocks // 2).astype(F32)
    shift = rot[ka] * level * level
    near = coupling[0, ka]
    near_low = coupling[0, jnp.maximum(ka - 1, 0)]
    far = coupling[1, ka]
    far_low = coupling[1, jnp.maximum(ka - 2, 0)]

    def mix16(load, store, table):
        xs = [[load(b, q) for q in range(2)] for b in range(16)]
        for a in range(16):
            total = None
            for b in range(16):
                k = splat(table, a * 16 + b)
                terms = [k * xs[b][q] for q in range(2)]
                total = terms if total is None else [t + s for t, s in zip(total, terms)]
            for q in range(2):
                store(a, q, total[q])

    def first_mode(c):
        @pl.loop(0, 2)
        def _(h):
            def at(q):
                return pl.ds(pl.multiple_of(h * 256 + q * LANES, LANES), LANES)

            def load(b, q):
                return zin[b // 2, b % 2, c, :, at(q)]

            def store(a, q, val):
                zout[a // 2, a % 2, c, :, at(q)] = val

            mix16(load, store, tab1)

        zret[z, :, c] = zout[z, :, c]

    def second_mode():
        @pl.loop(0, 8)
        def _(k):
            n, m, h = k // 4, (k // 2) % 2, k % 2

            def at(q):
                return pl.ds(pl.multiple_of(h * 256 + q * LANES, LANES), LANES)

            def load(b, q):
                return rin[b // 4, n, m, b % 4, :, at(q)]

            def store(a, q, val):
                rout[a // 4, n, m, a % 4, :, at(q)] = val

            mix16(load, store, tab2)

        rret[pl.ds(2 * r, 2)] = rout[r]

    def gather_products(c, left, right, spots, triangle):
        for g in range(4):
            pairs = [(j, i) for i in (2 * g, 2 * g + 1) for j in range(8) if j <= i or not triangle]
            sums = {}
            for m in range(n1):
                for q in range(4):
                    ls = [left[j, m, c, :, lane_block(q)] for j in range(8)]
                    rs = [right[i, m, c, :, lane_block(q)] for i in (2 * g, 2 * g + 1)]
                    for j, i in pairs:
                        term = ls[j] * rs[i - 2 * g]
                        sums[j, i] = term if (j, i) not in sums else sums[j, i] + term
            for j, i in pairs:
                for spot in spots(j, i):
                    acc[spot * 8 : spot * 8 + 8, :] += sums[j, i]

    def local_terms(c):
        x = v[:, :, c].reshape(nv * n1 * 8, 512)
        w[:, :, c] = three_pass(x, tkh[...], tkl[...]).reshape(nv, n1, 8, 512)

        @pl.loop(0, 4)
        def _(k):
            m, h = k // 2, k % 2
            for q in range(2):
                at = pl.ds(pl.multiple_of(h * 256 + q * LANES, LANES), LANES)
                old = [pv[j, m, c, :, at] for j in range(8)]
                diag = po[m, c, :, at] + shift
                for i in range(8):
                    xi = v[i, m, c, :, at]
                    total = w[i, m, c, :, at] + (diag + tab3[0]) * xi
                    for s in range(1, 8):
                        total = total + tab3[s] * pltpu.roll(xi, s, axis=0)
                    taken = splat(tabb, i * 8) * old[0]
                    for j in range(1, 8):
                        taken = taken + splat(tabb, i * 8 + j) * old[j]
                    w[i, m, c, :, at] = total - taken

        gather_products(c, v, v, lambda j, i: {(24 + j) * 8 + i, (24 + i) * 8 + j}, True)

    def turn(x):
        flat = x.reshape(nv * n1 * 8, 512)
        parts = [three_pass(flat[:, h * 256 : h * 256 + 256], twh[...], twl[...]) for h in range(2)]
        return jnp.concatenate(parts, axis=1).reshape(x.shape)

    def near_terms(c):
        fn = cf[:, c][None]
        above = turn(yb[1, :, :, c])
        w[:, :, c] += (near * fn) * above
        below = turn(fn * yb[0, :, :, c])
        w[:, :, c] -= near_low * below

    def wait_recv_when(cond, copy):
        @pl.when(cond)
        def _():
            copy.wait_recv()

    for copy in locals_:
        copy.wait()

    @pl.loop(0, n2)
    def _(c):
        for d in range(2):
            wait_recv_when(has_one[d], y_own(c, d))

            send_on(1, c, d, jnp.logical_and(has_one[d], can_send[d]))

        @pl.when(c < VIA)
        def _():
            pass_on(0, c)

        @pl.loop(1, 8)
        def _(o):
            z_forward(c, o).wait_recv()

        first_mode(c)

        @pl.loop(1, 8)
        def _(o):
            z_back(c, far_first(o)).start()

        @pl.when(c == 1)
        def _():
            for o in range(1, 4):
                r_forward(o).wait_recv()
            second_mode()
            for o in range(1, 4):
                r_back(o).start()

        local_terms(c)
        near_terms(c)

    lane = iota((8, LANES), 1)
    row = iota((8, LANES), 0)

    def sum_into(count, shift, at):
        rows = count * 8
        part = acc[pl.ds(at * 64, rows, stride=8), :]
        for s in range(1, 8):
            part = part + acc[pl.ds(at * 64 + s, rows, stride=8), :]
        sums = jnp.sum(part, axis=1, keepdims=True)
        for a in range(2):
            packed = total[a]
            for l in range(count):
                q = l + shift
                if q // 16 == a:
                    here = lane == row + (q % 16) * 8
                    packed = jnp.where(here, sums[l * 8 : l * 8 + 8], packed)
            total[a] = packed

    total[...] = jnp.zeros((2, 8, LANES), F32)
    sum_into(8, 0, 24)

    def w_copy(c):
        return pltpu.make_async_copy(w.at[:, :, c], wout.at[:, :, c], obs.at[c])

    for c in range(VIA):
        pass_on(1, c)

    @pl.loop(0, n2)
    def _(c):
        @pl.loop(1, 8)
        def _(o):
            z_forward(c, o).wait_send()

        for d in range(2):

            @pl.when(can_send[d])
            def _():
                y_own(c, d).wait_send()

    for o in range(1, 4):
        r_forward(o).wait_send()

    def wait_sends_back():
        @pl.loop(0, n2)
        def _(c):
            w_copy(c).wait()

            @pl.loop(1, 8)
            def _(o):
                z_back(c, o).wait_send()

            for d in range(2):

                @pl.when(jnp.logical_and(has_one[d], can_send[d]))
                def _():
                    y_relay(c, d).wait_send()

        for k in range(2):
            for c in range(VIA):
                for d in range(2):

                    @pl.when(is_via[d])
                    def _():
                        from_via(k, c, d).wait_send()

        for o in range(1, 4):
            r_back(o).wait_send()

    for o in range(1, 4):
        r_back(o).wait_recv()

    @pl.loop(0, n2)
    def _(c):
        @pl.loop(1, 8)
        def _(o):
            z_back(c, o).wait_recv()

        for d in range(2):
            wait_recv_when(has_two[d], y_relay(c, d))

        @pl.loop(0, nv)
        def _(n):
            for m in range(n1):
                skip = sf[m, c] * (far * yb[3, n, m, c] + far_low * yb[2, n, m, c])
                w[n, m, c] = (w[n, m, c] + rret[n, m, c]) + (zret[n, m, c] + skip)

        w_copy(c).start()
        gather_products(c, v, w, lambda j, i: (j * 8 + i, (16 + i) * 8 + j), False)
        gather_products(c, w, w, lambda j, i: {(8 + j) * 8 + i, (8 + i) * 8 + j}, True)

    sum_into(24, 8, 0)
    msg = jnp.concatenate([jnp.sum(total[a], axis=0, keepdims=True) for a in range(2)], axis=0)

    groups = ((u, x_peer), (z, z_peer), (y, y_peer))

    def ar_copy(g, o):
        me, peer = groups[g]
        return pltpu.make_async_remote_copy(
            arb.at[g, me], arb.at[g, me], ars.at[g, o], arr.at[g, o], device_id=peer(o)
        )

    for g in range(3):
        arb[g, groups[g][0]] = msg
        for i in range(1, 8):
            ar_copy(g, far_first(i)).start()
        if g == 0:
            wait_sends_back()
        else:
            for i in range(1, 8):
                ar_copy(g - 1, i).wait_send()
        for i in range(1, 8):
            ar_copy(g, i).wait_recv()
        msg = arb[g, 0]
        for t in range(1, 8):
            msg = msg + arb[g, t]

    msg = msg * (1.0 / float(16 * 8 * 4 * 32768))

    def mm(a, b):
        total = col(a, 0) * b[0:1, :]
        for k in range(1, 8):
            total = total + col(a, k) * b[k : k + 1, :]
        return total

    own = [jnp.where(lane % 8 == row, msg[a : a + 1, :], 0.0) for a in range(2)]
    whole = exact(jnp.concatenate(own, axis=0), hot((LANES, LANES), lambda q: q // 8))
    overlap = whole[0:8]
    first_t = pltpu.roll(overlap, LANES - 8, axis=1)
    square = whole[8:16]
    first = pltpu.roll(square, LANES - 8, axis=1)
    both_t = 2.0 * first_t - mm(first_t, overlap)
    both = 2.0 * first - mm(overlap, first)
    gram = square - mm(both_t, first) - mm(first_t, both) + mm(mm(both_t, overlap), both)
    work = jnp.where(lane < 8, gram, 0.0)
    work = jnp.where(lane == row + 8, 1.0, work)
    work = jnp.where((lane >= 16) & (lane < 24), pltpu.roll(both_t, 16, axis=1), work)
    factor = jnp.zeros((8, LANES), F32)
    for k in range(8):
        prow = jnp.broadcast_to(work[k : k + 1, :], (8, LANES))
        pivot = col(prow, k)
        column = col(work, k)
        root = lax.rsqrt(pivot)
        factor = jnp.where((lane == k) & (row >= k), column * root, factor)
        below = work - (column / pivot) * prow
        work = jnp.where(row > k, below, jnp.where(row == k, work * root, work))
    pack[0] = work
    pack[1] = both
    pack[2] = factor

    for i in range(1, 8):
        ar_copy(2, i).wait_send()


def finish(vec, wfin, pack_hbm, out, alpha_hbm, lower_hbm, v, w, ob, pack, coef, small, sem, osem):
    n2 = v.shape[2]

    def loads(c):
        return (
            pltpu.make_async_copy(vec.at[0, :, :, c], v.at[:, :, c], sem.at[0, c]),
            pltpu.make_async_copy(wfin.at[:, :, c], w.at[:, :, c], sem.at[1, c]),
        )

    first = pltpu.make_async_copy(pack_hbm, pack, sem.at[3, 0])
    first.start()
    for c in range(n2):
        for copy in loads(c):
            copy.start()
    first.wait()
    small[0] = pack[1, :, 0:8]
    small[1] = pack[2, :, 0:8]
    tiny = [
        pltpu.make_async_copy(small.at[0], alpha_hbm, sem.at[3, 1]),
        pltpu.make_async_copy(small.at[1], lower_hbm, sem.at[3, 2]),
    ]
    for copy in tiny:
        copy.start()
    work = pack[0]
    for j in range(8):
        coef[j * 8 : j * 8 + 8, :] = col(work, 8 + j)
        coef[64 + j * 8 : 72 + j * 8, :] = -col(work, 16 + j)

    def out_copy(k):
        m, c = k % 2, k // 2
        return pltpu.make_async_copy(ob.at[:, m, c], out.at[0, :, m, c], osem.at[k])

    @pl.loop(0, n2)
    def _(c):
        for copy in loads(c):
            copy.wait()

        @pl.loop(0, 4)
        def _(k):
            m, h = k // 2, k % 2
            at = [pl.ds(pl.multiple_of(h * 256 + q * LANES, LANES), LANES) for q in range(2)]
            vs = [[v[j, m, c, :, at[q]] for q in range(2)] for j in range(8)]
            ws = [[w[j, m, c, :, at[q]] for q in range(2)] for j in range(8)]
            for i in range(8):
                total = None
                for base, xs, count in ((64, vs, 8), (0, ws, i + 1)):
                    for j in range(count):
                        factor = splat(coef, base + j * 8 + i)
                        terms = [factor * xs[j][q] for q in range(2)]
                        total = terms if total is None else [t + s for t, s in zip(total, terms)]
                for q in range(2):
                    ob[i, m, c, :, at[q]] = total[q]

            @pl.when(h == 1)
            def _():
                out_copy(2 * c + m).start()


    @pl.loop(0, 2 * n2)
    def _(k):
        out_copy(k).wait()

    for copy in tiny:
        copy.wait()


def shards(*args):
    (vectors, previous, beta, potential, coriolis_fn, second_fn, rot_const, coupling, *mats) = args
    block = vectors.shape[1:]
    fn = potential.shape
    any_spec = pl.BlockSpec(memory_space=pltpu.HBM)
    vmem = pl.BlockSpec(memory_space=pltpu.VMEM)
    nv, n1, n2, n3, nr = block
    dma = pltpu.SemaphoreType.DMA
    scratch = [
        pltpu.VMEM(block, F32),
        pltpu.VMEM(block, F32),
        pltpu.VMEM(fn, F32),
        pltpu.VMEM(fn, F32),
        pltpu.VMEM(fn, F32),
        pltpu.VMEM(block, F32),
        pltpu.VMEM(block, F32),
        pltpu.VMEM(block, F32),
        pltpu.VMEM(block, F32),
        pltpu.VMEM((4, 2) + block[1:], F32),
        pltpu.VMEM((4, 2) + block[1:], F32),
        pltpu.VMEM(block, F32),
        pltpu.VMEM((4,) + block, F32),
        pltpu.VMEM((2 * n2, nv, n1, n3, nr), F32),
        pltpu.VMEM((8, 8), F32),
        pltpu.SMEM((16,), F32),
        pltpu.SMEM((2, 16), F32),
        pltpu.VMEM((16, 16), F32),
        pltpu.VMEM((16, 16), F32),
        *[pltpu.VMEM((8, 8), F32)] * 5,
        pltpu.VMEM((256, LANES), F32),
        pltpu.VMEM((256, LANES), F32),
        pltpu.VMEM((64, LANES), F32),
        pltpu.VMEM((8, 8, LANES), F32),
        pltpu.VMEM((8, nr), F32),
        pltpu.VMEM((nr, nr), BF16),
        pltpu.VMEM((nr, nr), BF16),
        pltpu.VMEM((256, 256), BF16),
        pltpu.VMEM((256, 256), BF16),
        pltpu.VMEM((256 * 8, LANES), F32),
        pltpu.VMEM((2, 8, LANES), F32),
        pltpu.VMEM((3, 8, 2, LANES), F32),
        dma((17,)),
        dma((n2, 8)),
        dma((n2, 8)),
        dma((n2, 8)),
        dma((n2, 8)),
        dma((4,)),
        dma((4,)),
        dma((4,)),
        dma((4,)),
        dma((2, n2)),
        dma((2, n2)),
        dma((2, n2)),
        dma((2, n2)),
        dma((2 * n2,)),
        dma((2 * n2,)),
        dma((3, 8)),
        dma((3, 8)),
        dma((n2,)),
        pltpu.SemaphoreType.REGULAR((2,)),
        pltpu.SemaphoreType.REGULAR((2,)),
    ]
    wfin, pack = pl.pallas_call(
        kernel,
        out_shape=(
            jax.ShapeDtypeStruct(block, F32),
            jax.ShapeDtypeStruct((3, nv, LANES), F32),
        ),
        in_specs=[any_spec] * 15,
        out_specs=(any_spec, vmem),
        scratch_shapes=scratch,
        compiler_params=pltpu.CompilerParams(
            collective_id=0, has_side_effects=True, vmem_limit_bytes=67043328
        ),
        name="lanczos",
    )(vectors, previous, potential, coriolis_fn, second_fn, beta, rot_const, coupling, *mats)
    return pl.pallas_call(
        finish,
        out_shape=(
            jax.ShapeDtypeStruct(vectors.shape, F32),
            jax.ShapeDtypeStruct((nv, nv), F32),
            jax.ShapeDtypeStruct((nv, nv), F32),
        ),
        in_specs=[any_spec] * 3,
        out_specs=(any_spec,) * 3,
        scratch_shapes=[
            pltpu.VMEM(block, F32),
            pltpu.VMEM(block, F32),
            pltpu.VMEM(block, F32),
            pltpu.VMEM((3, nv, LANES), F32),
            pltpu.VMEM((128, LANES), F32),
            pltpu.VMEM((2, nv, nv), F32),
            dma((4, n2)),
            dma((2 * n2,)),
        ],
        compiler_params=pltpu.CompilerParams(vmem_limit_bytes=67043328),
        name="basis",
    )(vectors, wfin, pack)


def solution(mesh):
    split = P("ka", None, "mode", "row", None, None)
    fn = P("mode", "row", None, None)
    return jax.shard_map(
        shards,
        mesh=mesh,
        in_specs=(split, split, P(), fn, fn, fn) + (P(),) * 9,
        out_specs=(split, P(), P()),
        check_vma=False,
    )
```

```python
import jax
import jax.numpy as jnp
from jax import lax
from jax.experimental import pallas as pl
from jax.experimental.pallas import tpu as pltpu
from jax.sharding import PartitionSpec as P

F32 = jnp.float32
BF16 = jnp.bfloat16
HI = lax.Precision.HIGHEST
LANES = 128
VIA = 2
NT = (((1,), (1,)), ((), ()))


def exact(a, b):
    return jnp.dot(a, b, precision=HI, preferred_element_type=F32)


def exact_nt(a, b):
    return lax.dot_general(a, b, NT, precision=HI, preferred_element_type=F32)


def iota(shape, axis):
    return lax.broadcasted_iota(jnp.int32, shape, axis)


def hot(shape, of):
    return (of(iota(shape, 0)) == iota(shape, 1)).astype(F32)


def halves(x):
    high = x.astype(BF16)
    return high, (x - high.astype(F32)).astype(BF16)


def three_pass(x, high, low):
    xh, xl = halves(x)

    def dot(a, b):
        return jnp.dot(a, b, preferred_element_type=F32)

    return dot(xh, high) + (dot(xl, high) + dot(xh, low))


def col(a, k):
    return jnp.broadcast_to(a[:, k : k + 1], (8, LANES))


def splat(table, row):
    return table[pl.ds(row, 8, stride=0), :]


def far_first(i):
    return 4 + (i // 2) * (1 - 2 * (i % 2))


def lane_block(q):
    return pl.ds(q * LANES, LANES)


def spread(rows, left, right, table):
    n = left.shape[1]
    picked = left * (iota((rows, n), 0) % n == iota((rows, n), 1)).astype(F32)
    table[...] = exact(picked, jnp.ones((n, LANES), F32))


def kernel(
    vec,
    prev,
    pot,
    cor,
    sec,
    beta_hbm,
    rot_hbm,
    coupling_hbm,
    one_hbm,
    two_hbm,
    three_hbm,
    four_hbm,
    five_hbm,
    six_hbm,
    deriv_hbm,
    wout,
    pack,
    v,
    pv,
    po,
    cf,
    sf,
    w,
    zin,
    zout,
    zret,
    rin,
    rout,
    rret,
    yb,
    via,
    beta,
    rot,
    coupling,
    kin_one,
    kin_two,
    kin_three,
    kin_four,
    kin_five,
    kin_six,
    deriv,
    tab1,
    tab2,
    tabb,
    tab3,
    rows4,
    tkh,
    tkl,
    twh,
    twl,
    acc,
    total,
    arb,
    loc,
    zfs,
    zfr,
    zrs,
    zrr,
    rfs,
    rfr,
    rrs,
    rrr,
    yfs,
    yfr,
    yrs,
    yrr,
    vr,
    vs,
    ars,
    arr,
    obs,
):
    ka = lax.axis_index("ka")
    z = lax.axis_index("mode")
    r = lax.axis_index("row")
    x_hi = ka // 8
    y = ka % 8
    nv, n1, n2 = v.shape[0], v.shape[1], v.shape[2]
    u = x_hi * 4 + r
    nblocks = 16

    def local_copy(i, src, dst):
        return pltpu.make_async_copy(src, dst, loc.at[i])

    locals_ = [
        local_copy(0, vec.at[0], v),
        local_copy(1, prev.at[0], pv),
        local_copy(2, pot, po),
        local_copy(3, cor, cf),
        local_copy(4, sec, sf),
        local_copy(5, vec.at[0, z], zin.at[z]),
        local_copy(6, vec.at[0, pl.ds(2 * r, 2)], rin.at[r]),
    ]
    small = [
        (beta_hbm, beta),
        (rot_hbm, rot),
        (coupling_hbm, coupling),
        (one_hbm, kin_one),
        (two_hbm, kin_two),
        (three_hbm, kin_three),
        (four_hbm, kin_four),
        (five_hbm, kin_five),
        (six_hbm, kin_six),
        (deriv_hbm, deriv),
    ]
    small = [local_copy(7 + i, *pair) for i, pair in enumerate(small)]

    def z_peer(o):
        return {"mode": (z + o) % 8}

    def y_peer(o):
        return {"ka": x_hi * 8 + (y + o) % 8}

    def x_peer(o):
        t = (u + o) % 8
        return {"ka": (t // 4) * 8 + y, "row": t % 4}

    def z_forward(c, o):
        t = (z + o) % 8
        return pltpu.make_async_remote_copy(
            vec.at[0, t, :, c],
            zin.at[z, :, c],
            zfs.at[c, o],
            zfr.at[c, o],
            device_id=z_peer(o),
        )

    def z_back(c, o):
        t = (z + o) % 8
        return pltpu.make_async_remote_copy(
            zout.at[t, :, c],
            zret.at[z, :, c],
            zrs.at[c, o],
            zrr.at[c, o],
            device_id=z_peer(o),
        )

    def r_forward(o):
        t = (r + o) % 4
        return pltpu.make_async_remote_copy(
            vec.at[0, pl.ds(2 * t, 2)],
            rin.at[r],
            rfs.at[o],
            rfr.at[o],
            device_id={"row": t},
        )

    def r_back(o):
        t = (r + o) % 4
        return pltpu.make_async_remote_copy(
            rout.at[t],
            rret.at[pl.ds(2 * r, 2)],
            rrs.at[o],
            rrr.at[o],
            device_id={"row": t},
        )

    def y_own(c, d):
        return pltpu.make_async_remote_copy(
            vec.at[0, :, :, c],
            yb.at[d, :, :, c],
            yfs.at[d, c],
            yfr.at[d, c],
            device_id={"ka": ka + 1 - 2 * d},
        )

    def y_relay(c, d):
        return pltpu.make_async_remote_copy(
            yb.at[d, :, :, c],
            yb.at[d + 2, :, :, c],
            yrs.at[d, c],
            yrr.at[d, c],
            device_id={"ka": ka + 1 - 2 * d},
        )

    def to_via(k, c, d):
        src = vec.at[0, :, :, c] if k == 0 else yb.at[d, :, :, c]
        return pltpu.make_async_remote_copy(
            src,
            via.at[k * n2 + c],
            (yfs, yrs)[k].at[d, c],
            vr.at[k * n2 + c],
            device_id={"ka": 15 - 15 * d},
        )

    def from_via(k, c, d):
        return pltpu.make_async_remote_copy(
            via.at[k * n2 + c],
            yb.at[d + 2 * k, :, :, c],
            vs.at[k * n2 + c],
            (yfr, yrr)[k].at[d, c],
            device_id={"ka": 8 - d},
        )

    at_edge = (ka == 7, ka == 8)
    is_via = (ka == 15, ka == 0)

    def send_on(k, c, d, cond):
        detour = jnp.logical_and(at_edge[d], c < VIA)

        @pl.when(jnp.logical_and(cond, detour))
        def _():
            to_via(k, c, d).start()

        @pl.when(jnp.logical_and(cond, jnp.logical_not(detour)))
        def _():
            (y_own, y_relay)[k](c, d).start()

    def pass_on(k, c):
        for d in range(2):

            @pl.when(is_via[d])
            def _():
                to_via(k, c, d).wait_recv()
                from_via(k, c, d).start()

    can_send = (ka < nblocks - 1, ka > 0)
    has_one = (ka > 0, ka < nblocks - 1)
    has_two = (ka > 1, ka < nblocks - 2)

    barrier = pltpu.get_barrier_semaphore()
    edge = jnp.logical_or(ka == 7, ka == 8)

    for i in range(1, 8):
        for peer in (z_peer, y_peer, x_peer):
            pl.semaphore_signal(barrier, inc=1, device_id=peer(far_first(i)))

    @pl.when(edge)
    def _():
        pl.semaphore_signal(barrier, inc=1, device_id={"ka": 15 - ka})

    pl.semaphore_wait(barrier, 21 + edge.astype(jnp.int32))

    def start_chunk(c):
        @pl.loop(1, 8)
        def _(o):
            z_forward(c, far_first(o)).start()

        for d in range(2):

            send_on(0, c, d, can_send[d])

    for o in range(1, 4):
        r_forward(o).start()
    start_chunk(0)
    for copy in small + locals_:
        copy.start()
    for c in range(1, n2):
        start_chunk(c)

    for d in range(2):

        @pl.when(jnp.logical_not(has_one[d]))
        def _():
            yb[d] = jnp.zeros(yb.shape[1:], F32)

        @pl.when(jnp.logical_not(has_two[d]))
        def _():
            yb[d + 2] = jnp.zeros(yb.shape[1:], F32)

    for copy in small:
        copy.wait()

    def table_of(matrix, table):
        n = matrix.shape[0]
        pick = hot((n * n, n), lambda q: q // n)
        both = 0.5 * (exact(pick, matrix[...]) + exact_nt(pick, matrix[...]))
        spread(n * n, both, None, table)

    table_of(kin_one, tab1)
    table_of(kin_two, tab2)
    spread(64, exact(hot((64, 8), lambda q: q // 8), beta[...]), None, tabb)
    eye8 = hot((8, 8), lambda q: q)
    sym3 = 0.5 * (kin_three[...] + exact_nt(eye8, kin_three[...]))
    for s in range(8):
        mask = (iota((8, 8), 0) + (8 - s)) % 8 == iota((8, 8), 1)
        tab3[s] = exact(jnp.where(mask, sym3, 0.0), jnp.ones((8, LANES), F32))

    def expand(pick, matrix, pick_t):
        both = 0.5 * (exact(pick, matrix[...]) + exact_nt(pick, matrix[...]))
        return exact_nt(both, pick_t)

    rows4[...] = expand(eye8, kin_four, hot((512, 8), lambda q: q // 64))
    e5 = expand(hot((64, 8), lambda q: q // 8), kin_five, hot((512, 8), lambda q: (q // 8) % 8))
    e6 = expand(hot((64, 8), lambda q: q % 8), kin_six, hot((512, 8), lambda q: q % 8))
    qi = iota((64, 512), 0)
    pi = iota((64, 512), 1)
    m56 = jnp.where(pi % 8 == qi % 8, e5, 0.0) + jnp.where((pi // 8) % 8 == qi // 8, e6, 0.0)
    diag64 = pi % 64 == qi
    for k in range(8):
        block = jnp.where(diag64, rows4[k : k + 1, :], 0.0) + jnp.where(pi // 64 == k, m56, 0.0)
        high, low = halves(block)
        tkh[k * 64 : (k + 1) * 64, :] = high
        tkl[k * 64 : (k + 1) * 64, :] = low
    pick6 = hot((256, 8), lambda q: q % 8)
    turned = 0.5 * (exact_nt(pick6, deriv[...]) - exact(pick6, deriv[...]))
    full = jnp.where(iota((256, 256), 0) // 8 == iota((256, 256), 1) // 8, exact_nt(turned, pick6), 0.0)
    high, low = halves(full)
    twh[...] = high
    twl[...] = low
    acc[...] = jnp.zeros(acc.shape, F32)

    level = (ka - nblocks // 2).astype(F32)
    shift = rot[ka] * level * level
    near = coupling[0, ka]
    near_low = coupling[0, jnp.maximum(ka - 1, 0)]
    far = coupling[1, ka]
    far_low = coupling[1, jnp.maximum(ka - 2, 0)]

    def mix16(load, store, table):
        xs = [[load(b, q) for q in range(2)] for b in range(16)]
        for a in range(16):
            total = None
            for b in range(16):
                k = splat(table, a * 16 + b)
                terms = [k * xs[b][q] for q in range(2)]
                total = terms if total is None else [t + s for t, s in zip(total, terms)]
            for q in range(2):
                store(a, q, total[q])

    def first_mode(c):
        @pl.loop(0, 2)
        def _(h):
            def at(q):
                return pl.ds(pl.multiple_of(h * 256 + q * LANES, LANES), LANES)

            def load(b, q):
                return zin[b // 2, b % 2, c, :, at(q)]

            def store(a, q, val):
                zout[a // 2, a % 2, c, :, at(q)] = val

            mix16(load, store, tab1)

        zret[z, :, c] = zout[z, :, c]

    def second_mode():
        @pl.loop(0, 8)
        def _(k):
            n, m, h = k // 4, (k // 2) % 2, k % 2

            def at(q):
                return pl.ds(pl.multiple_of(h * 256 + q * LANES, LANES), LANES)

            def load(b, q):
                return rin[b // 4, n, m, b % 4, :, at(q)]

            def store(a, q, val):
                rout[a // 4, n, m, a % 4, :, at(q)] = val

            mix16(load, store, tab2)

        rret[pl.ds(2 * r, 2)] = rout[r]

    def gather_products(c, left, right, spots, triangle):
        for g in range(4):
            pairs = [(j, i) for i in (2 * g, 2 * g + 1) for j in range(8) if j <= i or not triangle]
            sums = {}
            for m in range(n1):
                for q in range(4):
                    ls = [left[j, m, c, :, lane_block(q)] for j in range(8)]
                    rs = [right[i, m, c, :, lane_block(q)] for i in (2 * g, 2 * g + 1)]
                    for j, i in pairs:
                        term = ls[j] * rs[i - 2 * g]
                        sums[j, i] = term if (j, i) not in sums else sums[j, i] + term
            for j, i in pairs:
                for spot in spots(j, i):
                    acc[spot * 8 : spot * 8 + 8, :] += sums[j, i]

    def local_terms(c):
        x = v[:, :, c].reshape(nv * n1 * 8, 512)
        w[:, :, c] = three_pass(x, tkh[...], tkl[...]).reshape(nv, n1, 8, 512)

        @pl.loop(0, 4)
        def _(k):
            m, h = k // 2, k % 2
            for q in range(2):
                at = pl.ds(pl.multiple_of(h * 256 + q * LANES, LANES), LANES)
                old = [pv[j, m, c, :, at] for j in range(8)]
                diag = po[m, c, :, at] + shift
                for i in range(8):
                    xi = v[i, m, c, :, at]
                    total = w[i, m, c, :, at] + (diag + tab3[0]) * xi
                    for s in range(1, 8):
                        total = total + tab3[s] * pltpu.roll(xi, s, axis=0)
                    taken = splat(tabb, i * 8) * old[0]
                    for j in range(1, 8):
                        taken = taken + splat(tabb, i * 8 + j) * old[j]
                    w[i, m, c, :, at] = total - taken

        gather_products(c, v, v, lambda j, i: {(24 + j) * 8 + i, (24 + i) * 8 + j}, True)

    def turn(x):
        flat = x.reshape(nv * n1 * 8, 512)
        parts = [three_pass(flat[:, h * 256 : h * 256 + 256], twh[...], twl[...]) for h in range(2)]
        return jnp.concatenate(parts, axis=1).reshape(x.shape)

    def near_terms(c):
        fn = cf[:, c][None]
        above = turn(yb[1, :, :, c])
        w[:, :, c] += (near * fn) * above
        below = turn(fn * yb[0, :, :, c])
        w[:, :, c] -= near_low * below

    def wait_recv_when(cond, copy):
        @pl.when(cond)
        def _():
            copy.wait_recv()

    for copy in locals_:
        copy.wait()

    @pl.loop(0, n2)
    def _(c):
        for d in range(2):
            wait_recv_when(has_one[d], y_own(c, d))

            send_on(1, c, d, jnp.logical_and(has_one[d], can_send[d]))

        @pl.when(c < VIA)
        def _():
            pass_on(0, c)

        @pl.loop(1, 8)
        def _(o):
            z_forward(c, o).wait_recv()

        first_mode(c)

        @pl.loop(1, 8)
        def _(o):
            z_back(c, far_first(o)).start()

        @pl.when(c == 1)
        def _():
            for o in range(1, 4):
                r_forward(o).wait_recv()
            second_mode()
            for o in range(1, 4):
                r_back(o).start()

        local_terms(c)
        near_terms(c)

    lane = iota((8, LANES), 1)
    row = iota((8, LANES), 0)

    def sum_into(count, shift, at):
        rows = count * 8
        part = acc[pl.ds(at * 64, rows, stride=8), :]
        for s in range(1, 8):
            part = part + acc[pl.ds(at * 64 + s, rows, stride=8), :]
        sums = jnp.sum(part, axis=1, keepdims=True)
        for a in range(2):
            packed = total[a]
            for l in range(count):
                q = l + shift
                if q // 16 == a:
                    here = lane == row + (q % 16) * 8
                    packed = jnp.where(here, sums[l * 8 : l * 8 + 8], packed)
            total[a] = packed

    total[...] = jnp.zeros((2, 8, LANES), F32)
    sum_into(8, 0, 24)

    def w_copy(c):
        return pltpu.make_async_copy(w.at[:, :, c], wout.at[:, :, c], obs.at[c])

    for c in range(VIA):
        pass_on(1, c)

    @pl.loop(0, n2)
    def _(c):
        @pl.loop(1, 8)
        def _(o):
            z_forward(c, o).wait_send()

        for d in range(2):

            @pl.when(can_send[d])
            def _():
                y_own(c, d).wait_send()

    for o in range(1, 4):
        r_forward(o).wait_send()

    def wait_sends_back():
        @pl.loop(0, n2)
        def _(c):
            w_copy(c).wait()

            @pl.loop(1, 8)
            def _(o):
                z_back(c, o).wait_send()

            for d in range(2):

                @pl.when(jnp.logical_and(has_one[d], can_send[d]))
                def _():
                    y_relay(c, d).wait_send()

        for k in range(2):
            for c in range(VIA):
                for d in range(2):

                    @pl.when(is_via[d])
                    def _():
                        from_via(k, c, d).wait_send()

        for o in range(1, 4):
            r_back(o).wait_send()

    for o in range(1, 4):
        r_back(o).wait_recv()

    @pl.loop(0, n2)
    def _(c):
        @pl.loop(1, 8)
        def _(o):
            z_back(c, o).wait_recv()

        for d in range(2):
            wait_recv_when(has_two[d], y_relay(c, d))

        @pl.loop(0, nv)
        def _(n):
            for m in range(n1):
                skip = sf[m, c] * (far * yb[3, n, m, c] + far_low * yb[2, n, m, c])
                w[n, m, c] = (w[n, m, c] + rret[n, m, c]) + (zret[n, m, c] + skip)

        w_copy(c).start()
        gather_products(c, v, w, lambda j, i: (j * 8 + i, (16 + i) * 8 + j), False)
        gather_products(c, w, w, lambda j, i: {(8 + j) * 8 + i, (8 + i) * 8 + j}, True)

    sum_into(24, 8, 0)
    msg = jnp.concatenate([jnp.sum(total[a], axis=0, keepdims=True) for a in range(2)], axis=0)

    groups = ((u, x_peer), (z, z_peer), (y, y_peer))

    def ar_copy(g, o):
        me, peer = groups[g]
        return pltpu.make_async_remote_copy(
            arb.at[g, me], arb.at[g, me], ars.at[g, o], arr.at[g, o], device_id=peer(o)
        )

    for g in range(3):
        arb[g, groups[g][0]] = msg
        for i in range(1, 8):
            ar_copy(g, far_first(i)).start()
        if g == 0:
            wait_sends_back()
        else:
            for i in range(1, 8):
                ar_copy(g - 1, i).wait_send()
        for i in range(1, 8):
            ar_copy(g, i).wait_recv()
        msg = arb[g, 0]
        for t in range(1, 8):
            msg = msg + arb[g, t]

    msg = msg * (1.0 / float(16 * 8 * 4 * 32768))

    def mm(a, b):
        total = col(a, 0) * b[0:1, :]
        for k in range(1, 8):
            total = total + col(a, k) * b[k : k + 1, :]
        return total

    own = [jnp.where(lane % 8 == row, msg[a : a + 1, :], 0.0) for a in range(2)]
    own = jnp.concatenate(own, axis=0)
    high, low = halves(own)
    rest = ((own - high.astype(F32)) - low.astype(F32)).astype(BF16)
    parts = jnp.dot(
        jnp.concatenate([high, low, rest], axis=0),
        hot((LANES, LANES), lambda q: q // 8).astype(BF16),
        preferred_element_type=F32,
    )
    whole = parts[0:16] + (parts[16:32] + parts[32:48])
    overlap = whole[0:8]
    first_t = pltpu.roll(overlap, LANES - 8, axis=1)
    square = whole[8:16]
    first = pltpu.roll(square, LANES - 8, axis=1)
    both_t = 2.0 * first_t - mm(first_t, overlap)
    both = 2.0 * first - mm(overlap, first)
    gram = square - mm(both_t, first) - mm(first_t, both) + mm(mm(both_t, overlap), both)
    work = jnp.where(lane < 8, gram, 0.0)
    work = jnp.where(lane == row + 8, 1.0, work)
    work = jnp.where((lane >= 16) & (lane < 24), pltpu.roll(both_t, 16, axis=1), work)
    factor = jnp.zeros((8, LANES), F32)
    for k in range(8):
        prow = jnp.broadcast_to(work[k : k + 1, :], (8, LANES))
        pivot = col(prow, k)
        column = col(work, k)
        root = lax.rsqrt(pivot)
        factor = jnp.where((lane == k) & (row >= k), column * root, factor)
        below = work - (column * (root * root)) * prow
        work = jnp.where(row > k, below, jnp.where(row == k, work * root, work))
    pack[0] = work
    pack[1] = both
    pack[2] = factor

    for i in range(1, 8):
        ar_copy(2, i).wait_send()


def finish(vec, wfin, pack_hbm, out, alpha_hbm, lower_hbm, v, w, ob, pack, coef, small, sem):
    n2 = v.shape[2]

    def loads(c):
        return (
            pltpu.make_async_copy(vec.at[0, :, :, c], v.at[:, :, c], sem.at[0, c]),
            pltpu.make_async_copy(wfin.at[:, :, c], w.at[:, :, c], sem.at[1, c]),
        )

    first = pltpu.make_async_copy(pack_hbm, pack, sem.at[3, 0])
    first.start()
    for c in range(n2):
        for copy in loads(c):
            copy.start()
    first.wait()
    small[0] = pack[1, :, 0:8]
    small[1] = pack[2, :, 0:8]
    tiny = [
        pltpu.make_async_copy(small.at[0], alpha_hbm, sem.at[3, 1]),
        pltpu.make_async_copy(small.at[1], lower_hbm, sem.at[3, 2]),
    ]
    for copy in tiny:
        copy.start()
    work = pack[0]
    for j in range(8):
        coef[j * 8 : j * 8 + 8, :] = col(work, 8 + j)
        coef[64 + j * 8 : 72 + j * 8, :] = -col(work, 16 + j)

    def out_copy(c):
        return pltpu.make_async_copy(ob.at[:, :, c], out.at[0, :, :, c], sem.at[2, c])

    @pl.loop(0, n2)
    def _(c):
        for copy in loads(c):
            copy.wait()

        @pl.loop(0, 4)
        def _(k):
            m, h = k // 2, k % 2
            at = [pl.ds(pl.multiple_of(h * 256 + q * LANES, LANES), LANES) for q in range(2)]
            vs = [[v[j, m, c, :, at[q]] for q in range(2)] for j in range(8)]
            ws = [[w[j, m, c, :, at[q]] for q in range(2)] for j in range(8)]
            for i in range(8):
                total = None
                for base, xs, count in ((64, vs, 8), (0, ws, i + 1)):
                    for j in range(count):
                        factor = splat(coef, base + j * 8 + i)
                        terms = [factor * xs[j][q] for q in range(2)]
                        total = terms if total is None else [t + s for t, s in zip(total, terms)]
                for q in range(2):
                    ob[i, m, c, :, at[q]] = total[q]

        out_copy(c).start()

    @pl.loop(0, n2)
    def _(c):
        out_copy(c).wait()

    for copy in tiny:
        copy.wait()


def shards(*args):
    (vectors, previous, beta, potential, coriolis_fn, second_fn, rot_const, coupling, *mats) = args
    block = vectors.shape[1:]
    fn = potential.shape
    any_spec = pl.BlockSpec(memory_space=pltpu.HBM)
    vmem = pl.BlockSpec(memory_space=pltpu.VMEM)
    nv, n1, n2, n3, nr = block
    dma = pltpu.SemaphoreType.DMA
    scratch = [
        pltpu.VMEM(block, F32),
        pltpu.VMEM(block, F32),
        pltpu.VMEM(fn, F32),
        pltpu.VMEM(fn, F32),
        pltpu.VMEM(fn, F32),
        pltpu.VMEM(block, F32),
        pltpu.VMEM(block, F32),
        pltpu.VMEM(block, F32),
        pltpu.VMEM(block, F32),
        pltpu.VMEM((4, 2) + block[1:], F32),
        pltpu.VMEM((4, 2) + block[1:], F32),
        pltpu.VMEM(block, F32),
        pltpu.VMEM((4,) + block, F32),
        pltpu.VMEM((2 * n2, nv, n1, n3, nr), F32),
        pltpu.VMEM((8, 8), F32),
        pltpu.SMEM((16,), F32),
        pltpu.SMEM((2, 16), F32),
        pltpu.VMEM((16, 16), F32),
        pltpu.VMEM((16, 16), F32),
        *[pltpu.VMEM((8, 8), F32)] * 5,
        pltpu.VMEM((256, LANES), F32),
        pltpu.VMEM((256, LANES), F32),
        pltpu.VMEM((64, LANES), F32),
        pltpu.VMEM((8, 8, LANES), F32),
        pltpu.VMEM((8, nr), F32),
        pltpu.VMEM((nr, nr), BF16),
        pltpu.VMEM((nr, nr), BF16),
        pltpu.VMEM((256, 256), BF16),
        pltpu.VMEM((256, 256), BF16),
        pltpu.VMEM((256 * 8, LANES), F32),
        pltpu.VMEM((2, 8, LANES), F32),
        pltpu.VMEM((3, 8, 2, LANES), F32),
        dma((17,)),
        dma((n2, 8)),
        dma((n2, 8)),
        dma((n2, 8)),
        dma((n2, 8)),
        dma((4,)),
        dma((4,)),
        dma((4,)),
        dma((4,)),
        dma((2, n2)),
        dma((2, n2)),
        dma((2, n2)),
        dma((2, n2)),
        dma((2 * n2,)),
        dma((2 * n2,)),
        dma((3, 8)),
        dma((3, 8)),
        dma((n2,)),
    ]
    wfin, pack = pl.pallas_call(
        kernel,
        out_shape=(
            jax.ShapeDtypeStruct(block, F32),
            jax.ShapeDtypeStruct((3, nv, LANES), F32),
        ),
        in_specs=[any_spec] * 15,
        out_specs=(any_spec, vmem),
        scratch_shapes=scratch,
        compiler_params=pltpu.CompilerParams(
            collective_id=0, has_side_effects=True, vmem_limit_bytes=67043328
        ),
        name="lanczos",
    )(vectors, previous, potential, coriolis_fn, second_fn, beta, rot_const, coupling, *mats)
    return pl.pallas_call(
        finish,
        out_shape=(
            jax.ShapeDtypeStruct(vectors.shape, F32),
            jax.ShapeDtypeStruct((nv, nv), F32),
            jax.ShapeDtypeStruct((nv, nv), F32),
        ),
        in_specs=[any_spec] * 3,
        out_specs=(any_spec,) * 3,
        scratch_shapes=[
            pltpu.VMEM(block, F32),
            pltpu.VMEM(block, F32),
            pltpu.VMEM(block, F32),
            pltpu.VMEM((3, nv, LANES), F32),
            pltpu.VMEM((128, LANES), F32),
            pltpu.VMEM((2, nv, nv), F32),
            dma((4, n2)),
        ],
        compiler_params=pltpu.CompilerParams(vmem_limit_bytes=67043328),
        name="basis",
    )(vectors, wfin, pack)


def solution(mesh):
    split = P("ka", None, "mode", "row", None, None)
    fn = P("mode", "row", None, None)
    return jax.shard_map(
        shards,
        mesh=mesh,
        in_specs=(split, split, P(), fn, fn, fn) + (P(),) * 9,
        out_specs=(split, P(), P()),
        check_vma=False,
    )
```

```python
import jax
import jax.numpy as jnp
from jax import lax
from jax.experimental import pallas as pl
from jax.experimental.pallas import tpu as pltpu
from jax.sharding import PartitionSpec as P

F32 = jnp.float32
BF16 = jnp.bfloat16
HI = lax.Precision.HIGHEST
LANES = 128
VIA = 2
NT = (((1,), (1,)), ((), ()))


def exact(a, b):
    return jnp.dot(a, b, precision=HI, preferred_element_type=F32)


def exact_nt(a, b):
    return lax.dot_general(a, b, NT, precision=HI, preferred_element_type=F32)


def iota(shape, axis):
    return lax.broadcasted_iota(jnp.int32, shape, axis)


def hot(shape, of):
    return (of(iota(shape, 0)) == iota(shape, 1)).astype(F32)


def halves(x):
    high = x.astype(BF16)
    return high, (x - high.astype(F32)).astype(BF16)


def three_pass(x, high, low):
    xh, xl = halves(x)

    def dot(a, b):
        return jnp.dot(a, b, preferred_element_type=F32)

    return dot(xh, high) + (dot(xl, high) + dot(xh, low))


def col(a, k):
    return jnp.broadcast_to(a[:, k : k + 1], (8, LANES))


def splat(table, row):
    return table[pl.ds(row, 8, stride=0), :]


def far_first(i):
    return 4 + (i // 2) * (1 - 2 * (i % 2))


def lane_block(q):
    return pl.ds(q * LANES, LANES)


def spread(rows, left, right, table):
    n = left.shape[1]
    picked = left * (iota((rows, n), 0) % n == iota((rows, n), 1)).astype(F32)
    table[...] = exact(picked, jnp.ones((n, LANES), F32))


def kernel(
    vec,
    prev,
    pot,
    cor,
    sec,
    beta_hbm,
    rot_hbm,
    coupling_hbm,
    one_hbm,
    two_hbm,
    three_hbm,
    four_hbm,
    five_hbm,
    six_hbm,
    deriv_hbm,
    wout,
    pack,
    v,
    pv,
    po,
    cf,
    sf,
    w,
    zin,
    zout,
    zret,
    rin,
    rout,
    rret,
    yb,
    via,
    beta,
    rot,
    coupling,
    kin_one,
    kin_two,
    kin_three,
    kin_four,
    kin_five,
    kin_six,
    deriv,
    tab1,
    tab2,
    tabb,
    tab3,
    rows4,
    tkh,
    tkl,
    twh,
    twl,
    acc,
    total,
    arb,
    loc,
    zfs,
    zfr,
    zrs,
    zrr,
    rfs,
    rfr,
    rrs,
    rrr,
    yfs,
    yfr,
    yrs,
    yrr,
    vr,
    vs,
    ars,
    arr,
    obs,
):
    ka = lax.axis_index("ka")
    z = lax.axis_index("mode")
    r = lax.axis_index("row")
    x_hi = ka // 8
    y = ka % 8
    nv, n1, n2 = v.shape[0], v.shape[1], v.shape[2]
    u = x_hi * 4 + r
    nblocks = 16

    def local_copy(i, src, dst):
        return pltpu.make_async_copy(src, dst, loc.at[i])

    locals_ = [
        local_copy(0, vec.at[0], v),
        local_copy(1, prev.at[0], pv),
        local_copy(2, pot, po),
        local_copy(3, cor, cf),
        local_copy(4, sec, sf),
        local_copy(5, vec.at[0, z], zin.at[z]),
        local_copy(6, vec.at[0, pl.ds(2 * r, 2)], rin.at[r]),
    ]
    small = [
        (beta_hbm, beta),
        (rot_hbm, rot),
        (coupling_hbm, coupling),
        (one_hbm, kin_one),
        (two_hbm, kin_two),
        (three_hbm, kin_three),
        (four_hbm, kin_four),
        (five_hbm, kin_five),
        (six_hbm, kin_six),
        (deriv_hbm, deriv),
    ]
    small = [local_copy(7 + i, *pair) for i, pair in enumerate(small)]

    def z_peer(o):
        return {"mode": (z + o) % 8}

    def y_peer(o):
        return {"ka": x_hi * 8 + (y + o) % 8}

    def x_peer(o):
        t = (u + o) % 8
        return {"ka": (t // 4) * 8 + y, "row": t % 4}

    def z_forward(c, o):
        t = (z + o) % 8
        return pltpu.make_async_remote_copy(
            vec.at[0, t, :, c],
            zin.at[z, :, c],
            zfs.at[c, o],
            zfr.at[c, o],
            device_id=z_peer(o),
        )

    def z_back(c, o):
        t = (z + o) % 8
        return pltpu.make_async_remote_copy(
            zout.at[t, :, c],
            zret.at[z, :, c],
            zrs.at[c, o],
            zrr.at[c, o],
            device_id=z_peer(o),
        )

    def r_forward(o):
        t = (r + o) % 4
        return pltpu.make_async_remote_copy(
            vec.at[0, pl.ds(2 * t, 2)],
            rin.at[r],
            rfs.at[o],
            rfr.at[o],
            device_id={"row": t},
        )

    def r_back(o):
        t = (r + o) % 4
        return pltpu.make_async_remote_copy(
            rout.at[t],
            rret.at[pl.ds(2 * r, 2)],
            rrs.at[o],
            rrr.at[o],
            device_id={"row": t},
        )

    def y_own(c, d):
        return pltpu.make_async_remote_copy(
            vec.at[0, :, :, c],
            yb.at[d, :, :, c],
            yfs.at[d, c],
            yfr.at[d, c],
            device_id={"ka": ka + 1 - 2 * d},
        )

    def y_relay(c, d):
        return pltpu.make_async_remote_copy(
            yb.at[d, :, :, c],
            yb.at[d + 2, :, :, c],
            yrs.at[d, c],
            yrr.at[d, c],
            device_id={"ka": ka + 1 - 2 * d},
        )

    def to_via(k, c, d):
        src = vec.at[0, :, :, c] if k == 0 else yb.at[d, :, :, c]
        return pltpu.make_async_remote_copy(
            src,
            via.at[k * n2 + c],
            (yfs, yrs)[k].at[d, c],
            vr.at[k * n2 + c],
            device_id={"ka": 15 - 15 * d},
        )

    def from_via(k, c, d):
        return pltpu.make_async_remote_copy(
            via.at[k * n2 + c],
            yb.at[d + 2 * k, :, :, c],
            vs.at[k * n2 + c],
            (yfr, yrr)[k].at[d, c],
            device_id={"ka": 8 - d},
        )

    at_edge = (ka == 7, ka == 8)
    is_via = (ka == 15, ka == 0)

    def send_on(k, c, d, cond):
        detour = jnp.logical_and(at_edge[d], c < VIA)

        @pl.when(jnp.logical_and(cond, detour))
        def _():
            to_via(k, c, d).start()

        @pl.when(jnp.logical_and(cond, jnp.logical_not(detour)))
        def _():
            (y_own, y_relay)[k](c, d).start()

    def pass_on(k, c):
        for d in range(2):

            @pl.when(is_via[d])
            def _():
                to_via(k, c, d).wait_recv()
                from_via(k, c, d).start()

    can_send = (ka < nblocks - 1, ka > 0)
    has_one = (ka > 0, ka < nblocks - 1)
    has_two = (ka > 1, ka < nblocks - 2)

    barrier = pltpu.get_barrier_semaphore()
    edge = jnp.logical_or(ka == 7, ka == 8)

    for i in range(1, 8):
        for peer in (z_peer, y_peer, x_peer):
            pl.semaphore_signal(barrier, inc=1, device_id=peer(far_first(i)))

    @pl.when(edge)
    def _():
        pl.semaphore_signal(barrier, inc=1, device_id={"ka": 15 - ka})

    pl.semaphore_wait(barrier, 21 + edge.astype(jnp.int32))

    def start_chunk(c):
        @pl.loop(1, 8)
        def _(o):
            z_forward(c, far_first(o)).start()

        for d in range(2):

            send_on(0, c, d, can_send[d])

    for o in range(1, 4):
        r_forward(o).start()
    start_chunk(0)
    for copy in small + locals_:
        copy.start()
    for c in range(1, n2):
        start_chunk(c)

    for d in range(2):

        @pl.when(jnp.logical_not(has_one[d]))
        def _():
            yb[d] = jnp.zeros(yb.shape[1:], F32)

        @pl.when(jnp.logical_not(has_two[d]))
        def _():
            yb[d + 2] = jnp.zeros(yb.shape[1:], F32)

    for copy in small:
        copy.wait()

    def table_of(matrix, table):
        n = matrix.shape[0]
        pick = hot((n * n, n), lambda q: q // n)
        both = 0.5 * (exact(pick, matrix[...]) + exact_nt(pick, matrix[...]))
        spread(n * n, both, None, table)

    table_of(kin_one, tab1)
    table_of(kin_two, tab2)
    spread(64, exact(hot((64, 8), lambda q: q // 8), beta[...]), None, tabb)
    eye8 = hot((8, 8), lambda q: q)
    sym3 = 0.5 * (kin_three[...] + exact_nt(eye8, kin_three[...]))
    for s in range(8):
        mask = (iota((8, 8), 0) + (8 - s)) % 8 == iota((8, 8), 1)
        tab3[s] = exact(jnp.where(mask, sym3, 0.0), jnp.ones((8, LANES), F32))

    def expand(pick, matrix, pick_t):
        both = 0.5 * (exact(pick, matrix[...]) + exact_nt(pick, matrix[...]))
        return exact_nt(both, pick_t)

    rows4[...] = expand(eye8, kin_four, hot((512, 8), lambda q: q // 64))
    e5 = expand(hot((64, 8), lambda q: q // 8), kin_five, hot((512, 8), lambda q: (q // 8) % 8))
    e6 = expand(hot((64, 8), lambda q: q % 8), kin_six, hot((512, 8), lambda q: q % 8))
    qi = iota((64, 512), 0)
    pi = iota((64, 512), 1)
    m56 = jnp.where(pi % 8 == qi % 8, e5, 0.0) + jnp.where((pi // 8) % 8 == qi // 8, e6, 0.0)
    diag64 = pi % 64 == qi
    for k in range(8):
        block = jnp.where(diag64, rows4[k : k + 1, :], 0.0) + jnp.where(pi // 64 == k, m56, 0.0)
        high, low = halves(block)
        tkh[k * 64 : (k + 1) * 64, :] = high
        tkl[k * 64 : (k + 1) * 64, :] = low
    pick6 = hot((256, 8), lambda q: q % 8)
    turned = 0.5 * (exact_nt(pick6, deriv[...]) - exact(pick6, deriv[...]))
    full = jnp.where(iota((256, 256), 0) // 8 == iota((256, 256), 1) // 8, exact_nt(turned, pick6), 0.0)
    high, low = halves(full)
    twh[...] = high
    twl[...] = low
    acc[...] = jnp.zeros(acc.shape, F32)

    level = (ka - nblocks // 2).astype(F32)
    shift = rot[ka] * level * level
    near = coupling[0, ka]
    near_low = coupling[0, jnp.maximum(ka - 1, 0)]
    far = coupling[1, ka]
    far_low = coupling[1, jnp.maximum(ka - 2, 0)]

    def mix16(load, store, table):
        xs = [[load(b, q) for q in range(2)] for b in range(16)]
        for a in range(16):
            total = None
            for b in range(16):
                k = splat(table, a * 16 + b)
                terms = [k * xs[b][q] for q in range(2)]
                total = terms if total is None else [t + s for t, s in zip(total, terms)]
            for q in range(2):
                store(a, q, total[q])

    def first_mode(c):
        @pl.loop(0, 2)
        def _(h):
            def at(q):
                return pl.ds(pl.multiple_of(h * 256 + q * LANES, LANES), LANES)

            def load(b, q):
                return zin[b // 2, b % 2, c, :, at(q)]

            def store(a, q, val):
                zout[a // 2, a % 2, c, :, at(q)] = val

            mix16(load, store, tab1)

        zret[z, :, c] = zout[z, :, c]

    def second_mode():
        @pl.loop(0, 8)
        def _(k):
            n, m, h = k // 4, (k // 2) % 2, k % 2

            def at(q):
                return pl.ds(pl.multiple_of(h * 256 + q * LANES, LANES), LANES)

            def load(b, q):
                return rin[b // 4, n, m, b % 4, :, at(q)]

            def store(a, q, val):
                rout[a // 4, n, m, a % 4, :, at(q)] = val

            mix16(load, store, tab2)

        rret[pl.ds(2 * r, 2)] = rout[r]

    def gather_products(c, left, right, spot_of, triangle):
        for g in range(4):
            pairs = [(j, i) for i in (2 * g, 2 * g + 1) for j in range(8) if j <= i or not triangle]
            sums = {}
            for m in range(n1):
                for q in range(4):
                    ls = [left[j, m, c, :, lane_block(q)] for j in range(8)]
                    rs = [right[i, m, c, :, lane_block(q)] for i in (2 * g, 2 * g + 1)]
                    for j, i in pairs:
                        term = ls[j] * rs[i - 2 * g]
                        sums[j, i] = term if (j, i) not in sums else sums[j, i] + term
            for j, i in pairs:
                spot = spot_of(j, i)
                acc[spot * 8 : spot * 8 + 8, :] += sums[j, i]

    def local_terms(c):
        x = v[:, :, c].reshape(nv * n1 * 8, 512)
        w[:, :, c] = three_pass(x, tkh[...], tkl[...]).reshape(nv, n1, 8, 512)

        @pl.loop(0, 4)
        def _(k):
            m, h = k // 2, k % 2
            for q in range(2):
                at = pl.ds(pl.multiple_of(h * 256 + q * LANES, LANES), LANES)
                old = [pv[j, m, c, :, at] for j in range(8)]
                diag = po[m, c, :, at] + shift
                for i in range(8):
                    xi = v[i, m, c, :, at]
                    total = w[i, m, c, :, at] + (diag + tab3[0]) * xi
                    for s in range(1, 8):
                        total = total + tab3[s] * pltpu.roll(xi, s, axis=0)
                    taken = splat(tabb, i * 8) * old[0]
                    for j in range(1, 8):
                        taken = taken + splat(tabb, i * 8 + j) * old[j]
                    w[i, m, c, :, at] = total - taken

        gather_products(c, v, v, lambda j, i: (16 + j) * 8 + i, True)

    def turn(x):
        flat = x.reshape(nv * n1 * 8, 512)
        parts = [three_pass(flat[:, h * 256 : h * 256 + 256], twh[...], twl[...]) for h in range(2)]
        return jnp.concatenate(parts, axis=1).reshape(x.shape)

    def near_terms(c):
        fn = cf[:, c][None]
        above = turn(yb[1, :, :, c])
        w[:, :, c] += (near * fn) * above
        below = turn(fn * yb[0, :, :, c])
        w[:, :, c] -= near_low * below

    def wait_recv_when(cond, copy):
        @pl.when(cond)
        def _():
            copy.wait_recv()

    for copy in locals_:
        copy.wait()

    @pl.loop(0, n2)
    def _(c):
        for d in range(2):
            wait_recv_when(has_one[d], y_own(c, d))

            send_on(1, c, d, jnp.logical_and(has_one[d], can_send[d]))

        @pl.when(c < VIA)
        def _():
            pass_on(0, c)

        @pl.loop(1, 8)
        def _(o):
            z_forward(c, o).wait_recv()

        first_mode(c)

        @pl.loop(1, 8)
        def _(o):
            z_back(c, far_first(o)).start()

        @pl.when(c == 1)
        def _():
            for o in range(1, 4):
                r_forward(o).wait_recv()
            second_mode()
            for o in range(1, 4):
                r_back(o).start()

        local_terms(c)
        near_terms(c)

    lane = iota((8, LANES), 1)
    row = iota((8, LANES), 0)

    def sum_into(count, shift, at):
        rows = count * 8
        part = acc[pl.ds(at * 64, rows, stride=8), :]
        for s in range(1, 8):
            part = part + acc[pl.ds(at * 64 + s, rows, stride=8), :]
        sums = jnp.sum(part, axis=1, keepdims=True)
        for a in range(2):
            packed = total[a]
            for l in range(count):
                q = l + shift
                if q // 16 == a:
                    here = lane == row + (q % 16) * 8
                    packed = jnp.where(here, sums[l * 8 : l * 8 + 8], packed)
            total[a] = packed

    total[...] = jnp.zeros((2, 8, LANES), F32)
    sum_into(8, 0, 16)

    def w_copy(c):
        return pltpu.make_async_copy(w.at[:, :, c], wout.at[:, :, c], obs.at[c])

    for c in range(VIA):
        pass_on(1, c)

    @pl.loop(0, n2)
    def _(c):
        @pl.loop(1, 8)
        def _(o):
            z_forward(c, o).wait_send()

        for d in range(2):

            @pl.when(can_send[d])
            def _():
                y_own(c, d).wait_send()

    for o in range(1, 4):
        r_forward(o).wait_send()

    def wait_sends_back():
        @pl.loop(0, n2)
        def _(c):
            w_copy(c).wait()

            @pl.loop(1, 8)
            def _(o):
                z_back(c, o).wait_send()

            for d in range(2):

                @pl.when(jnp.logical_and(has_one[d], can_send[d]))
                def _():
                    y_relay(c, d).wait_send()

        for k in range(2):
            for c in range(VIA):
                for d in range(2):

                    @pl.when(is_via[d])
                    def _():
                        from_via(k, c, d).wait_send()

        for o in range(1, 4):
            r_back(o).wait_send()

    for o in range(1, 4):
        r_back(o).wait_recv()

    @pl.loop(0, n2)
    def _(c):
        @pl.loop(1, 8)
        def _(o):
            z_back(c, o).wait_recv()

        for d in range(2):
            wait_recv_when(has_two[d], y_relay(c, d))

        @pl.loop(0, nv)
        def _(n):
            for m in range(n1):
                skip = sf[m, c] * (far * yb[3, n, m, c] + far_low * yb[2, n, m, c])
                w[n, m, c] = (w[n, m, c] + rret[n, m, c]) + (zret[n, m, c] + skip)

        w_copy(c).start()
        gather_products(c, v, w, lambda j, i: j * 8 + i, False)
        gather_products(c, w, w, lambda j, i: (8 + j) * 8 + i, True)

    sum_into(16, 8, 0)
    msg = jnp.concatenate([jnp.sum(total[a], axis=0, keepdims=True) for a in range(2)], axis=0)

    groups = ((u, x_peer), (z, z_peer), (y, y_peer))

    def ar_copy(g, o):
        me, peer = groups[g]
        return pltpu.make_async_remote_copy(
            arb.at[g, me], arb.at[g, me], ars.at[g, o], arr.at[g, o], device_id=peer(o)
        )

    for g in range(3):
        arb[g, groups[g][0]] = msg
        for i in range(1, 8):
            ar_copy(g, far_first(i)).start()
        if g == 1:
            wait_sends_back()
        if g > 0:
            for i in range(1, 8):
                ar_copy(g - 1, i).wait_send()
        for i in range(1, 8):
            ar_copy(g, i).wait_recv()
        msg = arb[g, 0]
        for t in range(1, 8):
            msg = msg + arb[g, t]

    msg = msg * (1.0 / float(16 * 8 * 4 * 32768))

    def mm(a, b):
        total = col(a, 0) * b[0:1, :]
        for k in range(1, 8):
            total = total + col(a, k) * b[k : k + 1, :]
        return total

    def select(own, column):
        high, low = halves(own)
        rest = ((own - high.astype(F32)) - low.astype(F32)).astype(BF16)
        parts = jnp.dot(
            jnp.concatenate([high, low, rest], axis=0),
            hot((LANES, LANES), column).astype(BF16),
            preferred_element_type=F32,
        )
        n = own.shape[0]
        return parts[0:n] + (parts[n : 2 * n] + parts[2 * n : 3 * n])

    rows_of = [msg[a : a + 1, :] for a in range(2)]
    within, block = lane % 8, lane // 8
    plain = select(
        jnp.concatenate([jnp.where(within == row, x, 0.0) for x in rows_of], axis=0),
        lambda q: q // 8,
    )
    turned_over = select(
        jnp.concatenate(
            [
                jnp.where(block == row, rows_of[0], 0.0),
                jnp.where(block == row + 8, rows_of[0], 0.0),
                jnp.where(block == row, rows_of[1], 0.0),
            ],
            axis=0,
        ),
        lambda q: q % 8,
    )
    first_t = pltpu.roll(plain[0:8], LANES - 8, axis=1)
    first = turned_over[8:16]
    overlap = jnp.where(lane <= row, plain[0:8], turned_over[0:8])
    square = jnp.where(lane <= row, plain[8:16], turned_over[16:24])
    both_t = 2.0 * first_t - mm(first_t, overlap)
    both = 2.0 * first - mm(overlap, first)
    gram = square - mm(both_t, first) - mm(first_t, both) + mm(mm(both_t, overlap), both)
    work = jnp.where(lane < 8, gram, 0.0)
    work = jnp.where(lane == row + 8, 1.0, work)
    work = jnp.where((lane >= 16) & (lane < 24), pltpu.roll(both_t, 16, axis=1), work)
    factor = jnp.zeros((8, LANES), F32)
    for k in range(8):
        prow = jnp.broadcast_to(work[k : k + 1, :], (8, LANES))
        pivot = col(prow, k)
        column = col(work, k)
        root = lax.rsqrt(pivot)
        factor = jnp.where((lane == k) & (row >= k), column * root, factor)
        below = work - (column * (root * root)) * prow
        work = jnp.where(row > k, below, jnp.where(row == k, work * root, work))
    pack[0] = work
    pack[1] = both
    pack[2] = factor

    for i in range(1, 8):
        ar_copy(2, i).wait_send()


def finish(vec, wfin, pack_hbm, out, alpha_hbm, lower_hbm, v, w, ob, pack, coef, small, sem):
    n2 = v.shape[2]

    def loads(c):
        return (
            pltpu.make_async_copy(vec.at[0, :, :, c], v.at[:, :, c], sem.at[0, c]),
            pltpu.make_async_copy(wfin.at[:, :, c], w.at[:, :, c], sem.at[1, c]),
        )

    first = pltpu.make_async_copy(pack_hbm, pack, sem.at[3, 0])
    first.start()
    for c in range(n2):
        for copy in loads(c):
            copy.start()
    first.wait()
    small[0] = pack[1, :, 0:8]
    small[1] = pack[2, :, 0:8]
    tiny = [
        pltpu.make_async_copy(small.at[0], alpha_hbm, sem.at[3, 1]),
        pltpu.make_async_copy(small.at[1], lower_hbm, sem.at[3, 2]),
    ]
    for copy in tiny:
        copy.start()
    work = pack[0]
    for j in range(8):
        coef[j * 8 : j * 8 + 8, :] = col(work, 8 + j)
        coef[64 + j * 8 : 72 + j * 8, :] = -col(work, 16 + j)

    def out_copy(c):
        return pltpu.make_async_copy(ob.at[:, :, c], out.at[0, :, :, c], sem.at[2, c])

    @pl.loop(0, n2)
    def _(c):
        for copy in loads(c):
            copy.wait()

        @pl.loop(0, 4)
        def _(k):
            m, h = k // 2, k % 2
            at = [pl.ds(pl.multiple_of(h * 256 + q * LANES, LANES), LANES) for q in range(2)]
            vs = [[v[j, m, c, :, at[q]] for q in range(2)] for j in range(8)]
            ws = [[w[j, m, c, :, at[q]] for q in range(2)] for j in range(8)]
            for i in range(8):
                total = None
                for base, xs, count in ((64, vs, 8), (0, ws, i + 1)):
                    for j in range(count):
                        factor = splat(coef, base + j * 8 + i)
                        terms = [factor * xs[j][q] for q in range(2)]
                        total = terms if total is None else [t + s for t, s in zip(total, terms)]
                for q in range(2):
                    ob[i, m, c, :, at[q]] = total[q]

        out_copy(c).start()

    @pl.loop(0, n2)
    def _(c):
        out_copy(c).wait()

    for copy in tiny:
        copy.wait()


def shards(*args):
    (vectors, previous, beta, potential, coriolis_fn, second_fn, rot_const, coupling, *mats) = args
    block = vectors.shape[1:]
    fn = potential.shape
    any_spec = pl.BlockSpec(memory_space=pltpu.HBM)
    vmem = pl.BlockSpec(memory_space=pltpu.VMEM)
    nv, n1, n2, n3, nr = block
    dma = pltpu.SemaphoreType.DMA
    scratch = [
        pltpu.VMEM(block, F32),
        pltpu.VMEM(block, F32),
        pltpu.VMEM(fn, F32),
        pltpu.VMEM(fn, F32),
        pltpu.VMEM(fn, F32),
        pltpu.VMEM(block, F32),
        pltpu.VMEM(block, F32),
        pltpu.VMEM(block, F32),
        pltpu.VMEM(block, F32),
        pltpu.VMEM((4, 2) + block[1:], F32),
        pltpu.VMEM((4, 2) + block[1:], F32),
        pltpu.VMEM(block, F32),
        pltpu.VMEM((4,) + block, F32),
        pltpu.VMEM((2 * n2, nv, n1, n3, nr), F32),
        pltpu.VMEM((8, 8), F32),
        pltpu.SMEM((16,), F32),
        pltpu.SMEM((2, 16), F32),
        pltpu.VMEM((16, 16), F32),
        pltpu.VMEM((16, 16), F32),
        *[pltpu.VMEM((8, 8), F32)] * 5,
        pltpu.VMEM((256, LANES), F32),
        pltpu.VMEM((256, LANES), F32),
        pltpu.VMEM((64, LANES), F32),
        pltpu.VMEM((8, 8, LANES), F32),
        pltpu.VMEM((8, nr), F32),
        pltpu.VMEM((nr, nr), BF16),
        pltpu.VMEM((nr, nr), BF16),
        pltpu.VMEM((256, 256), BF16),
        pltpu.VMEM((256, 256), BF16),
        pltpu.VMEM((192 * 8, LANES), F32),
        pltpu.VMEM((2, 8, LANES), F32),
        pltpu.VMEM((3, 8, 2, LANES), F32),
        dma((17,)),
        dma((n2, 8)),
        dma((n2, 8)),
        dma((n2, 8)),
        dma((n2, 8)),
        dma((4,)),
        dma((4,)),
        dma((4,)),
        dma((4,)),
        dma((2, n2)),
        dma((2, n2)),
        dma((2, n2)),
        dma((2, n2)),
        dma((2 * n2,)),
        dma((2 * n2,)),
        dma((3, 8)),
        dma((3, 8)),
        dma((n2,)),
    ]
    wfin, pack = pl.pallas_call(
        kernel,
        out_shape=(
            jax.ShapeDtypeStruct(block, F32),
            jax.ShapeDtypeStruct((3, nv, LANES), F32),
        ),
        in_specs=[any_spec] * 15,
        out_specs=(any_spec, vmem),
        scratch_shapes=scratch,
        compiler_params=pltpu.CompilerParams(
            collective_id=0, has_side_effects=True, vmem_limit_bytes=67043328
        ),
        name="lanczos",
    )(vectors, previous, potential, coriolis_fn, second_fn, beta, rot_const, coupling, *mats)
    return pl.pallas_call(
        finish,
        out_shape=(
            jax.ShapeDtypeStruct(vectors.shape, F32),
            jax.ShapeDtypeStruct((nv, nv), F32),
            jax.ShapeDtypeStruct((nv, nv), F32),
        ),
        in_specs=[any_spec] * 3,
        out_specs=(any_spec,) * 3,
        scratch_shapes=[
            pltpu.VMEM(block, F32),
            pltpu.VMEM(block, F32),
            pltpu.VMEM(block, F32),
            pltpu.VMEM((3, nv, LANES), F32),
            pltpu.VMEM((128, LANES), F32),
            pltpu.VMEM((2, nv, nv), F32),
            dma((4, n2)),
        ],
        compiler_params=pltpu.CompilerParams(vmem_limit_bytes=67043328),
        name="basis",
    )(vectors, wfin, pack)


def solution(mesh):
    split = P("ka", None, "mode", "row", None, None)
    fn = P("mode", "row", None, None)
    return jax.shard_map(
        shards,
        mesh=mesh,
        in_specs=(split, split, P(), fn, fn, fn) + (P(),) * 9,
        out_specs=(split, P(), P()),
        check_vma=False,
    )
```

```python
import jax
import jax.numpy as jnp
from jax import lax
from jax.experimental import pallas as pl
from jax.experimental.pallas import tpu as pltpu
from jax.sharding import PartitionSpec as P

F32 = jnp.float32
BF16 = jnp.bfloat16
HI = lax.Precision.HIGHEST
LANES = 128
VIA = 2
NT = (((1,), (1,)), ((), ()))


def exact(a, b):
    return jnp.dot(a, b, precision=HI, preferred_element_type=F32)


def exact_nt(a, b):
    return lax.dot_general(a, b, NT, precision=HI, preferred_element_type=F32)


def iota(shape, axis):
    return lax.broadcasted_iota(jnp.int32, shape, axis)


def hot(shape, of):
    return (of(iota(shape, 0)) == iota(shape, 1)).astype(F32)


def halves(x):
    high = x.astype(BF16)
    return high, (x - high.astype(F32)).astype(BF16)


def three_pass(x, high, low):
    xh, xl = halves(x)

    def dot(a, b):
        return jnp.dot(a, b, preferred_element_type=F32)

    return dot(xh, high) + (dot(xl, high) + dot(xh, low))


def col(a, k):
    return jnp.broadcast_to(a[:, k : k + 1], (8, LANES))


def splat(table, row):
    return table[pl.ds(row, 8, stride=0), :]


def far_first(i):
    return 4 + (i // 2) * (1 - 2 * (i % 2))


def lane_block(q):
    return pl.ds(q * LANES, LANES)


def spread(rows, left, right, table):
    n = left.shape[1]
    picked = left * (iota((rows, n), 0) % n == iota((rows, n), 1)).astype(F32)
    table[...] = exact(picked, jnp.ones((n, LANES), F32))


def kernel(
    vec,
    prev,
    pot,
    cor,
    sec,
    beta_hbm,
    rot_hbm,
    coupling_hbm,
    one_hbm,
    two_hbm,
    three_hbm,
    four_hbm,
    five_hbm,
    six_hbm,
    deriv_hbm,
    wout,
    pack,
    v,
    pv,
    po,
    cf,
    sf,
    w,
    zin,
    zout,
    zret,
    rin,
    rout,
    rret,
    yb,
    via,
    beta,
    rot,
    coupling,
    kin_one,
    kin_two,
    kin_three,
    kin_four,
    kin_five,
    kin_six,
    deriv,
    tab1,
    tab2,
    tabb,
    tab3,
    rows4,
    tkh,
    tkl,
    twh,
    twl,
    acc,
    total,
    arb,
    loc,
    zfs,
    zfr,
    zrs,
    zrr,
    rfs,
    rfr,
    rrs,
    rrr,
    yfs,
    yfr,
    yrs,
    yrr,
    vr,
    vs,
    ars,
    arr,
    obs,
):
    ka = lax.axis_index("ka")
    z = lax.axis_index("mode")
    r = lax.axis_index("row")
    x_hi = ka // 8
    y = ka % 8
    nv, n1, n2 = v.shape[0], v.shape[1], v.shape[2]
    u = x_hi * 4 + r
    nblocks = 16

    def local_copy(i, src, dst):
        return pltpu.make_async_copy(src, dst, loc.at[i])

    locals_ = [
        local_copy(0, vec.at[0], v),
        local_copy(1, prev.at[0], pv),
        local_copy(2, pot, po),
        local_copy(3, cor, cf),
        local_copy(4, sec, sf),
        local_copy(5, vec.at[0, z], zin.at[z]),
        local_copy(6, vec.at[0, pl.ds(2 * r, 2)], rin.at[r]),
    ]
    small = [
        (beta_hbm, beta),
        (rot_hbm, rot),
        (coupling_hbm, coupling),
        (one_hbm, kin_one),
        (two_hbm, kin_two),
        (three_hbm, kin_three),
        (four_hbm, kin_four),
        (five_hbm, kin_five),
        (six_hbm, kin_six),
        (deriv_hbm, deriv),
    ]
    small = [local_copy(7 + i, *pair) for i, pair in enumerate(small)]

    def z_peer(o):
        return {"mode": (z + o) % 8}

    def y_peer(o):
        return {"ka": x_hi * 8 + (y + o) % 8}

    def x_peer(o):
        t = (u + o) % 8
        return {"ka": (t // 4) * 8 + y, "row": t % 4}

    def z_forward(c, o):
        t = (z + o) % 8
        return pltpu.make_async_remote_copy(
            vec.at[0, t, :, c],
            zin.at[z, :, c],
            zfs.at[c, o],
            zfr.at[c, o],
            device_id=z_peer(o),
        )

    def z_back(c, o):
        t = (z + o) % 8
        return pltpu.make_async_remote_copy(
            zout.at[t, :, c],
            zret.at[z, :, c],
            zrs.at[c, o],
            zrr.at[c, o],
            device_id=z_peer(o),
        )

    def r_forward(o):
        t = (r + o) % 4
        return pltpu.make_async_remote_copy(
            vec.at[0, pl.ds(2 * t, 2)],
            rin.at[r],
            rfs.at[o],
            rfr.at[o],
            device_id={"row": t},
        )

    def r_back(o):
        t = (r + o) % 4
        return pltpu.make_async_remote_copy(
            rout.at[t],
            rret.at[pl.ds(2 * r, 2)],
            rrs.at[o],
            rrr.at[o],
            device_id={"row": t},
        )

    def y_own(c, d):
        return pltpu.make_async_remote_copy(
            vec.at[0, :, :, c],
            yb.at[d, :, :, c],
            yfs.at[d, c],
            yfr.at[d, c],
            device_id={"ka": ka + 1 - 2 * d},
        )

    def y_relay(c, d):
        return pltpu.make_async_remote_copy(
            yb.at[d, :, :, c],
            yb.at[d + 2, :, :, c],
            yrs.at[d, c],
            yrr.at[d, c],
            device_id={"ka": ka + 1 - 2 * d},
        )

    def to_via(k, c, d):
        src = vec.at[0, :, :, c] if k == 0 else yb.at[d, :, :, c]
        return pltpu.make_async_remote_copy(
            src,
            via.at[k * n2 + c],
            (yfs, yrs)[k].at[d, c],
            vr.at[k * n2 + c],
            device_id={"ka": 15 - 15 * d},
        )

    def from_via(k, c, d):
        return pltpu.make_async_remote_copy(
            via.at[k * n2 + c],
            yb.at[d + 2 * k, :, :, c],
            vs.at[k * n2 + c],
            (yfr, yrr)[k].at[d, c],
            device_id={"ka": 8 - d},
        )

    at_edge = (ka == 7, ka == 8)
    is_via = (ka == 15, ka == 0)

    def send_on(k, c, d, cond):
        detour = jnp.logical_and(at_edge[d], c < VIA)

        @pl.when(jnp.logical_and(cond, detour))
        def _():
            to_via(k, c, d).start()

        @pl.when(jnp.logical_and(cond, jnp.logical_not(detour)))
        def _():
            (y_own, y_relay)[k](c, d).start()

    def pass_on(k, c):
        for d in range(2):

            @pl.when(is_via[d])
            def _():
                to_via(k, c, d).wait_recv()
                from_via(k, c, d).start()

    can_send = (ka < nblocks - 1, ka > 0)
    has_one = (ka > 0, ka < nblocks - 1)
    has_two = (ka > 1, ka < nblocks - 2)

    barrier = pltpu.get_barrier_semaphore()
    edge = jnp.logical_or(ka == 7, ka == 8)

    for i in range(1, 8):
        for peer in (z_peer, y_peer, x_peer):
            pl.semaphore_signal(barrier, inc=1, device_id=peer(far_first(i)))

    @pl.when(edge)
    def _():
        pl.semaphore_signal(barrier, inc=1, device_id={"ka": 15 - ka})

    pl.semaphore_wait(barrier, 21 + edge.astype(jnp.int32))

    def start_chunk(c):
        @pl.loop(1, 8)
        def _(o):
            z_forward(c, far_first(o)).start()

        for d in range(2):

            send_on(0, c, d, can_send[d])

    for o in range(1, 4):
        r_forward(o).start()
    for d in range(2):
        send_on(0, 0, d, can_send[d])
    for i in range(1, 8):
        z_forward(0, far_first(i)).start()
    for copy in small + locals_:
        copy.start()
    for c in range(1, n2):
        start_chunk(c)

    for d in range(2):

        @pl.when(jnp.logical_not(has_one[d]))
        def _():
            yb[d] = jnp.zeros(yb.shape[1:], F32)

        @pl.when(jnp.logical_not(has_two[d]))
        def _():
            yb[d + 2] = jnp.zeros(yb.shape[1:], F32)

    for copy in small:
        copy.wait()

    def table_of(matrix, table):
        n = matrix.shape[0]
        pick = hot((n * n, n), lambda q: q // n)
        both = 0.5 * (exact(pick, matrix[...]) + exact_nt(pick, matrix[...]))
        spread(n * n, both, None, table)

    table_of(kin_one, tab1)
    table_of(kin_two, tab2)
    spread(64, exact(hot((64, 8), lambda q: q // 8), beta[...]), None, tabb)
    eye8 = hot((8, 8), lambda q: q)
    sym3 = 0.5 * (kin_three[...] + exact_nt(eye8, kin_three[...]))
    for s in range(8):
        mask = (iota((8, 8), 0) + (8 - s)) % 8 == iota((8, 8), 1)
        tab3[s] = exact(jnp.where(mask, sym3, 0.0), jnp.ones((8, LANES), F32))

    def expand(pick, matrix, pick_t):
        both = 0.5 * (exact(pick, matrix[...]) + exact_nt(pick, matrix[...]))
        return exact_nt(both, pick_t)

    rows4[...] = expand(eye8, kin_four, hot((512, 8), lambda q: q // 64))
    e5 = expand(hot((64, 8), lambda q: q // 8), kin_five, hot((512, 8), lambda q: (q // 8) % 8))
    e6 = expand(hot((64, 8), lambda q: q % 8), kin_six, hot((512, 8), lambda q: q % 8))
    qi = iota((64, 512), 0)
    pi = iota((64, 512), 1)
    m56 = jnp.where(pi % 8 == qi % 8, e5, 0.0) + jnp.where((pi // 8) % 8 == qi // 8, e6, 0.0)
    diag64 = pi % 64 == qi
    for k in range(8):
        block = jnp.where(diag64, rows4[k : k + 1, :], 0.0) + jnp.where(pi // 64 == k, m56, 0.0)
        high, low = halves(block)
        tkh[k * 64 : (k + 1) * 64, :] = high
        tkl[k * 64 : (k + 1) * 64, :] = low
    pick6 = hot((256, 8), lambda q: q % 8)
    turned = 0.5 * (exact_nt(pick6, deriv[...]) - exact(pick6, deriv[...]))
    full = jnp.where(iota((256, 256), 0) // 8 == iota((256, 256), 1) // 8, exact_nt(turned, pick6), 0.0)
    high, low = halves(full)
    twh[...] = high
    twl[...] = low
    acc[...] = jnp.zeros(acc.shape, F32)

    level = (ka - nblocks // 2).astype(F32)
    shift = rot[ka] * level * level
    near = coupling[0, ka]
    near_low = coupling[0, jnp.maximum(ka - 1, 0)]
    far = coupling[1, ka]
    far_low = coupling[1, jnp.maximum(ka - 2, 0)]

    def mix16(load, store, table):
        xs = [[load(b, q) for q in range(2)] for b in range(16)]
        for a in range(16):
            total = None
            for b in range(16):
                k = splat(table, a * 16 + b)
                terms = [k * xs[b][q] for q in range(2)]
                total = terms if total is None else [t + s for t, s in zip(total, terms)]
            for q in range(2):
                store(a, q, total[q])

    def first_mode(c):
        @pl.loop(0, 2)
        def _(h):
            def at(q):
                return pl.ds(pl.multiple_of(h * 256 + q * LANES, LANES), LANES)

            def load(b, q):
                return zin[b // 2, b % 2, c, :, at(q)]

            def store(a, q, val):
                zout[a // 2, a % 2, c, :, at(q)] = val

            mix16(load, store, tab1)

        zret[z, :, c] = zout[z, :, c]

    def second_mode():
        @pl.loop(0, 8)
        def _(k):
            n, m, h = k // 4, (k // 2) % 2, k % 2

            def at(q):
                return pl.ds(pl.multiple_of(h * 256 + q * LANES, LANES), LANES)

            def load(b, q):
                return rin[b // 4, n, m, b % 4, :, at(q)]

            def store(a, q, val):
                rout[a // 4, n, m, a % 4, :, at(q)] = val

            mix16(load, store, tab2)

        rret[pl.ds(2 * r, 2)] = rout[r]

    def gather_products(c, left, right, spot_of, triangle):
        for g in range(4):
            pairs = [(j, i) for i in (2 * g, 2 * g + 1) for j in range(8) if j <= i or not triangle]
            sums = {}
            for m in range(n1):
                for q in range(4):
                    ls = [left[j, m, c, :, lane_block(q)] for j in range(8)]
                    rs = [right[i, m, c, :, lane_block(q)] for i in (2 * g, 2 * g + 1)]
                    for j, i in pairs:
                        term = ls[j] * rs[i - 2 * g]
                        sums[j, i] = term if (j, i) not in sums else sums[j, i] + term
            for j, i in pairs:
                spot = spot_of(j, i)
                acc[spot * 8 : spot * 8 + 8, :] += sums[j, i]

    def local_terms(c):
        x = v[:, :, c].reshape(nv * n1 * 8, 512)
        w[:, :, c] = three_pass(x, tkh[...], tkl[...]).reshape(nv, n1, 8, 512)

        @pl.loop(0, 4)
        def _(k):
            m, h = k // 2, k % 2
            for q in range(2):
                at = pl.ds(pl.multiple_of(h * 256 + q * LANES, LANES), LANES)
                old = [pv[j, m, c, :, at] for j in range(8)]
                diag = po[m, c, :, at] + shift
                for i in range(8):
                    xi = v[i, m, c, :, at]
                    total = w[i, m, c, :, at] + (diag + tab3[0]) * xi
                    for s in range(1, 8):
                        total = total + tab3[s] * pltpu.roll(xi, s, axis=0)
                    taken = splat(tabb, i * 8) * old[0]
                    for j in range(1, 8):
                        taken = taken + splat(tabb, i * 8 + j) * old[j]
                    w[i, m, c, :, at] = total - taken

        gather_products(c, v, v, lambda j, i: (16 + j) * 8 + i, True)

    def turn(x):
        flat = x.reshape(nv * n1 * 8, 512)
        parts = [three_pass(flat[:, h * 256 : h * 256 + 256], twh[...], twl[...]) for h in range(2)]
        return jnp.concatenate(parts, axis=1).reshape(x.shape)

    def near_terms(c):
        fn = cf[:, c][None]
        above = turn(yb[1, :, :, c])
        w[:, :, c] += (near * fn) * above
        below = turn(fn * yb[0, :, :, c])
        w[:, :, c] -= near_low * below

    def wait_recv_when(cond, copy):
        @pl.when(cond)
        def _():
            copy.wait_recv()

    for copy in locals_:
        copy.wait()

    @pl.loop(0, n2)
    def _(c):
        for d in range(2):
            wait_recv_when(has_one[d], y_own(c, d))

            send_on(1, c, d, jnp.logical_and(has_one[d], can_send[d]))

        @pl.when(c < VIA)
        def _():
            pass_on(0, c)

        @pl.loop(1, 8)
        def _(o):
            z_forward(c, o).wait_recv()

        first_mode(c)

        @pl.loop(1, 8)
        def _(o):
            z_back(c, far_first(o)).start()

        @pl.when(c == 1)
        def _():
            for o in range(1, 4):
                r_forward(o).wait_recv()
            second_mode()
            for o in range(1, 4):
                r_back(o).start()

        local_terms(c)
        near_terms(c)

    lane = iota((8, LANES), 1)
    row = iota((8, LANES), 0)

    def sum_into(count, shift, at):
        rows = count * 8
        part = acc[pl.ds(at * 64, rows, stride=8), :]
        for s in range(1, 8):
            part = part + acc[pl.ds(at * 64 + s, rows, stride=8), :]
        sums = jnp.sum(part, axis=1, keepdims=True)
        for a in range(2):
            packed = total[a]
            for l in range(count):
                q = l + shift
                if q // 16 == a:
                    here = lane == row + (q % 16) * 8
                    packed = jnp.where(here, sums[l * 8 : l * 8 + 8], packed)
            total[a] = packed

    total[...] = jnp.zeros((2, 8, LANES), F32)
    sum_into(8, 0, 16)

    def w_copy(c):
        return pltpu.make_async_copy(w.at[:, :, c], wout.at[:, :, c], obs.at[c])

    for c in range(VIA):
        pass_on(1, c)

    @pl.loop(0, n2)
    def _(c):
        @pl.loop(1, 8)
        def _(o):
            z_forward(c, o).wait_send()

        for d in range(2):

            @pl.when(can_send[d])
            def _():
                y_own(c, d).wait_send()

    for o in range(1, 4):
        r_forward(o).wait_send()

    def wait_sends_back():
        @pl.loop(0, n2)
        def _(c):
            w_copy(c).wait()

            @pl.loop(1, 8)
            def _(o):
                z_back(c, o).wait_send()

            for d in range(2):

                @pl.when(jnp.logical_and(has_one[d], can_send[d]))
                def _():
                    y_relay(c, d).wait_send()

        for k in range(2):
            for c in range(VIA):
                for d in range(2):

                    @pl.when(is_via[d])
                    def _():
                        from_via(k, c, d).wait_send()

        for o in range(1, 4):
            r_back(o).wait_send()

    for o in range(1, 4):
        r_back(o).wait_recv()

    @pl.loop(0, n2)
    def _(c):
        @pl.loop(1, 8)
        def _(o):
            z_back(c, o).wait_recv()

        for d in range(2):
            wait_recv_when(has_two[d], y_relay(c, d))

        @pl.loop(0, nv)
        def _(n):
            for m in range(n1):
                skip = sf[m, c] * (far * yb[3, n, m, c] + far_low * yb[2, n, m, c])
                w[n, m, c] = (w[n, m, c] + rret[n, m, c]) + (zret[n, m, c] + skip)

        w_copy(c).start()
        gather_products(c, v, w, lambda j, i: j * 8 + i, False)
        gather_products(c, w, w, lambda j, i: (8 + j) * 8 + i, True)

    sum_into(16, 8, 0)
    msg = jnp.concatenate([jnp.sum(total[a], axis=0, keepdims=True) for a in range(2)], axis=0)

    groups = ((u, x_peer), (z, z_peer), (y, y_peer))

    def ar_copy(g, o):
        me, peer = groups[g]
        return pltpu.make_async_remote_copy(
            arb.at[g, me], arb.at[g, me], ars.at[g, o], arr.at[g, o], device_id=peer(o)
        )

    for g in range(3):
        arb[g, groups[g][0]] = msg
        for i in range(1, 8):
            ar_copy(g, far_first(i)).start()
        if g == 1:
            wait_sends_back()
        if g > 0:
            for i in range(1, 8):
                ar_copy(g - 1, i).wait_send()
        for i in range(1, 8):
            ar_copy(g, i).wait_recv()
        msg = arb[g, 0]
        for t in range(1, 8):
            msg = msg + arb[g, t]

    msg = msg * (1.0 / float(16 * 8 * 4 * 32768))

    def mm(a, b):
        total = col(a, 0) * b[0:1, :]
        for k in range(1, 8):
            total = total + col(a, k) * b[k : k + 1, :]
        return total

    def select(own, column):
        high, low = halves(own)
        rest = ((own - high.astype(F32)) - low.astype(F32)).astype(BF16)
        parts = jnp.dot(
            jnp.concatenate([high, low, rest], axis=0),
            hot((LANES, LANES), column).astype(BF16),
            preferred_element_type=F32,
        )
        n = own.shape[0]
        return parts[0:n] + (parts[n : 2 * n] + parts[2 * n : 3 * n])

    rows_of = [msg[a : a + 1, :] for a in range(2)]
    within, block = lane % 8, lane // 8
    plain = select(
        jnp.concatenate([jnp.where(within == row, x, 0.0) for x in rows_of], axis=0),
        lambda q: q // 8,
    )
    turned_over = select(
        jnp.concatenate(
            [
                jnp.where(block == row, rows_of[0], 0.0),
                jnp.where(block == row + 8, rows_of[0], 0.0),
                jnp.where(block == row, rows_of[1], 0.0),
            ],
            axis=0,
        ),
        lambda q: q % 8,
    )
    first_t = pltpu.roll(plain[0:8], LANES - 8, axis=1)
    first = turned_over[8:16]
    overlap = jnp.where(lane <= row, plain[0:8], turned_over[0:8])
    square = jnp.where(lane <= row, plain[8:16], turned_over[16:24])
    both_t = 2.0 * first_t - mm(first_t, overlap)
    both = 2.0 * first - mm(overlap, first)
    gram = square - mm(both_t, first) - mm(first_t, both) + mm(mm(both_t, overlap), both)
    work = jnp.where(lane < 8, gram, 0.0)
    work = jnp.where(lane == row + 8, 1.0, work)
    work = jnp.where((lane >= 16) & (lane < 24), pltpu.roll(both_t, 16, axis=1), work)
    factor = jnp.zeros((8, LANES), F32)
    for k in range(8):
        prow = jnp.broadcast_to(work[k : k + 1, :], (8, LANES))
        pivot = col(prow, k)
        column = col(work, k)
        root = lax.rsqrt(pivot)
        factor = jnp.where((lane == k) & (row >= k), column * root, factor)
        below = work - (column * (root * root)) * prow
        work = jnp.where(row > k, below, jnp.where(row == k, work * root, work))
    pack[0] = work
    pack[1] = both
    pack[2] = factor

    for i in range(1, 8):
        ar_copy(2, i).wait_send()


def finish(vec, wfin, pack_hbm, out, alpha_hbm, lower_hbm, v, w, ob, pack, coef, small, sem):
    n2 = v.shape[2]

    def loads(c):
        return (
            pltpu.make_async_copy(vec.at[0, :, :, c], v.at[:, :, c], sem.at[0, c]),
            pltpu.make_async_copy(wfin.at[:, :, c], w.at[:, :, c], sem.at[1, c]),
        )

    first = pltpu.make_async_copy(pack_hbm, pack, sem.at[3, 0])
    first.start()
    for c in range(n2):
        for copy in loads(c):
            copy.start()
    first.wait()
    small[0] = pack[1, :, 0:8]
    small[1] = pack[2, :, 0:8]
    tiny = [
        pltpu.make_async_copy(small.at[0], alpha_hbm, sem.at[3, 1]),
        pltpu.make_async_copy(small.at[1], lower_hbm, sem.at[3, 2]),
    ]
    for copy in tiny:
        copy.start()
    work = pack[0]
    for j in range(8):
        coef[j * 8 : j * 8 + 8, :] = col(work, 8 + j)
        coef[64 + j * 8 : 72 + j * 8, :] = -col(work, 16 + j)

    def out_copy(c):
        return pltpu.make_async_copy(ob.at[:, :, c], out.at[0, :, :, c], sem.at[2, c])

    @pl.loop(0, n2)
    def _(c):
        for copy in loads(c):
            copy.wait()

        @pl.loop(0, 4)
        def _(k):
            m, h = k // 2, k % 2
            at = [pl.ds(pl.multiple_of(h * 256 + q * LANES, LANES), LANES) for q in range(2)]
            vs = [[v[j, m, c, :, at[q]] for q in range(2)] for j in range(8)]
            ws = [[w[j, m, c, :, at[q]] for q in range(2)] for j in range(8)]
            for i in range(8):
                total = None
                for base, xs, count in ((64, vs, 8), (0, ws, i + 1)):
                    for j in range(count):
                        factor = splat(coef, base + j * 8 + i)
                        terms = [factor * xs[j][q] for q in range(2)]
                        total = terms if total is None else [t + s for t, s in zip(total, terms)]
                for q in range(2):
                    ob[i, m, c, :, at[q]] = total[q]

        out_copy(c).start()

    @pl.loop(0, n2)
    def _(c):
        out_copy(c).wait()

    for copy in tiny:
        copy.wait()


def shards(*args):
    (vectors, previous, beta, potential, coriolis_fn, second_fn, rot_const, coupling, *mats) = args
    block = vectors.shape[1:]
    fn = potential.shape
    any_spec = pl.BlockSpec(memory_space=pltpu.HBM)
    vmem = pl.BlockSpec(memory_space=pltpu.VMEM)
    nv, n1, n2, n3, nr = block
    dma = pltpu.SemaphoreType.DMA
    scratch = [
        pltpu.VMEM(block, F32),
        pltpu.VMEM(block, F32),
        pltpu.VMEM(fn, F32),
        pltpu.VMEM(fn, F32),
        pltpu.VMEM(fn, F32),
        pltpu.VMEM(block, F32),
        pltpu.VMEM(block, F32),
        pltpu.VMEM(block, F32),
        pltpu.VMEM(block, F32),
        pltpu.VMEM((4, 2) + block[1:], F32),
        pltpu.VMEM((4, 2) + block[1:], F32),
        pltpu.VMEM(block, F32),
        pltpu.VMEM((4,) + block, F32),
        pltpu.VMEM((2 * n2, nv, n1, n3, nr), F32),
        pltpu.VMEM((8, 8), F32),
        pltpu.SMEM((16,), F32),
        pltpu.SMEM((2, 16), F32),
        pltpu.VMEM((16, 16), F32),
        pltpu.VMEM((16, 16), F32),
        *[pltpu.VMEM((8, 8), F32)] * 5,
        pltpu.VMEM((256, LANES), F32),
        pltpu.VMEM((256, LANES), F32),
        pltpu.VMEM((64, LANES), F32),
        pltpu.VMEM((8, 8, LANES), F32),
        pltpu.VMEM((8, nr), F32),
        pltpu.VMEM((nr, nr), BF16),
        pltpu.VMEM((nr, nr), BF16),
        pltpu.VMEM((256, 256), BF16),
        pltpu.VMEM((256, 256), BF16),
        pltpu.VMEM((192 * 8, LANES), F32),
        pltpu.VMEM((2, 8, LANES), F32),
        pltpu.VMEM((3, 8, 2, LANES), F32),
        dma((17,)),
        dma((n2, 8)),
        dma((n2, 8)),
        dma((n2, 8)),
        dma((n2, 8)),
        dma((4,)),
        dma((4,)),
        dma((4,)),
        dma((4,)),
        dma((2, n2)),
        dma((2, n2)),
        dma((2, n2)),
        dma((2, n2)),
        dma((2 * n2,)),
        dma((2 * n2,)),
        dma((3, 8)),
        dma((3, 8)),
        dma((n2,)),
    ]
    wfin, pack = pl.pallas_call(
        kernel,
        out_shape=(
            jax.ShapeDtypeStruct(block, F32),
            jax.ShapeDtypeStruct((3, nv, LANES), F32),
        ),
        in_specs=[any_spec] * 15,
        out_specs=(any_spec, vmem),
        scratch_shapes=scratch,
        compiler_params=pltpu.CompilerParams(
            collective_id=0, has_side_effects=True, vmem_limit_bytes=67043328
        ),
        name="lanczos",
    )(vectors, previous, potential, coriolis_fn, second_fn, beta, rot_const, coupling, *mats)
    return pl.pallas_call(
        finish,
        out_shape=(
            jax.ShapeDtypeStruct(vectors.shape, F32),
            jax.ShapeDtypeStruct((nv, nv), F32),
            jax.ShapeDtypeStruct((nv, nv), F32),
        ),
        in_specs=[any_spec] * 3,
        out_specs=(any_spec,) * 3,
        scratch_shapes=[
            pltpu.VMEM(block, F32),
            pltpu.VMEM(block, F32),
            pltpu.VMEM(block, F32),
            pltpu.VMEM((3, nv, LANES), F32),
            pltpu.VMEM((128, LANES), F32),
            pltpu.VMEM((2, nv, nv), F32),
            dma((4, n2)),
        ],
        compiler_params=pltpu.CompilerParams(vmem_limit_bytes=67043328),
        name="basis",
    )(vectors, wfin, pack)


def solution(mesh):
    split = P("ka", None, "mode", "row", None, None)
    fn = P("mode", "row", None, None)
    return jax.shard_map(
        shards,
        mesh=mesh,
        in_specs=(split, split, P(), fn, fn, fn) + (P(),) * 9,
        out_specs=(split, P(), P()),
        check_vma=False,
    )
```
